256 devices in a mesh: member: 16 (over z, y_hi), lat: 4 (over x), lon: 4 (over y_lo, core).
Axes of the slice: x: 4, y: 4 (y_hi: 2, y_lo: 2; y = y_hi * 2 + y_lo), z: 8, core: 2. Of those that a mesh axis runs over, the one named last changes fastest.
Arguments:
- ensemble: bfloat16 [32, 16, 64, 256], P('member', 'lat', 'lon'), may hold values from -12 to 12
- norm_gain: float32 [256], replicated, may hold values from 0.5 to 1.5
- project_weight: bfloat16 [256, 768], replicated, may hold values from -0.375 to 0.375
- output_weight: bfloat16 [256, 256], replicated, may hold values from -0.375 to 0.375
- conv_kernel: bfloat16 [3, 3, 256, 256], replicated, may hold values from -0.125 to 0.125
- cotangent: bfloat16 [32, 16, 64, 256], P('member', 'lat', 'lon'), may hold values from -6 to 6
Outputs:
- result: bfloat16 [32, 16, 64, 256], P('member', 'lat', 'lon')
- grad_ensemble: bfloat16 [32, 16, 64, 256], P('member', 'lat', 'lon')
The draws below stay inside these ranges and needn't reach their ends.
All inputs are finite; a program needn't handle non-finite values.
Results may differ from the reference program's by a relative error of at most 0.018.
Values may be sent and summed in bfloat16 or wider, within the bound.
A program may use at most 64 MiB of HBM per device.

```python
import math
import jax
import jax.numpy as jnp
from jax import lax

CHANNELS = 256
HEAD_COUNT = 8
MEMBERS = 32
LAT_ALL = 16
LON_ALL = 64


def draw_ensemble(key, part):
    first_key, second_key = jax.random.split(key, 2)
    shape_full = (MEMBERS, LAT_ALL, LON_ALL, CHANNELS)
    base = jax.random.truncated_normal(first_key, -4.0, 4.0, shape_full, jnp.float32)
    log_scale = jax.random.uniform(second_key, (MEMBERS, LAT_ALL, LON_ALL, 1), jnp.float32, jnp.log(0.3), jnp.log(3.0))
    return jnp.clip(base * jnp.exp(log_scale), -12.0, 12.0).astype(jnp.bfloat16)


def steps_of(stream_key, shape, cuts, low, top_value):
    gain = 1.0
    for position, shards_of in cuts:
        draws = jax.random.uniform(jax.random.fold_in(jax.random.fold_in(stream_key, 6), position), (shards_of,), jnp.float32, low / len(cuts), top_value / len(cuts))
        gain = gain * jnp.repeat(jnp.exp(draws), shape[position] // shards_of).reshape((-1,) + (1,) * (len(shape) - 1 - position))
    return gain


def bell_draw(rng, extent, spread, reach, pieces=(), held_as=jnp.bfloat16):
    level = steps_of(rng, extent, pieces, -0.22, 0.18) if pieces else 1.0
    array = jax.random.normal(rng, extent, jnp.float32) * spread * level
    return jnp.minimum(jnp.maximum(array, -reach), reach).astype(held_as)


def setup_inputs(seed: int = 0) -> dict:
    key_of = jax.random.split(jax.random.key(seed), 7)
    return {
        "ensemble": draw_ensemble(jax.random.fold_in(key_of[6], 71), 0),
        "norm_gain": jnp.clip(1.0 + 0.1 * jax.random.normal(key_of[1], (CHANNELS,), jnp.float32), 0.5, 1.5),
        "project_weight": bell_draw(key_of[2], (CHANNELS, 3 * CHANNELS), CHANNELS ** -0.5, 0.375),
        "output_weight": bell_draw(key_of[3], (CHANNELS, CHANNELS), CHANNELS ** -0.5, 0.375),
        "conv_kernel": bell_draw(key_of[4], (3, 3, CHANNELS, CHANNELS), (9 * CHANNELS) ** -0.5, 0.125),
        "cotangent": bell_draw(key_of[5], (MEMBERS, LAT_ALL, LON_ALL, CHANNELS), 1.0, 6.0, ((0, 16), (1, 4), (2, 4))),
    }


FLOOR = 0.5
EPSILON = 1e-06

def row_norm(values, gain_vec):
    mean_sq = lax.optimization_barrier(jnp.mean(values * values, axis=-1, keepdims=True))
    return values * lax.rsqrt(mean_sq + EPSILON) * gain_vec

def head_norm(values, head_count):
    shaped = values.reshape(values.shape[:-1] + (head_count, values.shape[-1] // head_count))
    mean_sq = lax.optimization_barrier(jnp.mean(shaped * shaped, axis=-1, keepdims=True))
    return (shaped * lax.rsqrt(jnp.maximum(mean_sq, FLOOR))).reshape(values.shape)

def split_heads(values, head_count):
    return values.reshape(values.shape[:-1] + (head_count, values.shape[-1] // head_count))

def widen(values):
    return lax.optimization_barrier(values).astype(jnp.float32)

def pad_globe(field_in):
    widened = jnp.concatenate([field_in[:, :, -1:], field_in, field_in[:, :, :1]], axis=2)
    zero_row = jnp.zeros_like(widened[:, :1])
    return jnp.concatenate([zero_row, widened, zero_row], axis=1)

def conv_taps(padded, kernel, lat_n, lon_n, adjoint):
    running = None
    for row_off in range(3):
        for col_off in range(3):
            tap = kernel[row_off, col_off].astype(jnp.float32)
            if adjoint:
                window = padded[:, 2 - row_off:2 - row_off + lat_n, 2 - col_off:2 - col_off + lon_n].astype(jnp.float32)
                summand = jnp.einsum('mabc,dc->mabd', window, tap)
            else:
                window = padded[:, row_off:row_off + lat_n, col_off:col_off + lon_n].astype(jnp.float32)
                summand = jnp.einsum('mabc,cd->mabd', window, tap)
            running = summand if running is None else running + summand
    return running

def reference(ensemble, norm_gain, project_weight, output_weight, conv_kernel, cotangent):
    members, lat_all, lon_all, channels = ensemble.shape
    cell_count = lat_all * lon_all
    score_scale = 1.0 / math.sqrt(channels // HEAD_COUNT)
    inputs = ensemble.reshape(members, cell_count, channels).astype(jnp.float32)
    normed = row_norm(inputs, norm_gain).astype(jnp.bfloat16)
    projected = jnp.dot(normed, project_weight, preferred_element_type=jnp.float32).astype(jnp.bfloat16)
    query_raw = projected[..., :channels]
    key_raw = projected[..., channels:2 * channels]
    value_rows = projected[..., 2 * channels:]
    queries = head_norm(query_raw.astype(jnp.float32), HEAD_COUNT).astype(jnp.bfloat16)
    key_rows = head_norm(key_raw.astype(jnp.float32), HEAD_COUNT).astype(jnp.bfloat16)
    query_heads = split_heads(widen(queries), HEAD_COUNT)
    key_heads = split_heads(widen(key_rows), HEAD_COUNT)
    value_heads = split_heads(value_rows.astype(jnp.float32), HEAD_COUNT)
    scores = jnp.einsum('mphd,nphd->mnhp', query_heads, key_heads) * score_scale
    expd = jnp.exp(scores)
    soft = expd / lax.optimization_barrier(jnp.sum(expd, axis=1, keepdims=True))
    rounded = soft.astype(jnp.bfloat16)
    rounded_wide = widen(rounded)
    mixed_out = jnp.einsum('mnhp,nphd->mphd', rounded_wide, value_heads)
    mixed_out = mixed_out.reshape(members, cell_count, channels).astype(jnp.bfloat16)
    updated = (inputs + jnp.dot(mixed_out, output_weight, preferred_element_type=jnp.float32)).astype(jnp.bfloat16)
    field_up = updated.reshape(members, lat_all, lon_all, channels)
    result = field_up.astype(jnp.float32) + conv_taps(pad_globe(field_up), conv_kernel, lat_all, lon_all, False)
    result = result.astype(jnp.bfloat16)
    grad_field = cotangent.astype(jnp.float32) + conv_taps(pad_globe(cotangent), conv_kernel, lat_all, lon_all, True)
    grad_rows = grad_field.reshape(members, cell_count, channels)
    grad_mixed = jnp.einsum('mpc,dc->mpd', widen(grad_rows.astype(jnp.bfloat16)), output_weight.astype(jnp.float32))
    grad_mixed = grad_mixed.astype(jnp.bfloat16)
    grad_heads = split_heads(widen(grad_mixed), HEAD_COUNT)
    dprob = jnp.einsum('mphd,nphd->mnhp', grad_heads, value_heads)
    dscore = soft * (dprob - lax.optimization_barrier(jnp.sum(soft * dprob, axis=1, keepdims=True)))
    dscore_wide = widen(dscore.astype(jnp.bfloat16))
    query_grad = (jnp.einsum('mnhp,nphd->mphd', dscore_wide, key_heads) * score_scale).reshape(members, cell_count, channels)
    key_grad = (jnp.einsum('mnhp,mphd->nphd', dscore_wide, query_heads) * score_scale).reshape(members, cell_count, channels)
    value_grad = jnp.einsum('mnhp,mphd->nphd', rounded_wide, grad_heads).reshape(members, cell_count, channels)
    _, pull_query = jax.vjp(lambda t: head_norm(t, HEAD_COUNT), query_raw.astype(jnp.float32))
    _, pull_key = jax.vjp(lambda t: head_norm(t, HEAD_COUNT), key_raw.astype(jnp.float32))
    grad_query_raw = pull_query(query_grad)[0]
    grad_key_raw = pull_key(key_grad)[0]
    grad_proj = jnp.concatenate([grad_query_raw, grad_key_raw, value_grad], axis=-1).astype(jnp.bfloat16)
    grad_normed = jnp.einsum('mpe,ce->mpc', widen(grad_proj), project_weight.astype(jnp.float32))
    _, pull_norm = jax.vjp(lambda t: row_norm(t, norm_gain), inputs)
    grad_inputs = pull_norm(grad_normed)[0]
    grad_ensemble = (grad_rows + grad_inputs).astype(jnp.bfloat16).reshape(members, lat_all, lon_all, channels)
    return (result, grad_ensemble)
```

```python
import math

import jax
import jax.numpy as jnp
from jax import lax
from jax.sharding import PartitionSpec as P

HEADS = 8
FLOOR = 0.5
EPSILON = 1e-06
BF = jnp.bfloat16
F32 = jnp.float32


def mm(a, b, dims):
    return lax.dot_general(a, b, (dims, ((), ())), preferred_element_type=F32)


def nn(a, b):
    return mm(a, b, ((1,), (0,)))


def nt(a, b):
    return mm(a, b, ((1,), (1,)))


def tn(a, b):
    return mm(a, b, ((0,), (0,)))


def head_blocks(channels, members):
    width = channels // HEADS
    row = lax.broadcasted_iota(jnp.int32, (HEADS * members, channels), 0) // members
    col = lax.broadcasted_iota(jnp.int32, (HEADS * members, channels), 1) // width
    return row == col


def spread(rows, blocks):
    return jnp.concatenate([rows] * HEADS, axis=0) * blocks


def head_scale(raw, ones):
    width = raw.shape[1] // HEADS
    mean_sq = nn((raw * raw).astype(BF), ones) * (1.0 / width)
    factor = lax.rsqrt(jnp.maximum(mean_sq, FLOOR))
    live = jnp.where(mean_sq > FLOOR, 1.0, jnp.where(mean_sq == FLOOR, 0.5, 0.0))
    return factor, live


def cell_forward(x, gain, w_proj, w_out, ones, members):
    rows, channels = x.shape
    cells = rows // members
    scale = 1.0 / math.sqrt(channels // HEADS)
    inputs = x.astype(F32)
    inv = lax.rsqrt(jnp.mean(inputs * inputs, axis=-1, keepdims=True) + EPSILON)
    normed = (inputs * inv * gain).astype(BF)
    proj = nn(normed, w_proj).astype(BF)
    q_raw = proj[:, :channels].astype(F32)
    k_raw = proj[:, channels : 2 * channels].astype(F32)
    values = proj[:, 2 * channels :]
    q_fac, q_live = head_scale(q_raw, ones)
    k_fac, k_live = head_scale(k_raw, ones)
    queries = (q_raw * q_fac).astype(BF)
    keys = (k_raw * k_fac).astype(BF)
    part = [slice(c * members, (c + 1) * members) for c in range(cells)]
    k_bd = [spread(keys[s], ones) for s in part]
    v_bd = [spread(values[s], ones) for s in part]
    scores = jnp.concatenate([nt(queries[s], k) for s, k in zip(part, k_bd)], axis=0)
    expd = jnp.exp(scores * scale)
    soft = expd / nn(expd.astype(BF), ones)
    rounded = soft.astype(BF)
    mixed = jnp.concatenate([nn(rounded[s], v) for s, v in zip(part, v_bd)], axis=0).astype(BF)
    updated = (inputs + nn(mixed, w_out)).astype(BF)
    saved = (inputs, inv, q_raw, k_raw, q_fac, k_fac, q_live, k_live, queries, k_bd, v_bd, soft, rounded)
    return updated, saved


def head_pull(raw, factor, live, grad, ones):
    width = raw.shape[1] // HEADS
    inner = nn((raw * grad).astype(BF), ones) * (1.0 / width)
    return grad * factor - raw * (factor * factor * factor * live * inner)


def fold(full, ones, members):
    kept = full * ones.astype(F32)
    total = kept[:members]
    for h in range(1, HEADS):
        total = total + kept[h * members : (h + 1) * members]
    return total


def cell_backward(grad_field, saved, gain, w_proj, w_out, ones, members):
    inputs, inv, q_raw, k_raw, q_fac, k_fac, q_live, k_live, queries, k_bd, v_bd, soft, rounded = saved
    rows, channels = inputs.shape
    cells = rows // members
    scale = 1.0 / math.sqrt(channels // HEADS)
    part = [slice(c * members, (c + 1) * members) for c in range(cells)]
    grad_mixed = nt(grad_field, w_out).astype(BF)
    dprob = jnp.concatenate([nt(grad_mixed[s], v) for s, v in zip(part, v_bd)], axis=0)
    delta = nn((soft * dprob).astype(BF), ones)
    dscore = (soft * (dprob - delta)).astype(BF)
    q_grad = jnp.concatenate([nn(dscore[s], k) for s, k in zip(part, k_bd)], axis=0) * scale
    k_grad = jnp.concatenate([fold(tn(dscore[s], queries[s]), ones, members) for s in part], axis=0) * scale
    v_grad = jnp.concatenate([fold(tn(rounded[s], grad_mixed[s]), ones, members) for s in part], axis=0)
    gq = head_pull(q_raw, q_fac, q_live, q_grad, ones).astype(BF)
    gk = head_pull(k_raw, k_fac, k_live, k_grad, ones).astype(BF)
    gv = v_grad.astype(BF)
    grad_normed = (
        nt(gq, w_proj[:, :channels])
        + nt(gk, w_proj[:, channels : 2 * channels])
        + nt(gv, w_proj[:, 2 * channels :])
    )
    lifted = grad_normed * gain
    inner = jnp.mean(lifted * inputs, axis=-1, keepdims=True)
    return lifted * inv - inputs * (inv * inv * inv * inner)


def padded(block):
    for axis, dim, periodic in (("lon", 2, True), ("lat", 1, False)):
        count = lax.axis_size(axis)
        forward = [(i, i + 1) for i in range(count - 1)]
        if periodic:
            forward.append((count - 1, 0))
        backward = [(t, s) for s, t in forward]
        low = lax.ppermute(lax.slice_in_dim(block, block.shape[dim] - 1, None, axis=dim), axis, forward)
        high = lax.ppermute(lax.slice_in_dim(block, 0, 1, axis=dim), axis, backward)
        block = jnp.concatenate([low, block, high], axis=dim)
    return block


def conv_taps(field, kernel, adjoint):
    mem, lat, lon, channels = field.shape
    wide = padded(field)
    total = None
    for r in range(3):
        for c in range(3):
            i, j = (2 - r, 2 - c) if adjoint else (r, c)
            window = wide[:, i : i + lat, j : j + lon].reshape(mem * lat * lon, channels)
            term = nt(window, kernel[r, c]) if adjoint else nn(window, kernel[r, c])
            total = term if total is None else total + term
    return total


def to_cells(rows):
    mem, lat, lon, channels = rows.shape
    count = lax.axis_size("member")
    out = rows.reshape(mem, lat, count, lon // count, channels).transpose(2, 1, 3, 0, 4)
    out = lax.all_to_all(out, "member", 0, 0, tiled=True)
    return out.transpose(1, 2, 0, 3, 4).reshape(-1, channels)


def to_home(rows, shape):
    mem, lat, lon, channels = shape
    count = lax.axis_size("member")
    out = rows.reshape(lat, lon // count, count, mem, channels).transpose(2, 0, 1, 3, 4)
    out = lax.all_to_all(out, "member", 0, 0, tiled=True)
    return out.transpose(3, 1, 0, 2, 4).reshape(shape)


def per_device(ensemble, norm_gain, project_weight, output_weight, conv_kernel, cotangent):
    mem, lat, lon, channels = ensemble.shape
    members = mem * lax.axis_size("member")
    ones = head_blocks(channels, members).astype(BF)
    gain = norm_gain.reshape(1, channels)
    x = to_cells(ensemble)
    updated, saved = cell_forward(x, gain, project_weight, output_weight, ones, members)
    field = to_home(updated, ensemble.shape)
    grad_field = cotangent.astype(F32).reshape(-1, channels) + conv_taps(cotangent, conv_kernel, True)
    grad_cells = to_cells(grad_field.astype(BF).reshape(ensemble.shape))
    grad_inputs = cell_backward(grad_cells, saved, gain, project_weight, output_weight, ones, members)
    result = field.astype(F32).reshape(-1, channels) + conv_taps(field, conv_kernel, False)
    back = to_home(grad_inputs.astype(BF), ensemble.shape).astype(F32).reshape(-1, channels)
    return (
        result.astype(BF).reshape(ensemble.shape),
        (grad_field + back).astype(BF).reshape(ensemble.shape),
    )


def solution(mesh):
    field = P("member", "lat", "lon", None)
    return jax.shard_map(
        per_device,
        mesh=mesh,
        in_specs=(field, P(), P(), P(), P(), field),
        out_specs=(field, field),
        check_vma=False,
    )
```

```python
import functools
import math

import jax
import jax.numpy as jnp
from jax import lax
from jax.experimental import pallas as pl
from jax.experimental.pallas import tpu as pltpu
from jax.sharding import PartitionSpec as P

HEADS = 8
FLOOR = 0.5
EPSILON = 1e-06
BF = jnp.bfloat16
F32 = jnp.float32


def mm(a, b, dims):
    return lax.dot_general(a, b, (dims, ((), ())), preferred_element_type=F32)


def nn(a, b):
    return mm(a, b, ((1,), (0,)))


def nt(a, b):
    return mm(a, b, ((1,), (1,)))


def tn(a, b):
    return mm(a, b, ((0,), (0,)))


def head_blocks(channels, members):
    width = channels // HEADS
    row = lax.broadcasted_iota(jnp.int32, (HEADS * members, channels), 0) // members
    col = lax.broadcasted_iota(jnp.int32, (HEADS * members, channels), 1) // width
    return row == col


def spread(rows, blocks):
    return jnp.concatenate([rows] * HEADS, axis=0) * blocks


def head_scale(raw, ones):
    width = raw.shape[1] // HEADS
    mean_sq = nn((raw * raw).astype(BF), ones) * (1.0 / width)
    factor = lax.rsqrt(jnp.maximum(mean_sq, FLOOR))
    live = jnp.where(mean_sq > FLOOR, 1.0, jnp.where(mean_sq == FLOOR, 0.5, 0.0))
    return factor, live


def cell_forward(x, gain, w_proj, w_out, ones, members):
    rows, channels = x.shape
    cells = rows // members
    scale = 1.0 / math.sqrt(channels // HEADS)
    inputs = x.astype(F32)
    inv = lax.rsqrt(jnp.mean(inputs * inputs, axis=-1, keepdims=True) + EPSILON)
    normed = (inputs * inv * gain).astype(BF)
    proj = nn(normed, w_proj).astype(BF)
    q_raw = proj[:, :channels].astype(F32)
    k_raw = proj[:, channels : 2 * channels].astype(F32)
    values = proj[:, 2 * channels :]
    q_fac, q_live = head_scale(q_raw, ones)
    k_fac, k_live = head_scale(k_raw, ones)
    queries = (q_raw * q_fac).astype(BF)
    keys = (k_raw * k_fac).astype(BF)
    part = [slice(c * members, (c + 1) * members) for c in range(cells)]
    k_bd = [spread(keys[s], ones) for s in part]
    v_bd = [spread(values[s], ones) for s in part]
    scores = jnp.concatenate([nt(queries[s], k) for s, k in zip(part, k_bd)], axis=0)
    expd = jnp.exp(scores * scale)
    soft = expd / nn(expd.astype(BF), ones)
    rounded = soft.astype(BF)
    mixed = jnp.concatenate([nn(rounded[s], v) for s, v in zip(part, v_bd)], axis=0).astype(BF)
    updated = (inputs + nn(mixed, w_out)).astype(BF)
    saved = (inputs, inv, q_raw, k_raw, q_fac, k_fac, q_live, k_live, queries, k_bd, v_bd, soft, rounded)
    return updated, saved


def head_pull(raw, factor, live, grad, ones):
    width = raw.shape[1] // HEADS
    inner = nn((raw * grad).astype(BF), ones) * (1.0 / width)
    return grad * factor - raw * (factor * factor * factor * live * inner)


def fold(full, ones, members):
    kept = full * ones.astype(F32)
    total = kept[:members]
    for h in range(1, HEADS):
        total = total + kept[h * members : (h + 1) * members]
    return total


def cell_backward(grad_field, saved, gain, w_proj, w_out, ones, members):
    inputs, inv, q_raw, k_raw, q_fac, k_fac, q_live, k_live, queries, k_bd, v_bd, soft, rounded = saved
    rows, channels = inputs.shape
    cells = rows // members
    scale = 1.0 / math.sqrt(channels // HEADS)
    part = [slice(c * members, (c + 1) * members) for c in range(cells)]
    grad_mixed = nt(grad_field, w_out).astype(BF)
    dprob = jnp.concatenate([nt(grad_mixed[s], v) for s, v in zip(part, v_bd)], axis=0)
    delta = nn((soft * dprob).astype(BF), ones)
    dscore = (soft * (dprob - delta)).astype(BF)
    q_grad = jnp.concatenate([nn(dscore[s], k) for s, k in zip(part, k_bd)], axis=0) * scale
    k_grad = jnp.concatenate([fold(tn(dscore[s], queries[s]), ones, members) for s in part], axis=0) * scale
    v_grad = jnp.concatenate([fold(tn(rounded[s], grad_mixed[s]), ones, members) for s in part], axis=0)
    gq = head_pull(q_raw, q_fac, q_live, q_grad, ones).astype(BF)
    gk = head_pull(k_raw, k_fac, k_live, k_grad, ones).astype(BF)
    gv = v_grad.astype(BF)
    grad_normed = (
        nt(gq, w_proj[:, :channels])
        + nt(gk, w_proj[:, channels : 2 * channels])
        + nt(gv, w_proj[:, 2 * channels :])
    )
    lifted = grad_normed * gain
    inner = jnp.mean(lifted * inputs, axis=-1, keepdims=True)
    return lifted * inv - inputs * (inv * inv * inv * inner)


def iota(shape, dim):
    return lax.broadcasted_iota(jnp.int32, shape, dim)


def one_hot(shape, source):
    return jnp.where(iota(shape, 1) == source(iota(shape, 0)), 1.0, 0.0).astype(BF)


def pack(rows, peers):
    half = rows.shape[1] // 2
    per = rows.shape[0] // peers
    low = rows[:, :half].reshape(peers, per, half)
    high = rows[:, half:].reshape(peers, per, half)
    return jnp.concatenate([low, high], axis=1).astype(BF)


def unpack(chunks):
    peers, double, half = chunks.shape
    wide = chunks.astype(F32)
    low = wide[:, : double // 2].reshape(peers * double // 2, half)
    high = wide[:, double // 2 :].reshape(peers * double // 2, half)
    return jnp.concatenate([low, high], axis=1).astype(BF)


X, G, U, B = range(4)


def kernel(
    dims,
    ens_ref,
    gain_ref,
    w_proj_any,
    w_out_any,
    conv_any,
    cot_ref,
    result_ref,
    grad_ref,
    w_proj_ref,
    w_out_ref,
    conv_ref,
    out_buf,
    in_buf,
    halo_cot,
    halo_up,
    edge_cot,
    edge_up,
    field_ref,
    gf_ref,
    load_sem,
    ex_send,
    ex_recv,
    halo_send,
    halo_recv,
):
    mem, lat, lon, channels, peers, lats, lons = dims
    cells = mem * lat * lon
    members = mem * peers
    me = lax.axis_index("member")
    my_lat = lax.axis_index("lat")
    my_lon = lax.axis_index("lon")

    loads = [
        pltpu.make_async_copy(src, dst, load_sem.at[i])
        for i, (src, dst) in enumerate(
            ((conv_any, conv_ref), (w_proj_any, w_proj_ref), (w_out_any, w_out_ref))
        )
    ]
    for load in loads:
        load.start()

    def partner(j):
        return {"member": lax.rem(me + j, peers)}

    def near(d_lat, d_lon):
        return {
            "lat": lax.rem(my_lat + d_lat + lats, lats),
            "lon": lax.rem(my_lon + d_lon + lons, lons),
        }

    around = [(a, b) for a in (-1, 0, 1) for b in (-1, 0, 1) if (a, b) != (0, 0)]
    barrier = pltpu.get_barrier_semaphore()
    for j in range(1, peers):
        pl.semaphore_signal(barrier, inc=1, device_id=partner(j), device_id_type=MESH)
    for d_lat, d_lon in around:
        pl.semaphore_signal(barrier, inc=1, device_id=near(d_lat, d_lon), device_id_type=MESH)

    def home_source(i):
        j, m, a = i // (mem * lat), (i // lat) % mem, i % lat
        return (m * lat + a) * lon + lax.rem(me + j, peers)

    def home_target(i):
        m, a, b = i // (lat * lon), (i // lon) % lat, i % lon
        return lax.rem(b - me + peers, peers) * (mem * lat) + m * lat + a

    def cell_source(i):
        c, j, m = i // members, (i // mem) % peers, i % mem
        return (j * mem + m) * lat + c

    def cell_target(i):
        j, m, c = i // (mem * lat), (i // lat) % mem, i % lat
        return (c * peers + j) * mem + m

    def edge_source(i):
        count = mem * lat
        return (i % count) * lon + (i // count) * (lon - 1)

    square = (cells, cells)
    home_out = one_hot(square, home_source)
    home_in = one_hot(square, home_target)
    cell_in = one_hot(square, cell_source)
    cell_out = one_hot(square, cell_target)
    edges = one_hot((2 * mem * lat, cells), edge_source)

    def exchange(kind, sign):
        return [
            pltpu.make_async_remote_copy(
                src_ref=out_buf.at[kind, j],
                dst_ref=in_buf.at[kind, j],
                send_sem=ex_send.at[kind],
                recv_sem=ex_recv.at[kind],
                device_id=partner(j if sign > 0 else peers - j),
                device_id_type=MESH,
            )
            for j in range(1, peers)
        ]

    def exchange_all(kind):
        return pltpu.make_async_remote_copy(
            src_ref=out_buf.at[kind, pl.ds(1, peers - 1)],
            dst_ref=in_buf.at[kind, pl.ds(1, peers - 1)],
            send_sem=ex_send.at[kind],
            recv_sem=ex_recv.at[kind],
            device_id=partner(1),
            device_id_type=MESH,
        )

    def send(kind, order, rows, sign):
        packed = pack(nn(order, rows), peers)
        out_buf[kind] = packed
        in_buf[kind, 0] = packed[0]
        for copy in exchange(kind, sign):
            copy.start()

    def receive(kind, order):
        exchange_all(kind).wait_recv()
        return nn(order, unpack(in_buf[kind]))

    def halo_copies(slot, rows_ref, edge_ref, halo):
        copies = []
        for side, (d_lat, a) in enumerate(((1, lat - 1), (-1, 0))):
            copies.append(
                pltpu.make_async_remote_copy(
                    src_ref=rows_ref.at[:, a],
                    dst_ref=halo.at[:, 0 if side == 0 else lat + 1],
                    send_sem=halo_send.at[slot, side],
                    recv_sem=halo_recv.at[slot, side],
                    device_id=near(d_lat, 0),
                    device_id_type=MESH,
                )
            )
        for d_lat in (-1, 0, 1):
            for d_lon in (-1, 1):
                copies.append(
                    pltpu.make_async_remote_copy(
                        src_ref=edge_ref,
                        dst_ref=halo.at[0 if d_lon > 0 else 1, lat + 2 + 1 - d_lat],
                        send_sem=halo_send.at[slot, 2],
                        recv_sem=halo_recv.at[slot, 2],
                        device_id=near(d_lat, d_lon),
                        device_id_type=MESH,
                    )
                )
        return copies

    def halo_cols(slot, halo):
        cols = halo.at[:, pl.ds(lat + 2, 3)]
        return pltpu.make_async_remote_copy(
            src_ref=cols,
            dst_ref=cols,
            send_sem=halo_send.at[slot, 2],
            recv_sem=halo_recv.at[slot, 2],
            device_id=near(0, 1),
            device_id_type=MESH,
        )

    def wait_halo(slot, copies, halo):
        copies[0].wait_recv()
        copies[1].wait_recv()
        halo_cols(slot, halo).wait_recv()

    def wait_halo_sent(slot, copies, halo):
        copies[0].wait_send()
        copies[1].wait_send()
        halo_cols(slot, halo).wait_send()

    strip = lat + 2
    extra = 3 * lon

    def column_source(shift):
        def source(i):
            a, b = i // lon, i % lon
            inner = a * lon + b + shift
            which = jnp.where(a == 0, 0, jnp.where(a == strip - 1, 2, 1))
            row = jnp.where(a == 0, lat - 1, jnp.where(a == strip - 1, 0, a - 1))
            base = (mem * lat if shift < 0 else 0) + row
            outer = strip * lon + which * lon + base
            edge = b == (0 if shift < 0 else lon - 1)
            return jnp.where(edge, outer, inner), edge

        return source

    def shifted(halo, body, m, shift):
        low = jnp.where(my_lat > 0, halo[m, 0].astype(F32), 0.0).astype(BF)
        high = jnp.where(my_lat < lats - 1, halo[m, strip - 1].astype(F32), 0.0).astype(BF)
        middle = body(m)
        field = jnp.concatenate([low, middle, high], axis=0)
        if shift == 0:
            return field
        side = 0 if shift < 0 else 1
        columns = halo[side, lat + 2 : lat + 5].reshape(extra, channels)
        shape = (strip * lon, strip * lon + extra)
        source, edge = column_source(shift)(iota(shape, 0))
        source = jnp.where(edge, source + m * lat, source)
        row = iota(shape, 0) // lon
        open_row = jnp.logical_and(
            jnp.logical_or(row > 0, my_lat > 0),
            jnp.logical_or(row < strip - 1, my_lat < lats - 1),
        )
        pick = jnp.where(jnp.logical_and(iota(shape, 1) == source, open_row), 1.0, 0.0).astype(BF)
        return nn(pick, jnp.concatenate([field, columns], axis=0)).astype(BF)

    def conv(halo, body, adjoint):
        total = None
        for c in range(3):
            shift = 1 - c if adjoint else c - 1
            wide = [shifted(halo, body, m, shift) for m in range(mem)]
            for r in range(3):
                start = (2 - r if adjoint else r) * lon
                window = jnp.concatenate([w[start : start + lat * lon] for w in wide], axis=0)
                term = nt(window, conv_ref[r, c]) if adjoint else nn(window, conv_ref[r, c])
                total = term if total is None else total + term
        return total

    def cot_body(m):
        return cot_ref[m].reshape(lat * lon, channels)

    def up_body(m):
        return field_ref[m].reshape(lat * lon, channels)

    ens = ens_ref[...].reshape(cells, channels)
    cot = cot_ref[...].reshape(cells, channels)
    packed = pack(nn(home_out, ens), peers)
    out_buf[X] = packed
    in_buf[X, 0] = packed[0]
    edge_cot[...] = nn(edges, cot).astype(BF)
    pl.semaphore_wait(barrier, peers - 1 + len(around))
    for copy in exchange(X, 1):
        copy.start()
    cot_copies = halo_copies(0, cot_ref, edge_cot, halo_cot)
    for copy in cot_copies:
        copy.start()

    ones = head_blocks(channels, members).astype(BF)
    gain = gain_ref[...]
    loads[0].wait()
    wait_halo(0, cot_copies, halo_cot)
    grad_field = cot.astype(F32) + conv(halo_cot, cot_body, True)
    gf_ref[...] = grad_field
    send(G, home_out, grad_field.astype(BF), 1)

    loads[1].wait()
    loads[2].wait()
    w_proj = w_proj_ref[...]
    w_out = w_out_ref[...]
    x = receive(X, cell_in).astype(BF)
    updated, saved = cell_forward(x, gain, w_proj, w_out, ones, members)
    send(U, cell_out, updated, -1)

    grads = receive(G, cell_in).astype(BF)
    grad_inputs = cell_backward(grads, saved, gain, w_proj, w_out, ones, members)
    send(B, cell_out, grad_inputs.astype(BF), -1)

    field = receive(U, home_in)
    field_ref[...] = field.astype(BF).reshape(field_ref.shape)
    edge_up[...] = nn(edges, field.astype(BF)).astype(BF)
    up_copies = halo_copies(1, field_ref, edge_up, halo_up)
    for copy in up_copies:
        copy.start()
    wait_halo(1, up_copies, halo_up)
    result = field + conv(halo_up, up_body, False)
    result_ref[...] = result.astype(BF).reshape(result_ref.shape)

    back = receive(B, home_in)
    grad_ref[...] = (gf_ref[...] + back).astype(BF).reshape(grad_ref.shape)

    for kind in (X, G, U, B):
        exchange_all(kind).wait_send()
    wait_halo_sent(0, cot_copies, halo_cot)
    wait_halo_sent(1, up_copies, halo_up)


MESH = pl.DeviceIdType.MESH


def per_device(ensemble, norm_gain, project_weight, output_weight, conv_kernel, cotangent):
    mem, lat, lon, channels = ensemble.shape
    peers = lax.axis_size("member")
    dims = (mem, lat, lon, channels, peers, lax.axis_size("lat"), lax.axis_size("lon"))
    vmem = pl.BlockSpec(memory_space=pltpu.VMEM)
    anywhere = pl.BlockSpec(memory_space=pl.ANY)
    chunk = (4, peers, 2 * mem * lat, channels // 2)
    halo = (mem, lat + 5, lon, channels)
    field = jax.ShapeDtypeStruct(ensemble.shape, BF)
    return pl.pallas_call(
        functools.partial(kernel, dims),
        out_shape=(field, field),
        in_specs=[vmem, vmem, anywhere, anywhere, anywhere, vmem],
        out_specs=(vmem, vmem),
        scratch_shapes=[
            pltpu.VMEM(project_weight.shape, BF),
            pltpu.VMEM(output_weight.shape, BF),
            pltpu.VMEM(conv_kernel.shape, BF),
            pltpu.VMEM(chunk, BF),
            pltpu.VMEM(chunk, BF),
            pltpu.VMEM(halo, BF),
            pltpu.VMEM(halo, BF),
            pltpu.VMEM((2 * mem * lat, channels), BF),
            pltpu.VMEM((2 * mem * lat, channels), BF),
            pltpu.VMEM(ensemble.shape, BF),
            pltpu.VMEM((mem * lat * lon, channels), F32),
            pltpu.SemaphoreType.DMA((3,)),
            pltpu.SemaphoreType.DMA((4,)),
            pltpu.SemaphoreType.DMA((4,)),
            pltpu.SemaphoreType.DMA((2, 3)),
            pltpu.SemaphoreType.DMA((2, 3)),
        ],
        compiler_params=pltpu.CompilerParams(collective_id=0, has_side_effects=True),
    )(
        ensemble,
        norm_gain.reshape(1, channels),
        project_weight,
        output_weight,
        conv_kernel,
        cotangent,
    )


def solution(mesh):
    field = P("member", "lat", "lon", None)
    return jax.shard_map(
        per_device,
        mesh=mesh,
        in_specs=(field, P(), P(), P(), P(), field),
        out_specs=(field, field),
        check_vma=False,
    )
```

```python
import functools
import math

import jax
import jax.numpy as jnp
from jax import lax
from jax.experimental import pallas as pl
from jax.experimental.pallas import tpu as pltpu
from jax.sharding import PartitionSpec as P

HEADS = 8
FLOOR = 0.5
EPSILON = 1e-06
BF = jnp.bfloat16
F32 = jnp.float32


def mm(a, b, dims):
    return lax.dot_general(a, b, (dims, ((), ())), preferred_element_type=F32)


def nn(a, b):
    return mm(a, b, ((1,), (0,)))


def nt(a, b):
    return mm(a, b, ((1,), (1,)))


def tn(a, b):
    return mm(a, b, ((0,), (0,)))


def head_blocks(channels, members):
    width = channels // HEADS
    row = lax.broadcasted_iota(jnp.int32, (HEADS * members, channels), 0) // members
    col = lax.broadcasted_iota(jnp.int32, (HEADS * members, channels), 1) // width
    return row == col


def spread(rows, blocks):
    return jnp.concatenate([rows] * HEADS, axis=0) * blocks


def head_scale(raw, ones):
    width = raw.shape[1] // HEADS
    mean_sq = nn((raw * raw).astype(BF), ones) * (1.0 / width)
    factor = lax.rsqrt(jnp.maximum(mean_sq, FLOOR))
    live = jnp.where(mean_sq > FLOOR, 1.0, jnp.where(mean_sq == FLOOR, 0.5, 0.0))
    return factor, live


def cell_forward(x, gain, w_proj, w_out, ones, members):
    rows, channels = x.shape
    cells = rows // members
    scale = 1.0 / math.sqrt(channels // HEADS)
    inputs = x.astype(F32)
    inv = lax.rsqrt(jnp.mean(inputs * inputs, axis=-1, keepdims=True) + EPSILON)
    normed = (inputs * inv * gain).astype(BF)
    proj = nn(normed, w_proj).astype(BF)
    q_raw = proj[:, :channels].astype(F32)
    k_raw = proj[:, channels : 2 * channels].astype(F32)
    values = proj[:, 2 * channels :]
    q_fac, q_live = head_scale(q_raw, ones)
    k_fac, k_live = head_scale(k_raw, ones)
    queries = (q_raw * q_fac).astype(BF)
    keys = (k_raw * k_fac).astype(BF)
    part = [slice(c * members, (c + 1) * members) for c in range(cells)]
    k_bd = [spread(keys[s], ones) for s in part]
    v_bd = [spread(values[s], ones) for s in part]
    scores = jnp.concatenate([nt(queries[s], k) for s, k in zip(part, k_bd)], axis=0)
    expd = jnp.exp(scores * scale)
    soft = expd / nn(expd.astype(BF), ones)
    rounded = soft.astype(BF)
    mixed = jnp.concatenate([nn(rounded[s], v) for s, v in zip(part, v_bd)], axis=0).astype(BF)
    updated = (inputs + nn(mixed, w_out)).astype(BF)
    saved = (inputs, inv, q_raw, k_raw, q_fac, k_fac, q_live, k_live, queries, k_bd, v_bd, soft, rounded)
    return updated, saved


def head_pull(raw, factor, live, grad, ones):
    width = raw.shape[1] // HEADS
    inner = nn((raw * grad).astype(BF), ones) * (1.0 / width)
    return grad * factor - raw * (factor * factor * factor * live * inner)


def fold(full, ones, members):
    kept = full * ones.astype(F32)
    total = kept[:members]
    for h in range(1, HEADS):
        total = total + kept[h * members : (h + 1) * members]
    return total


def cell_backward(grad_field, saved, gain, w_proj, w_out, ones, members):
    inputs, inv, q_raw, k_raw, q_fac, k_fac, q_live, k_live, queries, k_bd, v_bd, soft, rounded = saved
    rows, channels = inputs.shape
    cells = rows // members
    scale = 1.0 / math.sqrt(channels // HEADS)
    part = [slice(c * members, (c + 1) * members) for c in range(cells)]
    grad_mixed = nt(grad_field, w_out).astype(BF)
    dprob = jnp.concatenate([nt(grad_mixed[s], v) for s, v in zip(part, v_bd)], axis=0)
    delta = nn((soft * dprob).astype(BF), ones)
    dscore = (soft * (dprob - delta)).astype(BF)
    q_grad = jnp.concatenate([nn(dscore[s], k) for s, k in zip(part, k_bd)], axis=0) * scale
    k_grad = jnp.concatenate([fold(tn(dscore[s], queries[s]), ones, members) for s in part], axis=0) * scale
    v_grad = jnp.concatenate([fold(tn(rounded[s], grad_mixed[s]), ones, members) for s in part], axis=0)
    gq = head_pull(q_raw, q_fac, q_live, q_grad, ones).astype(BF)
    gk = head_pull(k_raw, k_fac, k_live, k_grad, ones).astype(BF)
    gv = v_grad.astype(BF)
    grad_normed = (
        nt(gq, w_proj[:, :channels])
        + nt(gk, w_proj[:, channels : 2 * channels])
        + nt(gv, w_proj[:, 2 * channels :])
    )
    lifted = grad_normed * gain
    inner = jnp.mean(lifted * inputs, axis=-1, keepdims=True)
    return lifted * inv - inputs * (inv * inv * inv * inner)


def iota(shape, dim):
    return lax.broadcasted_iota(jnp.int32, shape, dim)


def one_hot(shape, source):
    return jnp.where(iota(shape, 1) == source(iota(shape, 0)), 1.0, 0.0).astype(BF)


def pack(rows, peers):
    half = rows.shape[1] // 2
    per = rows.shape[0] // peers
    low = rows[:, :half].reshape(peers, per, half)
    high = rows[:, half:].reshape(peers, per, half)
    return jnp.concatenate([low, high], axis=1).astype(BF)


def unpack(chunks):
    peers, double, half = chunks.shape
    wide = chunks.astype(F32)
    low = wide[:, : double // 2].reshape(peers * double // 2, half)
    high = wide[:, double // 2 :].reshape(peers * double // 2, half)
    return jnp.concatenate([low, high], axis=1).astype(BF)


X, G, U, B = range(4)


def kernel(
    dims,
    ens_any,
    gain_any,
    w_proj_any,
    w_out_any,
    conv_any,
    cot_any,
    result_ref,
    grad_ref,
    ens_ref,
    cot_ref,
    gain_ref,
    w_proj_ref,
    w_out_ref,
    conv_ref,
    out_buf,
    in_buf,
    halo_cot,
    halo_up,
    edge_cot,
    edge_up,
    field_ref,
    gf_ref,
    load_sem,
    ex_send,
    ex_recv,
    halo_send,
    halo_recv,
):
    mem, lat, lon, channels, peers, lats, lons = dims
    cells = mem * lat * lon
    members = mem * peers
    me = lax.axis_index("member")
    my_lat = lax.axis_index("lat")
    my_lon = lax.axis_index("lon")

    pairs = (
        (ens_any, ens_ref),
        (cot_any, cot_ref),
        (conv_any, conv_ref),
        (w_proj_any, w_proj_ref),
        (w_out_any, w_out_ref),
        (gain_any, gain_ref),
    )
    loads = [
        pltpu.make_async_copy(src, dst, load_sem.at[i]) for i, (src, dst) in enumerate(pairs)
    ]
    for load in loads:
        load.start()

    def partner(j):
        return {"member": lax.rem(me + j, peers)}

    def near(d_lat, d_lon):
        return {
            "lat": lax.rem(my_lat + d_lat + lats, lats),
            "lon": lax.rem(my_lon + d_lon + lons, lons),
        }

    around = [(a, b) for a in (-1, 0, 1) for b in (-1, 0, 1) if (a, b) != (0, 0)]
    barrier = pltpu.get_barrier_semaphore()
    far_first = sorted(range(1, peers), key=lambda j: -min(j, peers - j))
    for j in far_first:
        pl.semaphore_signal(barrier, inc=1, device_id=partner(j), device_id_type=MESH)
    for d_lat, d_lon in around:
        pl.semaphore_signal(barrier, inc=1, device_id=near(d_lat, d_lon), device_id_type=MESH)

    def home_source(i):
        j, m, a = i // (mem * lat), (i // lat) % mem, i % lat
        return (m * lat + a) * lon + lax.rem(me + j, peers)

    def home_target(i):
        m, a, b = i // (lat * lon), (i // lon) % lat, i % lon
        return lax.rem(b - me + peers, peers) * (mem * lat) + m * lat + a

    def cell_source(i):
        c, j, m = i // members, (i // mem) % peers, i % mem
        return (j * mem + m) * lat + c

    def cell_target(i):
        j, m, c = i // (mem * lat), (i // lat) % mem, i % lat
        return (c * peers + j) * mem + m

    def edge_source(i):
        count = mem * lat
        return (i % count) * lon + (i // count) * (lon - 1)

    square = (cells, cells)
    home_out = one_hot(square, home_source)
    home_in = one_hot(square, home_target)
    cell_in = one_hot(square, cell_source)
    cell_out = one_hot(square, cell_target)
    edges = one_hot((2 * mem * lat, cells), edge_source)

    def exchange(kind, sign):
        return [
            pltpu.make_async_remote_copy(
                src_ref=out_buf.at[kind, j],
                dst_ref=in_buf.at[kind, j],
                send_sem=ex_send.at[kind],
                recv_sem=ex_recv.at[kind],
                device_id=partner(j if sign > 0 else peers - j),
                device_id_type=MESH,
            )
            for j in far_first
        ]

    def exchange_all(kind):
        return pltpu.make_async_remote_copy(
            src_ref=out_buf.at[kind, pl.ds(1, peers - 1)],
            dst_ref=in_buf.at[kind, pl.ds(1, peers - 1)],
            send_sem=ex_send.at[kind],
            recv_sem=ex_recv.at[kind],
            device_id=partner(1),
            device_id_type=MESH,
        )

    def send(kind, order, rows, sign):
        packed = pack(nn(order, rows), peers)
        out_buf[kind] = packed
        in_buf[kind, 0] = packed[0]
        for copy in exchange(kind, sign):
            copy.start()

    def receive(kind, order):
        exchange_all(kind).wait_recv()
        return nn(order, unpack(in_buf[kind]))

    def halo_copies(slot, rows_ref, edge_ref, halo):
        copies = []
        for side, (d_lat, a) in enumerate(((1, lat - 1), (-1, 0))):
            copies.append(
                pltpu.make_async_remote_copy(
                    src_ref=rows_ref.at[:, a],
                    dst_ref=halo.at[:, 0 if side == 0 else lat + 1],
                    send_sem=halo_send.at[slot, side],
                    recv_sem=halo_recv.at[slot, side],
                    device_id=near(d_lat, 0),
                    device_id_type=MESH,
                )
            )
        for d_lat in (-1, 0, 1):
            for d_lon in (-1, 1):
                copies.append(
                    pltpu.make_async_remote_copy(
                        src_ref=edge_ref,
                        dst_ref=halo.at[0 if d_lon > 0 else 1, lat + 2 + 1 - d_lat],
                        send_sem=halo_send.at[slot, 2],
                        recv_sem=halo_recv.at[slot, 2],
                        device_id=near(d_lat, d_lon),
                        device_id_type=MESH,
                    )
                )
        return copies

    def halo_cols(slot, halo):
        cols = halo.at[:, pl.ds(lat + 2, 3)]
        return pltpu.make_async_remote_copy(
            src_ref=cols,
            dst_ref=cols,
            send_sem=halo_send.at[slot, 2],
            recv_sem=halo_recv.at[slot, 2],
            device_id=near(0, 1),
            device_id_type=MESH,
        )

    def wait_halo(slot, copies, halo):
        copies[0].wait_recv()
        copies[1].wait_recv()
        halo_cols(slot, halo).wait_recv()

    def wait_halo_sent(slot, copies, halo):
        copies[0].wait_send()
        copies[1].wait_send()
        halo_cols(slot, halo).wait_send()

    strip = lat + 2
    extra = 3 * lon

    def column_source(shift):
        def source(i):
            a, b = i // lon, i % lon
            inner = a * lon + b + shift
            which = jnp.where(a == 0, 0, jnp.where(a == strip - 1, 2, 1))
            row = jnp.where(a == 0, lat - 1, jnp.where(a == strip - 1, 0, a - 1))
            base = (mem * lat if shift < 0 else 0) + row
            outer = strip * lon + which * lon + base
            edge = b == (0 if shift < 0 else lon - 1)
            return jnp.where(edge, outer, inner), edge

        return source

    def shifted(halo, body, m, shift):
        low = jnp.where(my_lat > 0, halo[m, 0].astype(F32), 0.0).astype(BF)
        high = jnp.where(my_lat < lats - 1, halo[m, strip - 1].astype(F32), 0.0).astype(BF)
        middle = body(m)
        field = jnp.concatenate([low, middle, high], axis=0)
        if shift == 0:
            return field
        side = 0 if shift < 0 else 1
        columns = halo[side, lat + 2 : lat + 5].reshape(extra, channels)
        shape = (strip * lon, strip * lon + extra)
        source, edge = column_source(shift)(iota(shape, 0))
        source = jnp.where(edge, source + m * lat, source)
        row = iota(shape, 0) // lon
        open_row = jnp.logical_and(
            jnp.logical_or(row > 0, my_lat > 0),
            jnp.logical_or(row < strip - 1, my_lat < lats - 1),
        )
        pick = jnp.where(jnp.logical_and(iota(shape, 1) == source, open_row), 1.0, 0.0).astype(BF)
        return nn(pick, jnp.concatenate([field, columns], axis=0)).astype(BF)

    def conv(halo, body, adjoint):
        total = None
        for c in range(3):
            shift = 1 - c if adjoint else c - 1
            wide = [shifted(halo, body, m, shift) for m in range(mem)]
            for r in range(3):
                start = (2 - r if adjoint else r) * lon
                window = jnp.concatenate([w[start : start + lat * lon] for w in wide], axis=0)
                term = nt(window, conv_ref[r, c]) if adjoint else nn(window, conv_ref[r, c])
                total = term if total is None else total + term
        return total

    def cot_body(m):
        return cot_ref[m].reshape(lat * lon, channels)

    def up_body(m):
        return field_ref[m].reshape(lat * lon, channels)

    loads[0].wait()
    ens = ens_ref[...].reshape(cells, channels)
    loads[1].wait()
    cot = cot_ref[...].reshape(cells, channels)
    packed = pack(nn(home_out, ens), peers)
    out_buf[X] = packed
    in_buf[X, 0] = packed[0]
    edge_cot[...] = nn(edges, cot).astype(BF)
    pl.semaphore_wait(barrier, peers - 1 + len(around))
    for copy in exchange(X, 1):
        copy.start()
    cot_copies = halo_copies(0, cot_ref, edge_cot, halo_cot)
    for copy in cot_copies:
        copy.start()

    ones = head_blocks(channels, members).astype(BF)
    loads[2].wait()
    wait_halo(0, cot_copies, halo_cot)
    grad_field = cot.astype(F32) + conv(halo_cot, cot_body, True)
    gf_ref[...] = grad_field
    send(G, home_out, grad_field.astype(BF), 1)

    for load in loads[3:]:
        load.wait()
    gain = gain_ref[...]
    w_proj = w_proj_ref[...]
    w_out = w_out_ref[...]
    x = receive(X, cell_in).astype(BF)
    updated, saved = cell_forward(x, gain, w_proj, w_out, ones, members)
    send(U, cell_out, updated, -1)

    grads = receive(G, cell_in).astype(BF)
    grad_inputs = cell_backward(grads, saved, gain, w_proj, w_out, ones, members)
    send(B, cell_out, grad_inputs.astype(BF), -1)

    field = receive(U, home_in)
    field_ref[...] = field.astype(BF).reshape(field_ref.shape)
    edge_up[...] = nn(edges, field.astype(BF)).astype(BF)
    up_copies = halo_copies(1, field_ref, edge_up, halo_up)
    for copy in up_copies:
        copy.start()
    wait_halo(1, up_copies, halo_up)
    result = field + conv(halo_up, up_body, False)
    result_ref[...] = result.astype(BF).reshape(result_ref.shape)

    back = receive(B, home_in)
    grad_ref[...] = (gf_ref[...] + back).astype(BF).reshape(grad_ref.shape)

    for kind in (X, G, U, B):
        exchange_all(kind).wait_send()
    wait_halo_sent(0, cot_copies, halo_cot)
    wait_halo_sent(1, up_copies, halo_up)


def store_kernel(result_in, grad_in, result_out, grad_out, sem):
    copies = [
        pltpu.make_async_copy(result_in, result_out, sem.at[0]),
        pltpu.make_async_copy(grad_in, grad_out, sem.at[1]),
    ]
    for copy in copies:
        copy.start()
    for copy in copies:
        copy.wait()


MESH = pl.DeviceIdType.MESH
LIMIT = 16 * 1024 * 1024


def per_device(ensemble, norm_gain, project_weight, output_weight, conv_kernel, cotangent):
    mem, lat, lon, channels = ensemble.shape
    peers = lax.axis_size("member")
    dims = (mem, lat, lon, channels, peers, lax.axis_size("lat"), lax.axis_size("lon"))
    vmem = pl.BlockSpec(memory_space=pltpu.VMEM)
    anywhere = pl.BlockSpec(memory_space=pl.ANY)
    chunk = (4, peers, 2 * mem * lat, channels // 2)
    halo = (mem, lat + 5, lon, channels)
    field = jax.ShapeDtypeStruct(ensemble.shape, BF)
    outs = pl.pallas_call(
        functools.partial(kernel, dims),
        out_shape=(field, field),
        in_specs=[pl.BlockSpec(memory_space=pltpu.HBM)] * 6,
        out_specs=(vmem, vmem),
        scratch_shapes=[
            pltpu.VMEM(ensemble.shape, BF),
            pltpu.VMEM(ensemble.shape, BF),
            pltpu.VMEM((1, channels), F32),
            pltpu.VMEM(project_weight.shape, BF),
            pltpu.VMEM(output_weight.shape, BF),
            pltpu.VMEM(conv_kernel.shape, BF),
            pltpu.VMEM(chunk, BF),
            pltpu.VMEM(chunk, BF),
            pltpu.VMEM(halo, BF),
            pltpu.VMEM(halo, BF),
            pltpu.VMEM((2 * mem * lat, channels), BF),
            pltpu.VMEM((2 * mem * lat, channels), BF),
            pltpu.VMEM(ensemble.shape, BF),
            pltpu.VMEM((mem * lat * lon, channels), F32),
            pltpu.SemaphoreType.DMA((6,)),
            pltpu.SemaphoreType.DMA((4,)),
            pltpu.SemaphoreType.DMA((4,)),
            pltpu.SemaphoreType.DMA((2, 3)),
            pltpu.SemaphoreType.DMA((2, 3)),
        ],
        compiler_params=pltpu.CompilerParams(
            collective_id=0, has_side_effects=True, vmem_limit_bytes=LIMIT
        ),
    )(
        *(
            pltpu.with_memory_space_constraint(value, pltpu.HBM)
            for value in (
                ensemble,
                norm_gain.reshape(1, channels),
                project_weight,
                output_weight,
                conv_kernel,
                cotangent,
            )
        )
    )
    return pl.pallas_call(
        store_kernel,
        out_shape=(field, field),
        in_specs=[vmem, vmem],
        out_specs=(anywhere, anywhere),
        scratch_shapes=[pltpu.SemaphoreType.DMA((2,))],
        compiler_params=pltpu.CompilerParams(vmem_limit_bytes=LIMIT),
    )(*outs)


def solution(mesh):
    field = P("member", "lat", "lon", None)
    return jax.shard_map(
        per_device,
        mesh=mesh,
        in_specs=(field, P(), P(), P(), P(), field),
        out_specs=(field, field),
        check_vma=False,
    )
```

```python
import functools
import math

import jax
import jax.numpy as jnp
from jax import lax
from jax.experimental import pallas as pl
from jax.experimental.pallas import tpu as pltpu
from jax.sharding import PartitionSpec as P

HEADS = 8
FLOOR = 0.5
EPSILON = 1e-06
BF = jnp.bfloat16
F32 = jnp.float32


def mm(a, b, dims):
    return lax.dot_general(a, b, (dims, ((), ())), preferred_element_type=F32)


def nn(a, b):
    return mm(a, b, ((1,), (0,)))


def nt(a, b):
    return mm(a, b, ((1,), (1,)))


def tn(a, b):
    return mm(a, b, ((0,), (0,)))


def head_blocks(channels, members):
    width = channels // HEADS
    row = lax.broadcasted_iota(jnp.int32, (HEADS * members, channels), 0) // members
    col = lax.broadcasted_iota(jnp.int32, (HEADS * members, channels), 1) // width
    return row == col


def spread(rows, blocks):
    return jnp.concatenate([rows] * HEADS, axis=0) * blocks


def head_scale(raw, ones):
    width = raw.shape[1] // HEADS
    mean_sq = nn((raw * raw).astype(BF), ones) * (1.0 / width)
    factor = lax.rsqrt(jnp.maximum(mean_sq, FLOOR))
    live = jnp.where(mean_sq > FLOOR, 1.0, jnp.where(mean_sq == FLOOR, 0.5, 0.0))
    return factor, live


def cell_forward(x, gain, w_proj, w_out, ones, members):
    rows, channels = x.shape
    cells = rows // members
    scale = 1.0 / math.sqrt(channels // HEADS)
    inputs = x.astype(F32)
    inv = lax.rsqrt(jnp.mean(inputs * inputs, axis=-1, keepdims=True) + EPSILON)
    normed = (inputs * inv * gain).astype(BF)
    proj = nn(normed, w_proj).astype(BF)
    q_raw = proj[:, :channels].astype(F32)
    k_raw = proj[:, channels : 2 * channels].astype(F32)
    values = proj[:, 2 * channels :]
    q_fac, q_live = head_scale(q_raw, ones)
    k_fac, k_live = head_scale(k_raw, ones)
    queries = (q_raw * q_fac).astype(BF)
    keys = (k_raw * k_fac).astype(BF)
    part = [slice(c * members, (c + 1) * members) for c in range(cells)]
    k_bd = [spread(keys[s], ones) for s in part]
    v_bd = [spread(values[s], ones) for s in part]
    scores = jnp.concatenate([nt(queries[s], k) for s, k in zip(part, k_bd)], axis=0)
    expd = jnp.exp(scores * scale)
    soft = expd / nn(expd.astype(BF), ones)
    rounded = soft.astype(BF)
    mixed = jnp.concatenate([nn(rounded[s], v) for s, v in zip(part, v_bd)], axis=0).astype(BF)
    updated = (inputs + nn(mixed, w_out)).astype(BF)
    saved = (inputs, inv, q_raw, k_raw, q_fac, k_fac, q_live, k_live, queries, k_bd, v_bd, soft, rounded)
    return updated, saved


def head_pull(raw, factor, live, grad, ones):
    width = raw.shape[1] // HEADS
    inner = nn((raw * grad).astype(BF), ones) * (1.0 / width)
    return grad * factor - raw * (factor * factor * factor * live * inner)


def fold(full, ones, members):
    kept = full * ones.astype(F32)
    total = kept[:members]
    for h in range(1, HEADS):
        total = total + kept[h * members : (h + 1) * members]
    return total


def cell_backward(grad_field, saved, gain, w_proj, w_out, ones, members):
    inputs, inv, q_raw, k_raw, q_fac, k_fac, q_live, k_live, queries, k_bd, v_bd, soft, rounded = saved
    rows, channels = inputs.shape
    cells = rows // members
    scale = 1.0 / math.sqrt(channels // HEADS)
    part = [slice(c * members, (c + 1) * members) for c in range(cells)]
    grad_mixed = nt(grad_field, w_out).astype(BF)
    dprob = jnp.concatenate([nt(grad_mixed[s], v) for s, v in zip(part, v_bd)], axis=0)
    delta = nn((soft * dprob).astype(BF), ones)
    dscore = (soft * (dprob - delta)).astype(BF)
    q_grad = jnp.concatenate([nn(dscore[s], k) for s, k in zip(part, k_bd)], axis=0) * scale
    k_grad = jnp.concatenate([fold(tn(dscore[s], queries[s]), ones, members) for s in part], axis=0) * scale
    v_grad = jnp.concatenate([fold(tn(rounded[s], grad_mixed[s]), ones, members) for s in part], axis=0)
    gq = head_pull(q_raw, q_fac, q_live, q_grad, ones).astype(BF)
    gk = head_pull(k_raw, k_fac, k_live, k_grad, ones).astype(BF)
    gv = v_grad.astype(BF)
    grad_normed = (
        nt(gq, w_proj[:, :channels])
        + nt(gk, w_proj[:, channels : 2 * channels])
        + nt(gv, w_proj[:, 2 * channels :])
    )
    lifted = grad_normed * gain
    inner = jnp.mean(lifted * inputs, axis=-1, keepdims=True)
    return lifted * inv - inputs * (inv * inv * inv * inner)


def iota(shape, dim):
    return lax.broadcasted_iota(jnp.int32, shape, dim)


def one_hot(shape, source):
    return jnp.where(iota(shape, 1) == source(iota(shape, 0)), 1.0, 0.0).astype(BF)


def pack(rows, peers):
    half = rows.shape[1] // 2
    per = rows.shape[0] // peers
    low = rows[:, :half].reshape(peers, per, half)
    high = rows[:, half:].reshape(peers, per, half)
    return jnp.concatenate([low, high], axis=1).astype(BF)


def unpack(chunks):
    peers, double, half = chunks.shape
    wide = chunks.astype(F32)
    low = wide[:, : double // 2].reshape(peers * double // 2, half)
    high = wide[:, double // 2 :].reshape(peers * double // 2, half)
    return jnp.concatenate([low, high], axis=1).astype(BF)


X, G, U, B = range(4)


def kernel(
    dims,
    ens_any,
    gain_any,
    w_proj_any,
    w_out_any,
    conv_any,
    cot_any,
    result_ref,
    grad_ref,
    ens_ref,
    cot_ref,
    gain_ref,
    w_proj_ref,
    w_out_ref,
    conv_ref,
    out_buf,
    in_buf,
    halo_cot,
    halo_up,
    edge_cot,
    edge_up,
    field_ref,
    gf_ref,
    load_sem,
    ex_send,
    ex_recv,
    halo_send,
    halo_recv,
    flag,
):
    mem, lat, lon, channels, peers, lats, lons = dims
    cells = mem * lat * lon
    members = mem * peers
    me = lax.axis_index("member")
    my_lat = lax.axis_index("lat")
    my_lon = lax.axis_index("lon")

    pairs = (
        (ens_any, ens_ref),
        (cot_any, cot_ref),
        (conv_any, conv_ref),
        (w_proj_any, w_proj_ref),
        (w_out_any, w_out_ref),
        (gain_any, gain_ref),
    )
    loads = [
        pltpu.make_async_copy(src, dst, load_sem.at[i]) for i, (src, dst) in enumerate(pairs)
    ]
    for load in loads:
        load.start()

    def partner(j):
        return {"member": lax.rem(me + j, peers)}

    def near(d_lat, d_lon):
        return {
            "lat": lax.rem(my_lat + d_lat + lats, lats),
            "lon": lax.rem(my_lon + d_lon + lons, lons),
        }

    around = [(a, b) for a in (-1, 0, 1) for b in (-1, 0, 1) if (a, b) != (0, 0)]
    barrier = pltpu.get_barrier_semaphore()
    far_first = sorted(range(1, peers), key=lambda j: -min(j, peers - j))
    ring = peers // 2
    my_z, my_y = me // 2, lax.rem(me, 2)

    def along(dz):
        return {"member": lax.rem(my_z + dz + ring, ring) * 2 + my_y}

    twin = {"member": my_z * 2 + 1 - my_y}
    close = [along(dz) for dz in (-2, 2, -1, 1)] + [twin]
    for device in close:
        pl.semaphore_signal(barrier, inc=1, device_id=device, device_id_type=MESH)
    for d_lat, d_lon in around:
        pl.semaphore_signal(barrier, inc=1, device_id=near(d_lat, d_lon), device_id_type=MESH)

    def home_source(i):
        j, m, a = i // (mem * lat), (i // lat) % mem, i % lat
        return (m * lat + a) * lon + lax.rem(me + j, peers)

    def home_target(i):
        m, a, b = i // (lat * lon), (i // lon) % lat, i % lon
        return lax.rem(b - me + peers, peers) * (mem * lat) + m * lat + a

    def cell_source(i):
        c, j, m = i // members, (i // mem) % peers, i % mem
        return (j * mem + m) * lat + c

    def cell_target(i):
        j, m, c = i // (mem * lat), (i // lat) % mem, i % lat
        return (c * peers + j) * mem + m

    def edge_source(i):
        count = mem * lat
        return (i % count) * lon + (i // count) * (lon - 1)

    square = (cells, cells)
    home_out = one_hot(square, home_source)
    home_in = one_hot(square, home_target)
    cell_in = one_hot(square, cell_source)
    cell_out = one_hot(square, cell_target)
    edges = one_hot((2 * mem * lat, cells), edge_source)

    def exchange(kind, sign):
        return [
            pltpu.make_async_remote_copy(
                src_ref=out_buf.at[kind, j],
                dst_ref=in_buf.at[kind, j],
                send_sem=ex_send.at[kind],
                recv_sem=ex_recv.at[kind],
                device_id=partner(j if sign > 0 else peers - j),
                device_id_type=MESH,
            )
            for j in far_first
        ]

    def exchange_all(kind):
        return pltpu.make_async_remote_copy(
            src_ref=out_buf.at[kind, pl.ds(1, peers - 1)],
            dst_ref=in_buf.at[kind, pl.ds(1, peers - 1)],
            send_sem=ex_send.at[kind],
            recv_sem=ex_recv.at[kind],
            device_id=partner(1),
            device_id_type=MESH,
        )

    def send(kind, order, rows, sign):
        packed = pack(nn(order, rows), peers)
        out_buf[kind] = packed
        in_buf[kind, 0] = packed[0]
        for copy in exchange(kind, sign):
            copy.start()

    def receive(kind, order):
        exchange_all(kind).wait_recv()
        return nn(order, unpack(in_buf[kind]))

    def halo_copies(slot, rows_ref, edge_ref, halo):
        copies = []
        for side, (d_lat, a) in enumerate(((1, lat - 1), (-1, 0))):
            copies.append(
                pltpu.make_async_remote_copy(
                    src_ref=rows_ref.at[:, a],
                    dst_ref=halo.at[:, 0 if side == 0 else lat + 1],
                    send_sem=halo_send.at[slot, side],
                    recv_sem=halo_recv.at[slot, side],
                    device_id=near(d_lat, 0),
                    device_id_type=MESH,
                )
            )
        for d_lat in (-1, 0, 1):
            for d_lon in (-1, 1):
                copies.append(
                    pltpu.make_async_remote_copy(
                        src_ref=edge_ref,
                        dst_ref=halo.at[0 if d_lon > 0 else 1, lat + 2 + 1 - d_lat],
                        send_sem=halo_send.at[slot, 2],
                        recv_sem=halo_recv.at[slot, 2],
                        device_id=near(d_lat, d_lon),
                        device_id_type=MESH,
                    )
                )
        return copies

    def halo_cols(slot, halo):
        cols = halo.at[:, pl.ds(lat + 2, 3)]
        return pltpu.make_async_remote_copy(
            src_ref=cols,
            dst_ref=cols,
            send_sem=halo_send.at[slot, 2],
            recv_sem=halo_recv.at[slot, 2],
            device_id=near(0, 1),
            device_id_type=MESH,
        )

    def wait_halo(slot, copies, halo):
        copies[0].wait_recv()
        copies[1].wait_recv()
        halo_cols(slot, halo).wait_recv()

    def wait_halo_sent(slot, copies, halo):
        copies[0].wait_send()
        copies[1].wait_send()
        halo_cols(slot, halo).wait_send()

    strip = lat + 2
    extra = 3 * lon

    def column_source(shift):
        def source(i):
            a, b = i // lon, i % lon
            inner = a * lon + b + shift
            which = jnp.where(a == 0, 0, jnp.where(a == strip - 1, 2, 1))
            row = jnp.where(a == 0, lat - 1, jnp.where(a == strip - 1, 0, a - 1))
            base = (mem * lat if shift < 0 else 0) + row
            outer = strip * lon + which * lon + base
            edge = b == (0 if shift < 0 else lon - 1)
            return jnp.where(edge, outer, inner), edge

        return source

    def shifted(halo, body, m, shift):
        low = jnp.where(my_lat > 0, halo[m, 0].astype(F32), 0.0).astype(BF)
        high = jnp.where(my_lat < lats - 1, halo[m, strip - 1].astype(F32), 0.0).astype(BF)
        middle = body(m)
        field = jnp.concatenate([low, middle, high], axis=0)
        if shift == 0:
            return field
        side = 0 if shift < 0 else 1
        columns = halo[side, lat + 2 : lat + 5].reshape(extra, channels)
        shape = (strip * lon, strip * lon + extra)
        source, edge = column_source(shift)(iota(shape, 0))
        source = jnp.where(edge, source + m * lat, source)
        row = iota(shape, 0) // lon
        open_row = jnp.logical_and(
            jnp.logical_or(row > 0, my_lat > 0),
            jnp.logical_or(row < strip - 1, my_lat < lats - 1),
        )
        pick = jnp.where(jnp.logical_and(iota(shape, 1) == source, open_row), 1.0, 0.0).astype(BF)
        return nn(pick, jnp.concatenate([field, columns], axis=0)).astype(BF)

    def conv(halo, body, adjoint):
        total = None
        for c in range(3):
            shift = 1 - c if adjoint else c - 1
            wide = [shifted(halo, body, m, shift) for m in range(mem)]
            for r in range(3):
                start = (2 - r if adjoint else r) * lon
                window = jnp.concatenate([w[start : start + lat * lon] for w in wide], axis=0)
                term = nt(window, conv_ref[r, c]) if adjoint else nn(window, conv_ref[r, c])
                total = term if total is None else total + term
        return total

    def cot_body(m):
        return cot_ref[m].reshape(lat * lon, channels)

    def up_body(m):
        return field_ref[m].reshape(lat * lon, channels)

    loads[0].wait()
    ens = ens_ref[...].reshape(cells, channels)
    loads[1].wait()
    cot = cot_ref[...].reshape(cells, channels)
    packed = pack(nn(home_out, ens), peers)
    out_buf[X] = packed
    in_buf[X, 0] = packed[0]
    edge_cot[...] = nn(edges, cot).astype(BF)
    pl.semaphore_wait(barrier, len(close) + len(around))
    for device in (along(-2), along(2), twin):
        pl.semaphore_signal(flag.at[0], inc=1, device_id=device, device_id_type=MESH)
    cot_copies = halo_copies(0, cot_ref, edge_cot, halo_cot)
    for copy in cot_copies:
        copy.start()
    pl.semaphore_wait(flag.at[0], 3)
    for device in (along(-2), along(2)):
        pl.semaphore_signal(flag.at[1], inc=1, device_id=device, device_id_type=MESH)
    pl.semaphore_wait(flag.at[1], 2)
    for copy in exchange(X, 1):
        copy.start()

    ones = head_blocks(channels, members).astype(BF)
    loads[2].wait()
    wait_halo(0, cot_copies, halo_cot)
    grad_field = cot.astype(F32) + conv(halo_cot, cot_body, True)
    gf_ref[...] = grad_field
    send(G, home_out, grad_field.astype(BF), 1)

    for load in loads[3:]:
        load.wait()
    gain = gain_ref[...]
    w_proj = w_proj_ref[...]
    w_out = w_out_ref[...]
    x = receive(X, cell_in).astype(BF)
    updated, saved = cell_forward(x, gain, w_proj, w_out, ones, members)
    send(U, cell_out, updated, -1)

    grads = receive(G, cell_in).astype(BF)
    grad_inputs = cell_backward(grads, saved, gain, w_proj, w_out, ones, members)
    send(B, cell_out, grad_inputs.astype(BF), -1)

    field = receive(U, home_in)
    field_ref[...] = field.astype(BF).reshape(field_ref.shape)
    edge_up[...] = nn(edges, field.astype(BF)).astype(BF)
    up_copies = halo_copies(1, field_ref, edge_up, halo_up)
    for copy in up_copies:
        copy.start()
    wait_halo(1, up_copies, halo_up)
    result = field + conv(halo_up, up_body, False)
    result_ref[...] = result.astype(BF).reshape(result_ref.shape)

    back = receive(B, home_in)
    grad_ref[...] = (gf_ref[...] + back).astype(BF).reshape(grad_ref.shape)

    for kind in (X, G, U, B):
        exchange_all(kind).wait_send()
    wait_halo_sent(0, cot_copies, halo_cot)
    wait_halo_sent(1, up_copies, halo_up)


def store_kernel(result_in, grad_in, result_out, grad_out, sem):
    copies = [
        pltpu.make_async_copy(result_in, result_out, sem.at[0]),
        pltpu.make_async_copy(grad_in, grad_out, sem.at[1]),
    ]
    for copy in copies:
        copy.start()
    for copy in copies:
        copy.wait()


MESH = pl.DeviceIdType.MESH
LIMIT = 16 * 1024 * 1024


def per_device(ensemble, norm_gain, project_weight, output_weight, conv_kernel, cotangent):
    mem, lat, lon, channels = ensemble.shape
    peers = lax.axis_size("member")
    dims = (mem, lat, lon, channels, peers, lax.axis_size("lat"), lax.axis_size("lon"))
    vmem = pl.BlockSpec(memory_space=pltpu.VMEM)
    anywhere = pl.BlockSpec(memory_space=pl.ANY)
    chunk = (4, peers, 2 * mem * lat, channels // 2)
    halo = (mem, lat + 5, lon, channels)
    field = jax.ShapeDtypeStruct(ensemble.shape, BF)
    outs = pl.pallas_call(
        functools.partial(kernel, dims),
        out_shape=(field, field),
        in_specs=[pl.BlockSpec(memory_space=pltpu.HBM)] * 6,
        out_specs=(vmem, vmem),
        scratch_shapes=[
            pltpu.VMEM(ensemble.shape, BF),
            pltpu.VMEM(ensemble.shape, BF),
            pltpu.VMEM((1, channels), F32),
            pltpu.VMEM(project_weight.shape, BF),
            pltpu.VMEM(output_weight.shape, BF),
            pltpu.VMEM(conv_kernel.shape, BF),
            pltpu.VMEM(chunk, BF),
            pltpu.VMEM(chunk, BF),
            pltpu.VMEM(halo, BF),
            pltpu.VMEM(halo, BF),
            pltpu.VMEM((2 * mem * lat, channels), BF),
            pltpu.VMEM((2 * mem * lat, channels), BF),
            pltpu.VMEM(ensemble.shape, BF),
            pltpu.VMEM((mem * lat * lon, channels), F32),
            pltpu.SemaphoreType.DMA((6,)),
            pltpu.SemaphoreType.DMA((4,)),
            pltpu.SemaphoreType.DMA((4,)),
            pltpu.SemaphoreType.DMA((2, 3)),
            pltpu.SemaphoreType.DMA((2, 3)),
            pltpu.SemaphoreType.REGULAR((2,)),
        ],
        compiler_params=pltpu.CompilerParams(
            collective_id=0, has_side_effects=True, vmem_limit_bytes=LIMIT
        ),
    )(
        *(
            pltpu.with_memory_space_constraint(value, pltpu.HBM)
            for value in (
                ensemble,
                norm_gain.reshape(1, channels),
                project_weight,
                output_weight,
                conv_kernel,
                cotangent,
            )
        )
    )
    return pl.pallas_call(
        store_kernel,
        out_shape=(field, field),
        in_specs=[vmem, vmem],
        out_specs=(anywhere, anywhere),
        scratch_shapes=[pltpu.SemaphoreType.DMA((2,))],
        compiler_params=pltpu.CompilerParams(vmem_limit_bytes=LIMIT),
    )(*outs)


def solution(mesh):
    field = P("member", "lat", "lon", None)
    return jax.shard_map(
        per_device,
        mesh=mesh,
        in_specs=(field, P(), P(), P(), P(), field),
        out_specs=(field, field),
        check_vma=False,
    )
```

```python
import functools
import math

import jax
import jax.numpy as jnp
from jax import lax
from jax.experimental import pallas as pl
from jax.experimental.pallas import tpu as pltpu
from jax.sharding import PartitionSpec as P

HEADS = 8
FLOOR = 0.5
EPSILON = 1e-06
BF = jnp.bfloat16
F32 = jnp.float32


def mm(a, b, dims):
    return lax.dot_general(a, b, (dims, ((), ())), preferred_element_type=F32)


def nn(a, b):
    return mm(a, b, ((1,), (0,)))


def nt(a, b):
    return mm(a, b, ((1,), (1,)))


def tn(a, b):
    return mm(a, b, ((0,), (0,)))


def head_blocks(channels, members):
    width = channels // HEADS
    row = lax.broadcasted_iota(jnp.int32, (HEADS * members, channels), 0) // members
    col = lax.broadcasted_iota(jnp.int32, (HEADS * members, channels), 1) // width
    return row == col


def spread(rows, blocks):
    return jnp.concatenate([rows] * HEADS, axis=0) * blocks


def head_scale(raw, ones):
    width = raw.shape[1] // HEADS
    mean_sq = nn((raw * raw).astype(BF), ones) * (1.0 / width)
    factor = lax.rsqrt(jnp.maximum(mean_sq, FLOOR))
    live = jnp.where(mean_sq > FLOOR, 1.0, jnp.where(mean_sq == FLOOR, 0.5, 0.0))
    return factor, live


def cell_forward(x, gain, w_proj, w_out, ones, members):
    rows, channels = x.shape
    cells = rows // members
    scale = 1.0 / math.sqrt(channels // HEADS)
    inputs = x.astype(F32)
    inv = lax.rsqrt(jnp.mean(inputs * inputs, axis=-1, keepdims=True) + EPSILON)
    normed = (inputs * inv * gain).astype(BF)
    proj = nn(normed, w_proj).astype(BF)
    q_raw = proj[:, :channels].astype(F32)
    k_raw = proj[:, channels : 2 * channels].astype(F32)
    values = proj[:, 2 * channels :]
    q_fac, q_live = head_scale(q_raw, ones)
    k_fac, k_live = head_scale(k_raw, ones)
    queries = (q_raw * q_fac).astype(BF)
    keys = (k_raw * k_fac).astype(BF)
    part = [slice(c * members, (c + 1) * members) for c in range(cells)]
    k_bd = [spread(keys[s], ones) for s in part]
    v_bd = [spread(values[s], ones) for s in part]
    scores = jnp.concatenate([nt(queries[s], k) for s, k in zip(part, k_bd)], axis=0)
    expd = jnp.exp(scores * scale)
    soft = expd / nn(expd.astype(BF), ones)
    rounded = soft.astype(BF)
    mixed = jnp.concatenate([nn(rounded[s], v) for s, v in zip(part, v_bd)], axis=0).astype(BF)
    updated = (inputs + nn(mixed, w_out)).astype(BF)
    saved = (inputs, inv, q_raw, k_raw, q_fac, k_fac, q_live, k_live, queries, k_bd, v_bd, soft, rounded)
    return updated, saved


def head_pull(raw, factor, live, grad, ones):
    width = raw.shape[1] // HEADS
    inner = nn((raw * grad).astype(BF), ones) * (1.0 / width)
    return grad * factor - raw * (factor * factor * factor * live * inner)


def fold(full, ones, members):
    kept = full * ones.astype(F32)
    total = kept[:members]
    for h in range(1, HEADS):
        total = total + kept[h * members : (h + 1) * members]
    return total


def cell_backward(grad_field, saved, gain, w_proj, w_out, ones, members):
    inputs, inv, q_raw, k_raw, q_fac, k_fac, q_live, k_live, queries, k_bd, v_bd, soft, rounded = saved
    rows, channels = inputs.shape
    cells = rows // members
    scale = 1.0 / math.sqrt(channels // HEADS)
    part = [slice(c * members, (c + 1) * members) for c in range(cells)]
    grad_mixed = nt(grad_field, w_out).astype(BF)
    dprob = jnp.concatenate([nt(grad_mixed[s], v) for s, v in zip(part, v_bd)], axis=0)
    delta = nn((soft * dprob).astype(BF), ones)
    dscore = (soft * (dprob - delta)).astype(BF)
    q_grad = jnp.concatenate([nn(dscore[s], k) for s, k in zip(part, k_bd)], axis=0) * scale
    k_grad = jnp.concatenate([fold(tn(dscore[s], queries[s]), ones, members) for s in part], axis=0) * scale
    v_grad = jnp.concatenate([fold(tn(rounded[s], grad_mixed[s]), ones, members) for s in part], axis=0)
    gq = head_pull(q_raw, q_fac, q_live, q_grad, ones).astype(BF)
    gk = head_pull(k_raw, k_fac, k_live, k_grad, ones).astype(BF)
    gv = v_grad.astype(BF)
    grad_normed = (
        nt(gq, w_proj[:, :channels])
        + nt(gk, w_proj[:, channels : 2 * channels])
        + nt(gv, w_proj[:, 2 * channels :])
    )
    lifted = grad_normed * gain
    inner = jnp.mean(lifted * inputs, axis=-1, keepdims=True)
    return lifted * inv - inputs * (inv * inv * inv * inner)


def iota(shape, dim):
    return lax.broadcasted_iota(jnp.int32, shape, dim)


def one_hot(shape, source):
    return jnp.where(iota(shape, 1) == source(iota(shape, 0)), 1.0, 0.0).astype(BF)


def pack(rows, peers):
    half = rows.shape[1] // 2
    per = rows.shape[0] // peers
    low = rows[:, :half].reshape(peers, per, half)
    high = rows[:, half:].reshape(peers, per, half)
    return jnp.concatenate([low, high], axis=1).astype(BF)


def unpack(chunks):
    peers, double, half = chunks.shape
    wide = chunks.astype(F32)
    low = wide[:, : double // 2].reshape(peers * double // 2, half)
    high = wide[:, double // 2 :].reshape(peers * double // 2, half)
    return jnp.concatenate([low, high], axis=1).astype(BF)


X, G, U, B = range(4)


def kernel(
    dims,
    ens_any,
    gain_any,
    w_proj_any,
    w_out_any,
    conv_any,
    cot_any,
    result_ref,
    grad_ref,
    ens_ref,
    cot_ref,
    gain_ref,
    w_proj_ref,
    w_out_ref,
    conv_ref,
    out_buf,
    in_buf,
    halo_cot,
    edge_cot,
    gf_ref,
    rim_out,
    rim_in,
    side_in,
    corner_in,
    column_ref,
    load_sem,
    ex_send,
    ex_recv,
    halo_send,
    halo_recv,
    rim_send,
    rim_recv,
    side_send,
    side_recv,
    corner_send,
    corner_recv,
    flag,
):
    mem, lat, lon, channels, peers, lats, lons = dims
    cells = mem * lat * lon
    members = mem * peers
    me = lax.axis_index("member")
    my_lat = lax.axis_index("lat")
    my_lon = lax.axis_index("lon")

    pairs = (
        (ens_any, ens_ref),
        (cot_any, cot_ref),
        (conv_any, conv_ref),
        (w_proj_any, w_proj_ref),
        (w_out_any, w_out_ref),
        (gain_any, gain_ref),
    )
    loads = [
        pltpu.make_async_copy(src, dst, load_sem.at[i]) for i, (src, dst) in enumerate(pairs)
    ]
    for load in loads:
        load.start()

    def partner(j):
        return {"member": lax.rem(me + j, peers)}

    def near(d_lat, d_lon):
        return {
            "lat": lax.rem(my_lat + d_lat + lats, lats),
            "lon": lax.rem(my_lon + d_lon + lons, lons),
        }

    around = [(a, b) for a in (-1, 0, 1) for b in (-1, 0, 1) if (a, b) != (0, 0)]
    barrier = pltpu.get_barrier_semaphore()
    far_first = sorted(range(1, peers), key=lambda j: -min(j, peers - j))
    ring = peers // 2
    my_z, my_y = me // 2, lax.rem(me, 2)

    def along(dz):
        return {"member": lax.rem(my_z + dz, ring) * 2 + my_y}

    twin = {"member": my_z * 2 + 1 - my_y}
    z_steps = sorted(range(1, ring), key=lambda j: -min(j, ring - j))
    close = [along(dz) for dz in z_steps] + [twin]
    for device in close:
        pl.semaphore_signal(barrier, inc=1, device_id=device, device_id_type=MESH)
    for d_lat, d_lon in around:
        pl.semaphore_signal(barrier, inc=1, device_id=near(d_lat, d_lon), device_id_type=MESH)

    def home_source(i):
        j, m, a = i // (mem * lat), (i // lat) % mem, i % lat
        return (m * lat + a) * lon + lax.rem(me + j, peers)

    def home_target(i):
        m, a, b = i // (lat * lon), (i // lon) % lat, i % lon
        return lax.rem(b - me + peers, peers) * (mem * lat) + m * lat + a

    def cell_source(i):
        c, j, m = i // members, (i // mem) % peers, i % mem
        return (j * mem + m) * lat + c

    def cell_target(i):
        j, m, c = i // (mem * lat), (i // lat) % mem, i % lat
        return (c * peers + j) * mem + m

    def edge_source(i):
        count = mem * lat
        return (i % count) * lon + (i // count) * (lon - 1)

    square = (cells, cells)
    home_out = one_hot(square, home_source)
    home_in = one_hot(square, home_target)
    cell_in = one_hot(square, cell_source)
    cell_out = one_hot(square, cell_target)
    edges = one_hot((2 * mem * lat, cells), edge_source)

    def exchange(kind, sign):
        return [
            pltpu.make_async_remote_copy(
                src_ref=out_buf.at[kind, j],
                dst_ref=in_buf.at[kind, j],
                send_sem=ex_send.at[kind],
                recv_sem=ex_recv.at[kind],
                device_id=partner(j if sign > 0 else peers - j),
                device_id_type=MESH,
            )
            for j in far_first
        ]

    def exchange_all(kind):
        return pltpu.make_async_remote_copy(
            src_ref=out_buf.at[kind, pl.ds(1, peers - 1)],
            dst_ref=in_buf.at[kind, pl.ds(1, peers - 1)],
            send_sem=ex_send.at[kind],
            recv_sem=ex_recv.at[kind],
            device_id=partner(1),
            device_id_type=MESH,
        )

    def send(kind, order, rows, sign):
        packed = pack(nn(order, rows), peers)
        out_buf[kind] = packed
        in_buf[kind, 0] = packed[0]
        for copy in exchange(kind, sign):
            copy.start()

    def receive(kind, order):
        exchange_all(kind).wait_recv()
        return nn(order, unpack(in_buf[kind]))

    has_low, has_high = my_lat > 0, my_lat < lats - 1

    def halo_group(d_lat):
        which = 1 - d_lat
        copies = [
            pltpu.make_async_remote_copy(
                src_ref=edge_cot,
                dst_ref=halo_cot.at[0 if d_lon > 0 else 1, lat + 2 + which],
                send_sem=halo_send.at[which],
                recv_sem=halo_recv.at[which],
                device_id=near(d_lat, d_lon),
                device_id_type=MESH,
            )
            for d_lon in (-1, 1)
        ]
        if d_lat:
            copies.append(
                pltpu.make_async_remote_copy(
                    src_ref=cot_ref.at[:, lat - 1 if d_lat > 0 else 0],
                    dst_ref=halo_cot.at[:, 0 if d_lat > 0 else lat + 1],
                    send_sem=halo_send.at[3 + (which > 1)],
                    recv_sem=halo_recv.at[3 + (which > 1)],
                    device_id=near(d_lat, 0),
                    device_id_type=MESH,
                )
            )
        return copies

    def halo_columns(which):
        columns = halo_cot.at[:, lat + 2 + which]
        return pltpu.make_async_remote_copy(
            src_ref=columns,
            dst_ref=columns,
            send_sem=halo_send.at[which],
            recv_sem=halo_recv.at[which],
            device_id=near(0, 1),
            device_id_type=MESH,
        )

    def start_halo():
        @pl.when(has_high)
        def _():
            for copy in halo_group(1):
                copy.start()

        @pl.when(has_low)
        def _():
            for copy in halo_group(-1):
                copy.start()

        for copy in halo_group(0):
            copy.start()

    def wait_halo():
        halo_columns(1).wait_recv()

        @pl.when(has_low)
        def _():
            halo_columns(0).wait_recv()
            halo_group(1)[2].wait_recv()

        @pl.when(has_high)
        def _():
            halo_columns(2).wait_recv()
            halo_group(-1)[2].wait_recv()

    def wait_halo_sent():
        halo_columns(1).wait_send()

        @pl.when(has_high)
        def _():
            halo_columns(0).wait_send()
            halo_group(1)[2].wait_send()

        @pl.when(has_low)
        def _():
            halo_columns(2).wait_send()
            halo_group(-1)[2].wait_send()

    every = [0] + far_first

    def shift_of(rim):
        return 1 if rim == 0 else lats - 1

    def home_of(j, d_lat, d_lon):
        return {
            "member": lax.rem(me + peers - j, peers),
            "lat": lax.rem(my_lat + d_lat, lats),
            "lon": lax.rem(my_lon + d_lon, lons),
        }

    def rim_copies(rim):
        return [
            pltpu.make_async_remote_copy(
                src_ref=rim_out.at[rim, j],
                dst_ref=rim_in.at[rim, j],
                send_sem=rim_send.at[rim],
                recv_sem=rim_recv.at[rim],
                device_id=home_of(j, shift_of(rim), 0),
                device_id_type=MESH,
            )
            for j in every
        ]

    def rim_all(rim):
        return pltpu.make_async_remote_copy(
            src_ref=rim_out.at[rim],
            dst_ref=rim_in.at[rim],
            send_sem=rim_send.at[rim],
            recv_sem=rim_recv.at[rim],
            device_id=home_of(0, shift_of(rim), 0),
            device_id_type=MESH,
        )

    def side_copies(side):
        return [
            pltpu.make_async_remote_copy(
                src_ref=out_buf.at[U, j],
                dst_ref=side_in.at[side],
                send_sem=side_send.at[side],
                recv_sem=side_recv.at[side],
                device_id=home_of(j, 0, 1 if side == 0 else lons - 1),
                device_id_type=MESH,
            )
            for j in every
        ]

    def side_all(side):
        return pltpu.make_async_remote_copy(
            src_ref=out_buf.at[U],
            dst_ref=out_buf.at[U],
            send_sem=side_send.at[side],
            recv_sem=side_recv.at[side],
            device_id=home_of(0, 0, 1),
            device_id_type=MESH,
        )

    def corner_copies(side, rim):
        return [
            pltpu.make_async_remote_copy(
                src_ref=rim_out.at[rim, j],
                dst_ref=corner_in.at[side, rim],
                send_sem=corner_send.at[side, rim],
                recv_sem=corner_recv.at[side, rim],
                device_id=home_of(j, shift_of(rim), 1 if side == 0 else lons - 1),
                device_id_type=MESH,
            )
            for j in every
        ]

    def corner_all(side, rim):
        return pltpu.make_async_remote_copy(
            src_ref=rim_out.at[rim],
            dst_ref=rim_in.at[rim],
            send_sem=corner_send.at[side, rim],
            recv_sem=corner_recv.at[side, rim],
            device_id=home_of(0, shift_of(rim), 1),
            device_id_type=MESH,
        )

    def sends_rim(rim):
        return has_high if rim == 0 else has_low

    def gets_rim(rim):
        return has_low if rim == 0 else has_high

    def sends_side(side):
        return me == (peers - 1 if side == 0 else 0)

    def start_rims():
        for side in range(2):

            @pl.when(sends_side(side))
            def _():
                for copy in side_copies(side):
                    copy.start()

        for rim in range(2):

            @pl.when(sends_rim(rim))
            def _():
                for copy in rim_copies(rim):
                    copy.start()

            for side in range(2):

                @pl.when(jnp.logical_and(sends_side(side), sends_rim(rim)))
                def _():
                    for copy in corner_copies(side, rim):
                        copy.start()

    def wait_rims():
        for side in range(2):
            side_copies(side)[0].wait_recv()
        for rim in range(2):

            @pl.when(gets_rim(rim))
            def _():
                rim_all(rim).wait_recv()
                for side in range(2):
                    corner_copies(side, rim)[0].wait_recv()

    def wait_rims_sent():
        for side in range(2):

            @pl.when(sends_side(side))
            def _():
                side_all(side).wait_send()

        for rim in range(2):

            @pl.when(sends_rim(rim))
            def _():
                rim_all(rim).wait_send()

            for side in range(2):

                @pl.when(jnp.logical_and(sends_side(side), sends_rim(rim)))
                def _():
                    corner_all(side, rim).wait_send()

    def rim_pack(rows):
        half = channels // 2
        shape = (2 * mem * peers, mem * peers)
        i, k = iota(shape, 0), iota(shape, 1)
        same = (i // (2 * mem)) * mem + i % mem == k
        upper = (i // mem) % 2 == 1
        low = jnp.where(jnp.logical_and(same, jnp.logical_not(upper)), 1.0, 0.0).astype(BF)
        high = jnp.where(jnp.logical_and(same, upper), 1.0, 0.0).astype(BF)
        return nn(low, rows[:, :half]) + nn(high, rows[:, half:])

    def rim_rows(rim):
        got = rim_in[rim].reshape(2 * mem * peers, channels // 2).astype(BF)
        shape = (mem * lon, 2 * mem * peers)
        i, k = iota(shape, 0), iota(shape, 1)
        row = lax.rem(i % lon - me + peers, peers) * (2 * mem) + i // lon
        low = jnp.where(k == row, 1.0, 0.0).astype(BF)
        high = jnp.where(k == row + mem, 1.0, 0.0).astype(BF)
        return jnp.concatenate([nn(low, got), nn(high, got)], axis=1).astype(BF)

    def side_column(side):
        half = channels // 2
        per = mem * lat
        main = side_in[side].astype(F32)
        column_ref[side, 0:per, 0:half] = main[:per]
        column_ref[side, 0:per, half:channels] = main[per:]
        for rim in range(2):
            at = per + rim * mem
            column_ref[side, at : at + mem, 0:half] = corner_in[side, rim, 0:mem]
            column_ref[side, at : at + mem, half:channels] = corner_in[side, rim, mem : 2 * mem]
        return column_ref[side].astype(BF)

    strip = lat + 2

    def cot_edge(m, shift, a):
        which = jnp.where(a == 0, 0, jnp.where(a == strip - 1, 2, 1))
        row = jnp.where(a == 0, lat - 1, jnp.where(a == strip - 1, 0, a - 1))
        return which * lon + (mem * lat if shift < 0 else 0) + m * lat + row

    def up_edge(m, shift, a):
        outer = mem * lat + m
        return jnp.where(a == 0, outer, jnp.where(a == strip - 1, outer + mem, m * lat + a - 1))

    def shifted(field, columns, edge_row, m, shift):
        if shift == 0:
            return field
        shape = (strip * lon, strip * lon + columns.shape[0])
        a, b = iota(shape, 0) // lon, iota(shape, 0) % lon
        outer = strip * lon + edge_row(m, shift, a)
        source = jnp.where(b == (0 if shift < 0 else lon - 1), outer, a * lon + b + shift)
        open_row = jnp.logical_and(
            jnp.logical_or(a > 0, has_low), jnp.logical_or(a < strip - 1, has_high)
        )
        pick = jnp.where(jnp.logical_and(iota(shape, 1) == source, open_row), 1.0, 0.0).astype(BF)
        return nn(pick, jnp.concatenate([field, columns], axis=0)).astype(BF)

    def conv(fields, columns, edge_row, adjoint):
        total = None
        for c in range(3):
            shift = 1 - c if adjoint else c - 1
            side = 0 if shift < 0 else 1
            wide = [shifted(fields[m], columns[side], edge_row, m, shift) for m in range(mem)]
            for r in range(3):
                start = (2 - r if adjoint else r) * lon
                window = jnp.concatenate([w[start : start + lat * lon] for w in wide], axis=0)
                term = nt(window, conv_ref[r, c]) if adjoint else nn(window, conv_ref[r, c])
                total = term if total is None else total + term
        return total

    def closed(rows, there):
        return jnp.where(there, rows.astype(F32), 0.0).astype(BF)

    @pl.when(jnp.logical_not(has_low))
    def _():
        halo_cot[:, 0] = jnp.zeros((mem, lon, channels), BF)
        halo_cot[:, lat + 2] = jnp.zeros((mem, lon, channels), BF)
        rim_in[0] = jnp.zeros(rim_in.shape[1:], F32)
        corner_in[:, 0] = jnp.zeros((2,) + corner_in.shape[2:], F32)

    @pl.when(jnp.logical_not(has_high))
    def _():
        halo_cot[:, lat + 1] = jnp.zeros((mem, lon, channels), BF)
        halo_cot[:, lat + 4] = jnp.zeros((mem, lon, channels), BF)
        rim_in[1] = jnp.zeros(rim_in.shape[1:], F32)
        corner_in[:, 1] = jnp.zeros((2,) + corner_in.shape[2:], F32)

    column_ref[...] = jnp.zeros(column_ref.shape, F32)
    loads[0].wait()
    ens = ens_ref[...].reshape(cells, channels)
    loads[1].wait()
    cot = cot_ref[...].reshape(cells, channels)
    packed = pack(nn(home_out, ens), peers)
    out_buf[X] = packed
    in_buf[X, 0] = packed[0]
    edge_cot[...] = nn(edges, cot).astype(BF)
    pl.semaphore_wait(barrier, len(close) + len(around))
    pl.semaphore_signal(flag, inc=1, device_id=twin, device_id_type=MESH)
    start_halo()
    copies = dict(zip(far_first, exchange(X, 1)))
    for j in far_first:
        if j % 2 == 0:
            copies[j].start()
    pl.semaphore_wait(flag, 1)
    for j in far_first:
        if j % 2 == 1:
            copies[j].start()

    ones = head_blocks(channels, members).astype(BF)
    loads[2].wait()
    wait_halo()
    cot_fields = [
        jnp.concatenate(
            [
                closed(halo_cot[m, 0], has_low),
                cot_ref[m].reshape(lat * lon, channels),
                closed(halo_cot[m, lat + 1], has_high),
            ],
            axis=0,
        )
        for m in range(mem)
    ]
    cot_columns = [halo_cot[side, lat + 2 : lat + 5].reshape(3 * lon, channels) for side in range(2)]
    grad_field = cot.astype(F32) + conv(cot_fields, cot_columns, cot_edge, True)
    gf_ref[...] = grad_field
    send(G, home_out, grad_field.astype(BF), 1)

    for load in loads[3:]:
        load.wait()
    gain = gain_ref[...]
    w_proj = w_proj_ref[...]
    w_out = w_out_ref[...]
    x = receive(X, cell_in).astype(BF)
    updated, saved = cell_forward(x, gain, w_proj, w_out, ones, members)
    send(U, cell_out, updated, -1)
    for rim, c in enumerate((lat - 1, 0)):
        rows = updated[c * members : (c + 1) * members]
        rim_out[rim] = rim_pack(rows).reshape(rim_out.shape[1:])
    start_rims()

    grads = receive(G, cell_in).astype(BF)
    grad_inputs = cell_backward(grads, saved, gain, w_proj, w_out, ones, members)
    send(B, cell_out, grad_inputs.astype(BF), -1)

    field = receive(U, home_in)
    wait_rims()
    rows = field.astype(BF)
    low = closed(rim_rows(0), has_low)
    high = closed(rim_rows(1), has_high)
    up_fields = [
        jnp.concatenate(
            [
                low[m * lon : (m + 1) * lon],
                rows[m * lat * lon : (m + 1) * lat * lon],
                high[m * lon : (m + 1) * lon],
            ],
            axis=0,
        )
        for m in range(mem)
    ]
    result = field + conv(up_fields, [side_column(0), side_column(1)], up_edge, False)
    result_ref[...] = result.astype(BF).reshape(result_ref.shape)

    back = receive(B, home_in)
    grad_ref[...] = (gf_ref[...] + back).astype(BF).reshape(grad_ref.shape)

    for kind in (X, G, U, B):
        exchange_all(kind).wait_send()
    wait_halo_sent()
    wait_rims_sent()


def store_kernel(result_in, grad_in, result_out, grad_out, sem):
    copies = [
        pltpu.make_async_copy(result_in, result_out, sem.at[0]),
        pltpu.make_async_copy(grad_in, grad_out, sem.at[1]),
    ]
    for copy in copies:
        copy.start()
    for copy in copies:
        copy.wait()


MESH = pl.DeviceIdType.MESH
LIMIT = 16 * 1024 * 1024


def per_device(ensemble, norm_gain, project_weight, output_weight, conv_kernel, cotangent):
    mem, lat, lon, channels = ensemble.shape
    peers = lax.axis_size("member")
    dims = (mem, lat, lon, channels, peers, lax.axis_size("lat"), lax.axis_size("lon"))
    vmem = pl.BlockSpec(memory_space=pltpu.VMEM)
    anywhere = pl.BlockSpec(memory_space=pl.ANY)
    chunk = (4, peers, 2 * mem * lat, channels // 2)
    halo = (mem, lat + 5, lon, channels)
    field = jax.ShapeDtypeStruct(ensemble.shape, BF)
    outs = pl.pallas_call(
        functools.partial(kernel, dims),
        out_shape=(field, field),
        in_specs=[pl.BlockSpec(memory_space=pltpu.HBM)] * 6,
        out_specs=(vmem, vmem),
        scratch_shapes=[
            pltpu.VMEM(ensemble.shape, BF),
            pltpu.VMEM(ensemble.shape, BF),
            pltpu.VMEM((1, channels), F32),
            pltpu.VMEM(project_weight.shape, BF),
            pltpu.VMEM(output_weight.shape, BF),
            pltpu.VMEM(conv_kernel.shape, BF),
            pltpu.VMEM(chunk, BF),
            pltpu.VMEM(chunk, BF),
            pltpu.VMEM(halo, BF),
            pltpu.VMEM((2 * mem * lat, channels), BF),
            pltpu.VMEM((mem * lat * lon, channels), F32),
            pltpu.VMEM((2, peers, 2 * mem, channels // 2), F32),
            pltpu.VMEM((2, peers, 2 * mem, channels // 2), F32),
            pltpu.VMEM((2, 2 * mem * lat, channels // 2), BF),
            pltpu.VMEM((2, 2, 2 * mem, channels // 2), F32),
            pltpu.VMEM((2, 16, channels), F32),
            pltpu.SemaphoreType.DMA((6,)),
            pltpu.SemaphoreType.DMA((4,)),
            pltpu.SemaphoreType.DMA((4,)),
            pltpu.SemaphoreType.DMA((5,)),
            pltpu.SemaphoreType.DMA((5,)),
            pltpu.SemaphoreType.DMA((2,)),
            pltpu.SemaphoreType.DMA((2,)),
            pltpu.SemaphoreType.DMA((2,)),
            pltpu.SemaphoreType.DMA((2,)),
            pltpu.SemaphoreType.DMA((2, 2)),
            pltpu.SemaphoreType.DMA((2, 2)),
            pltpu.SemaphoreType.REGULAR,
        ],
        compiler_params=pltpu.CompilerParams(
            collective_id=0, has_side_effects=True, vmem_limit_bytes=LIMIT
        ),
    )(
        *(
            pltpu.with_memory_space_constraint(value, pltpu.HBM)
            for value in (
                ensemble,
                norm_gain.reshape(1, channels),
                project_weight,
                output_weight,
                conv_kernel,
                cotangent,
            )
        )
    )
    return pl.pallas_call(
        store_kernel,
        out_shape=(field, field),
        in_specs=[vmem, vmem],
        out_specs=(anywhere, anywhere),
        scratch_shapes=[pltpu.SemaphoreType.DMA((2,))],
        compiler_params=pltpu.CompilerParams(vmem_limit_bytes=LIMIT),
    )(*outs)


def solution(mesh):
    field = P("member", "lat", "lon", None)
    return jax.shard_map(
        per_device,
        mesh=mesh,
        in_specs=(field, P(), P(), P(), P(), field),
        out_specs=(field, field),
        check_vma=False,
    )
```

```python
import functools
import math

import jax
import jax.numpy as jnp
from jax import lax
from jax.experimental import pallas as pl
from jax.experimental.pallas import tpu as pltpu
from jax.sharding import PartitionSpec as P

HEADS = 8
FLOOR = 0.5
EPSILON = 1e-06
BF = jnp.bfloat16
F32 = jnp.float32


def mm(a, b, dims):
    return lax.dot_general(a, b, (dims, ((), ())), preferred_element_type=F32)


def nn(a, b):
    return mm(a, b, ((1,), (0,)))


def nt(a, b):
    return mm(a, b, ((1,), (1,)))


def tn(a, b):
    return mm(a, b, ((0,), (0,)))


def head_blocks(channels, members):
    width = channels // HEADS
    row = lax.broadcasted_iota(jnp.int32, (HEADS * members, channels), 0) // members
    col = lax.broadcasted_iota(jnp.int32, (HEADS * members, channels), 1) // width
    return row == col


def spread(rows, blocks):
    return jnp.concatenate([rows] * HEADS, axis=0) * blocks


def head_scale(raw, ones):
    width = raw.shape[1] // HEADS
    mean_sq = nn((raw * raw).astype(BF), ones) * (1.0 / width)
    factor = lax.rsqrt(jnp.maximum(mean_sq, FLOOR))
    live = jnp.where(mean_sq > FLOOR, 1.0, jnp.where(mean_sq == FLOOR, 0.5, 0.0))
    return factor, live


def cell_forward(x, gain, w_proj, w_out, ones, members):
    rows, channels = x.shape
    cells = rows // members
    scale = 1.0 / math.sqrt(channels // HEADS)
    inputs = x.astype(F32)
    inv = lax.rsqrt(jnp.mean(inputs * inputs, axis=-1, keepdims=True) + EPSILON)
    normed = (inputs * inv * gain).astype(BF)
    proj = nn(normed, w_proj).astype(BF)
    q_raw = proj[:, :channels].astype(F32)
    k_raw = proj[:, channels : 2 * channels].astype(F32)
    values = proj[:, 2 * channels :]
    q_fac, q_live = head_scale(q_raw, ones)
    k_fac, k_live = head_scale(k_raw, ones)
    queries = (q_raw * q_fac).astype(BF)
    keys = (k_raw * k_fac).astype(BF)
    part = [slice(c * members, (c + 1) * members) for c in range(cells)]
    k_bd = [spread(keys[s], ones) for s in part]
    v_bd = [spread(values[s], ones) for s in part]
    scores = jnp.concatenate([nt(queries[s], k) for s, k in zip(part, k_bd)], axis=0)
    expd = jnp.exp(scores * scale)
    narrow = expd.astype(BF)
    inv_total = 1.0 / nn(narrow, ones)
    mixed = jnp.concatenate([nn(narrow[s], v) for s, v in zip(part, v_bd)], axis=0)
    updated = (inputs + nn((mixed * inv_total).astype(BF), w_out)).astype(BF)
    soft = expd * inv_total
    rounded = soft.astype(BF)
    saved = (inputs, inv, q_raw, k_raw, q_fac, k_fac, q_live, k_live, queries, k_bd, v_bd, soft, rounded)
    return updated, saved


def head_pull(raw, factor, live, grad, ones):
    width = raw.shape[1] // HEADS
    inner = nn((raw * grad).astype(BF), ones) * (1.0 / width)
    return grad * factor - raw * (factor * factor * factor * live * inner)


def fold(full, ones, members):
    kept = full * ones.astype(F32)
    total = kept[:members]
    for h in range(1, HEADS):
        total = total + kept[h * members : (h + 1) * members]
    return total


def cell_backward(grad_field, saved, gain, w_proj, w_out, ones, members):
    inputs, inv, q_raw, k_raw, q_fac, k_fac, q_live, k_live, queries, k_bd, v_bd, soft, rounded = saved
    rows, channels = inputs.shape
    cells = rows // members
    scale = 1.0 / math.sqrt(channels // HEADS)
    part = [slice(c * members, (c + 1) * members) for c in range(cells)]
    grad_mixed = nt(grad_field, w_out).astype(BF)
    dprob = jnp.concatenate([nt(grad_mixed[s], v) for s, v in zip(part, v_bd)], axis=0)
    delta = nn((soft * dprob).astype(BF), ones)
    dscore = (soft * (dprob - delta)).astype(BF)
    q_grad = jnp.concatenate([nn(dscore[s], k) for s, k in zip(part, k_bd)], axis=0) * scale
    k_grad = jnp.concatenate([fold(tn(dscore[s], queries[s]), ones, members) for s in part], axis=0) * scale
    v_grad = jnp.concatenate([fold(tn(rounded[s], grad_mixed[s]), ones, members) for s in part], axis=0)
    gq = head_pull(q_raw, q_fac, q_live, q_grad, ones).astype(BF)
    gk = head_pull(k_raw, k_fac, k_live, k_grad, ones).astype(BF)
    gv = v_grad.astype(BF)
    grad_normed = (
        nt(gq, w_proj[:, :channels])
        + nt(gk, w_proj[:, channels : 2 * channels])
        + nt(gv, w_proj[:, 2 * channels :])
    )
    lifted = grad_normed * gain
    inner = jnp.mean(lifted * inputs, axis=-1, keepdims=True)
    return lifted * inv - inputs * (inv * inv * inv * inner)


def iota(shape, dim):
    return lax.broadcasted_iota(jnp.int32, shape, dim)


def one_hot(shape, source):
    return jnp.where(iota(shape, 1) == source(iota(shape, 0)), 1.0, 0.0).astype(BF)


def pack(rows, peers):
    half = rows.shape[1] // 2
    per = rows.shape[0] // peers
    low = rows[:, :half].reshape(peers, per, half)
    high = rows[:, half:].reshape(peers, per, half)
    return jnp.concatenate([low, high], axis=1).astype(BF)


def unpack(chunks):
    peers, double, half = chunks.shape
    wide = chunks.astype(F32)
    low = wide[:, : double // 2].reshape(peers * double // 2, half)
    high = wide[:, double // 2 :].reshape(peers * double // 2, half)
    return jnp.concatenate([low, high], axis=1).astype(BF)


X, G, U, B = range(4)


def kernel(
    dims,
    ens_any,
    gain_any,
    w_proj_any,
    w_out_any,
    conv_any,
    cot_any,
    result_ref,
    grad_ref,
    ens_ref,
    cot_ref,
    gain_ref,
    w_proj_ref,
    w_out_ref,
    conv_ref,
    out_buf,
    in_buf,
    halo_cot,
    edge_cot,
    gf_ref,
    rim_out,
    rim_in,
    side_in,
    corner_in,
    column_ref,
    load_sem,
    ex_send,
    ex_recv,
    halo_send,
    halo_recv,
    rim_send,
    rim_recv,
    side_send,
    side_recv,
    corner_send,
    corner_recv,
    flag,
):
    mem, lat, lon, channels, peers, lats, lons = dims
    cells = mem * lat * lon
    members = mem * peers
    me = lax.axis_index("member")
    my_lat = lax.axis_index("lat")
    my_lon = lax.axis_index("lon")

    pairs = (
        (ens_any, ens_ref),
        (cot_any, cot_ref),
        (conv_any, conv_ref),
        (w_proj_any, w_proj_ref),
        (w_out_any, w_out_ref),
        (gain_any, gain_ref),
    )
    loads = [
        pltpu.make_async_copy(src, dst, load_sem.at[i]) for i, (src, dst) in enumerate(pairs)
    ]
    for load in loads:
        load.start()

    def partner(j):
        return {"member": lax.rem(me + j, peers)}

    def near(d_lat, d_lon):
        return {
            "lat": lax.rem(my_lat + d_lat + lats, lats),
            "lon": lax.rem(my_lon + d_lon + lons, lons),
        }

    around = [(a, b) for a in (-1, 0, 1) for b in (-1, 0, 1) if (a, b) != (0, 0)]
    barrier = pltpu.get_barrier_semaphore()
    far_first = sorted(range(1, peers), key=lambda j: -min(j, peers - j))
    ring = peers // 2
    my_z, my_y = me // 2, lax.rem(me, 2)

    def along(dz):
        return {"member": lax.rem(my_z + dz, ring) * 2 + my_y}

    twin = {"member": my_z * 2 + 1 - my_y}
    z_steps = sorted(range(1, ring), key=lambda j: -min(j, ring - j))
    close = [along(dz) for dz in z_steps] + [twin]
    for device in close:
        pl.semaphore_signal(barrier, inc=1, device_id=device, device_id_type=MESH)
    for d_lat, d_lon in around:
        pl.semaphore_signal(barrier, inc=1, device_id=near(d_lat, d_lon), device_id_type=MESH)

    def home_source(i):
        j, m, a = i // (mem * lat), (i // lat) % mem, i % lat
        return (m * lat + a) * lon + lax.rem(me + j, peers)

    def home_target(i):
        m, a, b = i // (lat * lon), (i // lon) % lat, i % lon
        return lax.rem(b - me + peers, peers) * (mem * lat) + m * lat + a

    def cell_source(i):
        c, j, m = i // members, (i // mem) % peers, i % mem
        return (j * mem + m) * lat + c

    def cell_target(i):
        j, m, c = i // (mem * lat), (i // lat) % mem, i % lat
        return (c * peers + j) * mem + m

    def edge_source(i):
        count = mem * lat
        return (i % count) * lon + (i // count) * (lon - 1)

    square = (cells, cells)
    home_out = one_hot(square, home_source)
    home_in = one_hot(square, home_target)
    cell_in = one_hot(square, cell_source)
    cell_out = one_hot(square, cell_target)
    edges = one_hot((2 * mem * lat, cells), edge_source)

    def exchange(kind, sign):
        return [
            pltpu.make_async_remote_copy(
                src_ref=out_buf.at[kind, j],
                dst_ref=in_buf.at[kind, j],
                send_sem=ex_send.at[kind],
                recv_sem=ex_recv.at[kind],
                device_id=partner(j if sign > 0 else peers - j),
                device_id_type=MESH,
            )
            for j in far_first
        ]

    def exchange_all(kind):
        return pltpu.make_async_remote_copy(
            src_ref=out_buf.at[kind, pl.ds(1, peers - 1)],
            dst_ref=in_buf.at[kind, pl.ds(1, peers - 1)],
            send_sem=ex_send.at[kind],
            recv_sem=ex_recv.at[kind],
            device_id=partner(1),
            device_id_type=MESH,
        )

    def send(kind, order, rows, sign):
        packed = pack(nn(order, rows), peers)
        out_buf[kind] = packed
        in_buf[kind, 0] = packed[0]
        for copy in exchange(kind, sign):
            copy.start()

    def receive(kind, order):
        exchange_all(kind).wait_recv()
        return nn(order, unpack(in_buf[kind]))

    has_low, has_high = my_lat > 0, my_lat < lats - 1

    def halo_group(d_lat):
        which = 1 - d_lat
        copies = [
            pltpu.make_async_remote_copy(
                src_ref=edge_cot,
                dst_ref=halo_cot.at[0 if d_lon > 0 else 1, lat + 2 + which],
                send_sem=halo_send.at[which],
                recv_sem=halo_recv.at[which],
                device_id=near(d_lat, d_lon),
                device_id_type=MESH,
            )
            for d_lon in (-1, 1)
        ]
        if d_lat:
            copies.append(
                pltpu.make_async_remote_copy(
                    src_ref=cot_ref.at[:, lat - 1 if d_lat > 0 else 0],
                    dst_ref=halo_cot.at[:, 0 if d_lat > 0 else lat + 1],
                    send_sem=halo_send.at[3 + (which > 1)],
                    recv_sem=halo_recv.at[3 + (which > 1)],
                    device_id=near(d_lat, 0),
                    device_id_type=MESH,
                )
            )
        return copies

    def halo_columns(which):
        columns = halo_cot.at[:, lat + 2 + which]
        return pltpu.make_async_remote_copy(
            src_ref=columns,
            dst_ref=columns,
            send_sem=halo_send.at[which],
            recv_sem=halo_recv.at[which],
            device_id=near(0, 1),
            device_id_type=MESH,
        )

    def start_halo():
        @pl.when(has_high)
        def _():
            for copy in halo_group(1):
                copy.start()

        @pl.when(has_low)
        def _():
            for copy in halo_group(-1):
                copy.start()

        for copy in halo_group(0):
            copy.start()

    def wait_halo():
        halo_columns(1).wait_recv()

        @pl.when(has_low)
        def _():
            halo_columns(0).wait_recv()
            halo_group(1)[2].wait_recv()

        @pl.when(has_high)
        def _():
            halo_columns(2).wait_recv()
            halo_group(-1)[2].wait_recv()

    def wait_halo_sent():
        halo_columns(1).wait_send()

        @pl.when(has_high)
        def _():
            halo_columns(0).wait_send()
            halo_group(1)[2].wait_send()

        @pl.when(has_low)
        def _():
            halo_columns(2).wait_send()
            halo_group(-1)[2].wait_send()

    every = [0] + far_first

    def shift_of(rim):
        return 1 if rim == 0 else lats - 1

    def home_of(j, d_lat, d_lon):
        return {
            "member": lax.rem(me + peers - j, peers),
            "lat": lax.rem(my_lat + d_lat, lats),
            "lon": lax.rem(my_lon + d_lon, lons),
        }

    def rim_copies(rim):
        return [
            pltpu.make_async_remote_copy(
                src_ref=rim_out.at[rim, j],
                dst_ref=rim_in.at[rim, j],
                send_sem=rim_send.at[rim],
                recv_sem=rim_recv.at[rim],
                device_id=home_of(j, shift_of(rim), 0),
                device_id_type=MESH,
            )
            for j in every
        ]

    def rim_all(rim):
        return pltpu.make_async_remote_copy(
            src_ref=rim_out.at[rim],
            dst_ref=rim_in.at[rim],
            send_sem=rim_send.at[rim],
            recv_sem=rim_recv.at[rim],
            device_id=home_of(0, shift_of(rim), 0),
            device_id_type=MESH,
        )

    def side_copies(side):
        return [
            pltpu.make_async_remote_copy(
                src_ref=out_buf.at[U, j],
                dst_ref=side_in.at[side],
                send_sem=side_send.at[side],
                recv_sem=side_recv.at[side],
                device_id=home_of(j, 0, 1 if side == 0 else lons - 1),
                device_id_type=MESH,
            )
            for j in every
        ]

    def side_all(side):
        return pltpu.make_async_remote_copy(
            src_ref=out_buf.at[U],
            dst_ref=out_buf.at[U],
            send_sem=side_send.at[side],
            recv_sem=side_recv.at[side],
            device_id=home_of(0, 0, 1),
            device_id_type=MESH,
        )

    def corner_copies(side, rim):
        return [
            pltpu.make_async_remote_copy(
                src_ref=rim_out.at[rim, j],
                dst_ref=corner_in.at[side, rim],
                send_sem=corner_send.at[side, rim],
                recv_sem=corner_recv.at[side, rim],
                device_id=home_of(j, shift_of(rim), 1 if side == 0 else lons - 1),
                device_id_type=MESH,
            )
            for j in every
        ]

    def corner_all(side, rim):
        return pltpu.make_async_remote_copy(
            src_ref=rim_out.at[rim],
            dst_ref=rim_in.at[rim],
            send_sem=corner_send.at[side, rim],
            recv_sem=corner_recv.at[side, rim],
            device_id=home_of(0, shift_of(rim), 1),
            device_id_type=MESH,
        )

    def sends_rim(rim):
        return has_high if rim == 0 else has_low

    def gets_rim(rim):
        return has_low if rim == 0 else has_high

    def sends_side(side):
        return me == (peers - 1 if side == 0 else 0)

    def start_rims():
        for side in range(2):

            @pl.when(sends_side(side))
            def _():
                for copy in side_copies(side):
                    copy.start()

        for rim in range(2):

            @pl.when(sends_rim(rim))
            def _():
                for copy in rim_copies(rim):
                    copy.start()

            for side in range(2):

                @pl.when(jnp.logical_and(sends_side(side), sends_rim(rim)))
                def _():
                    for copy in corner_copies(side, rim):
                        copy.start()

    def wait_rims():
        for side in range(2):
            side_copies(side)[0].wait_recv()
        for rim in range(2):

            @pl.when(gets_rim(rim))
            def _():
                rim_all(rim).wait_recv()
                for side in range(2):
                    corner_copies(side, rim)[0].wait_recv()

    def wait_rims_sent():
        for side in range(2):

            @pl.when(sends_side(side))
            def _():
                side_all(side).wait_send()

        for rim in range(2):

            @pl.when(sends_rim(rim))
            def _():
                rim_all(rim).wait_send()

            for side in range(2):

                @pl.when(jnp.logical_and(sends_side(side), sends_rim(rim)))
                def _():
                    corner_all(side, rim).wait_send()

    def rim_pack(rows):
        half = channels // 2
        shape = (2 * mem * peers, mem * peers)
        i, k = iota(shape, 0), iota(shape, 1)
        same = (i // (2 * mem)) * mem + i % mem == k
        upper = (i // mem) % 2 == 1
        low = jnp.where(jnp.logical_and(same, jnp.logical_not(upper)), 1.0, 0.0).astype(BF)
        high = jnp.where(jnp.logical_and(same, upper), 1.0, 0.0).astype(BF)
        return nn(low, rows[:, :half]) + nn(high, rows[:, half:])

    def rim_rows(rim, low, high):
        got = rim_in[rim].astype(F32).reshape(2 * mem * peers, channels // 2).astype(BF)
        return jnp.concatenate([nn(low, got), nn(high, got)], axis=1).astype(BF)

    def rim_selection():
        shape = (mem * lon, 2 * mem * peers)
        i, k = iota(shape, 0), iota(shape, 1)
        row = lax.rem(i % lon - me + peers, peers) * (2 * mem) + i // lon
        low = jnp.where(k == row, 1.0, 0.0).astype(BF)
        high = jnp.where(k == row + mem, 1.0, 0.0).astype(BF)
        return low, high

    def side_column(side):
        half = channels // 2
        per = mem * lat
        main = side_in[side].astype(F32)
        column_ref[side, 0:per, 0:half] = main[:per]
        column_ref[side, 0:per, half:channels] = main[per:]
        for rim in range(2):
            at = per + rim * mem
            corner = corner_in[side, rim].astype(F32)
            column_ref[side, at : at + mem, 0:half] = corner[:mem]
            column_ref[side, at : at + mem, half:channels] = corner[mem:]
        return column_ref[side].astype(BF)

    strip = lat + 2

    def cot_edge(m, shift, a):
        which = jnp.where(a == 0, 0, jnp.where(a == strip - 1, 2, 1))
        row = jnp.where(a == 0, lat - 1, jnp.where(a == strip - 1, 0, a - 1))
        return which * lon + (mem * lat if shift < 0 else 0) + m * lat + row

    def up_edge(m, shift, a):
        outer = mem * lat + m
        return jnp.where(a == 0, outer, jnp.where(a == strip - 1, outer + mem, m * lat + a - 1))

    def picks_of(edge_row, count):
        return {(m, shift): pick_of(count, edge_row, m, shift) for m in range(mem) for shift in (-1, 1)}

    def pick_of(count, edge_row, m, shift):
        shape = (strip * lon, strip * lon + count)
        a, b = iota(shape, 0) // lon, iota(shape, 0) % lon
        outer = strip * lon + edge_row(m, shift, a)
        source = jnp.where(b == (0 if shift < 0 else lon - 1), outer, a * lon + b + shift)
        open_row = jnp.logical_and(
            jnp.logical_or(a > 0, has_low), jnp.logical_or(a < strip - 1, has_high)
        )
        return jnp.where(jnp.logical_and(iota(shape, 1) == source, open_row), 1.0, 0.0).astype(BF)

    def shifted(field, columns, picks, m, shift):
        if shift == 0:
            return field
        return nn(picks[m, shift], jnp.concatenate([field, columns], axis=0)).astype(BF)

    def conv(fields, columns, picks, adjoint):
        total = None
        for c in range(3):
            shift = 1 - c if adjoint else c - 1
            side = 0 if shift < 0 else 1
            wide = [shifted(fields[m], columns[side], picks, m, shift) for m in range(mem)]
            for r in range(3):
                start = (2 - r if adjoint else r) * lon
                window = jnp.concatenate([w[start : start + lat * lon] for w in wide], axis=0)
                term = nt(window, conv_ref[r, c]) if adjoint else nn(window, conv_ref[r, c])
                total = term if total is None else total + term
        return total

    def closed(rows, there):
        return jnp.where(there, rows.astype(F32), 0.0).astype(BF)

    @pl.when(jnp.logical_not(has_low))
    def _():
        halo_cot[:, 0] = jnp.zeros((mem, lon, channels), BF)
        halo_cot[:, lat + 2] = jnp.zeros((mem, lon, channels), BF)
        rim_in[0] = jnp.zeros(rim_in.shape[1:], BF)
        corner_in[:, 0] = jnp.zeros((2,) + corner_in.shape[2:], BF)

    @pl.when(jnp.logical_not(has_high))
    def _():
        halo_cot[:, lat + 1] = jnp.zeros((mem, lon, channels), BF)
        halo_cot[:, lat + 4] = jnp.zeros((mem, lon, channels), BF)
        rim_in[1] = jnp.zeros(rim_in.shape[1:], BF)
        corner_in[:, 1] = jnp.zeros((2,) + corner_in.shape[2:], BF)

    column_ref[...] = jnp.zeros(column_ref.shape, F32)
    loads[0].wait()
    ens = ens_ref[...].reshape(cells, channels)
    loads[1].wait()
    cot = cot_ref[...].reshape(cells, channels)
    packed = pack(nn(home_out, ens), peers)
    out_buf[X] = packed
    in_buf[X, 0] = packed[0]
    edge_cot[...] = nn(edges, cot).astype(BF)
    pl.semaphore_wait(barrier, len(close) + len(around))
    pl.semaphore_signal(flag, inc=1, device_id=twin, device_id_type=MESH)
    start_halo()
    copies = dict(zip(far_first, exchange(X, 1)))
    for j in far_first:
        if j % 2 == 0:
            copies[j].start()
    pl.semaphore_wait(flag, 1)
    for j in far_first:
        if j % 2 == 1:
            copies[j].start()

    ones = head_blocks(channels, members).astype(BF)
    loads[2].wait()
    cot_picks = picks_of(cot_edge, 3 * lon)
    wait_halo()
    cot_fields = [
        jnp.concatenate(
            [
                closed(halo_cot[m, 0], has_low),
                cot_ref[m].reshape(lat * lon, channels),
                closed(halo_cot[m, lat + 1], has_high),
            ],
            axis=0,
        )
        for m in range(mem)
    ]
    cot_columns = [halo_cot[side, lat + 2 : lat + 5].reshape(3 * lon, channels) for side in range(2)]
    grad_field = cot.astype(F32) + conv(cot_fields, cot_columns, cot_picks, True)
    gf_ref[...] = grad_field
    send(G, home_out, grad_field.astype(BF), 1)

    for load in loads[3:]:
        load.wait()
    gain = gain_ref[...]
    w_proj = w_proj_ref[...]
    w_out = w_out_ref[...]
    x = receive(X, cell_in).astype(BF)
    updated, saved = cell_forward(x, gain, w_proj, w_out, ones, members)
    send(U, cell_out, updated, -1)
    for rim, c in enumerate((lat - 1, 0)):
        rows = updated[c * members : (c + 1) * members]
        rim_out[rim] = rim_pack(rows).reshape(rim_out.shape[1:]).astype(BF)
    start_rims()

    grads = receive(G, cell_in).astype(BF)
    grad_inputs = cell_backward(grads, saved, gain, w_proj, w_out, ones, members)
    send(B, cell_out, grad_inputs.astype(BF), -1)

    up_picks = picks_of(up_edge, column_ref.shape[1])
    rim_picks = rim_selection()
    field = receive(U, home_in)
    wait_rims()
    rows = field.astype(BF)
    low = closed(rim_rows(0, *rim_picks), has_low)
    high = closed(rim_rows(1, *rim_picks), has_high)
    up_fields = [
        jnp.concatenate(
            [
                low[m * lon : (m + 1) * lon],
                rows[m * lat * lon : (m + 1) * lat * lon],
                high[m * lon : (m + 1) * lon],
            ],
            axis=0,
        )
        for m in range(mem)
    ]
    result = field + conv(up_fields, [side_column(0), side_column(1)], up_picks, False)
    result_ref[...] = result.astype(BF).reshape(result_ref.shape)

    back = receive(B, home_in)
    grad_ref[...] = (gf_ref[...] + back).astype(BF).reshape(grad_ref.shape)

    for kind in (X, G, U, B):
        exchange_all(kind).wait_send()
    wait_halo_sent()
    wait_rims_sent()


def store_kernel(result_in, grad_in, result_out, grad_out, sem):
    copies = [
        pltpu.make_async_copy(result_in, result_out, sem.at[0]),
        pltpu.make_async_copy(grad_in, grad_out, sem.at[1]),
    ]
    for copy in copies:
        copy.start()
    for copy in copies:
        copy.wait()


MESH = pl.DeviceIdType.MESH
LIMIT = 16 * 1024 * 1024


def per_device(ensemble, norm_gain, project_weight, output_weight, conv_kernel, cotangent):
    mem, lat, lon, channels = ensemble.shape
    peers = lax.axis_size("member")
    dims = (mem, lat, lon, channels, peers, lax.axis_size("lat"), lax.axis_size("lon"))
    vmem = pl.BlockSpec(memory_space=pltpu.VMEM)
    anywhere = pl.BlockSpec(memory_space=pl.ANY)
    chunk = (4, peers, 2 * mem * lat, channels // 2)
    halo = (mem, lat + 5, lon, channels)
    field = jax.ShapeDtypeStruct(ensemble.shape, BF)
    outs = pl.pallas_call(
        functools.partial(kernel, dims),
        out_shape=(field, field),
        in_specs=[pl.BlockSpec(memory_space=pltpu.HBM)] * 6,
        out_specs=(vmem, vmem),
        scratch_shapes=[
            pltpu.VMEM(ensemble.shape, BF),
            pltpu.VMEM(ensemble.shape, BF),
            pltpu.VMEM((1, channels), F32),
            pltpu.VMEM(project_weight.shape, BF),
            pltpu.VMEM(output_weight.shape, BF),
            pltpu.VMEM(conv_kernel.shape, BF),
            pltpu.VMEM(chunk, BF),
            pltpu.VMEM(chunk, BF),
            pltpu.VMEM(halo, BF),
            pltpu.VMEM((2 * mem * lat, channels), BF),
            pltpu.VMEM((mem * lat * lon, channels), F32),
            pltpu.VMEM((2, peers, 2 * mem, channels // 2), BF),
            pltpu.VMEM((2, peers, 2 * mem, channels // 2), BF),
            pltpu.VMEM((2, 2 * mem * lat, channels // 2), BF),
            pltpu.VMEM((2, 2, 2 * mem, channels // 2), BF),
            pltpu.VMEM((2, 16, channels), F32),
            pltpu.SemaphoreType.DMA((6,)),
            pltpu.SemaphoreType.DMA((4,)),
            pltpu.SemaphoreType.DMA((4,)),
            pltpu.SemaphoreType.DMA((5,)),
            pltpu.SemaphoreType.DMA((5,)),
            pltpu.SemaphoreType.DMA((2,)),
            pltpu.SemaphoreType.DMA((2,)),
            pltpu.SemaphoreType.DMA((2,)),
            pltpu.SemaphoreType.DMA((2,)),
            pltpu.SemaphoreType.DMA((2, 2)),
            pltpu.SemaphoreType.DMA((2, 2)),
            pltpu.SemaphoreType.REGULAR,
        ],
        compiler_params=pltpu.CompilerParams(
            collective_id=0, has_side_effects=True, vmem_limit_bytes=LIMIT
        ),
    )(
        *(
            pltpu.with_memory_space_constraint(value, pltpu.HBM)
            for value in (
                ensemble,
                norm_gain.reshape(1, channels),
                project_weight,
                output_weight,
                conv_kernel,
                cotangent,
            )
        )
    )
    return pl.pallas_call(
        store_kernel,
        out_shape=(field, field),
        in_specs=[vmem, vmem],
        out_specs=(anywhere, anywhere),
        scratch_shapes=[pltpu.SemaphoreType.DMA((2,))],
        compiler_params=pltpu.CompilerParams(vmem_limit_bytes=LIMIT),
    )(*outs)


def solution(mesh):
    field = P("member", "lat", "lon", None)
    return jax.shard_map(
        per_device,
        mesh=mesh,
        in_specs=(field, P(), P(), P(), P(), field),
        out_specs=(field, field),
        check_vma=False,
    )
```

```python
import functools
import math

import jax
import jax.numpy as jnp
from jax import lax
from jax.experimental import pallas as pl
from jax.experimental.pallas import tpu as pltpu
from jax.sharding import PartitionSpec as P

HEADS = 8
FLOOR = 0.5
EPSILON = 1e-06
BF = jnp.bfloat16
F32 = jnp.float32


def mm(a, b, dims):
    return lax.dot_general(a, b, (dims, ((), ())), preferred_element_type=F32)


def nn(a, b):
    return mm(a, b, ((1,), (0,)))


def nt(a, b):
    return mm(a, b, ((1,), (1,)))


def tn(a, b):
    return mm(a, b, ((0,), (0,)))


def head_blocks(channels, members):
    width = channels // HEADS
    row = lax.broadcasted_iota(jnp.int32, (HEADS * members, channels), 0) // members
    col = lax.broadcasted_iota(jnp.int32, (HEADS * members, channels), 1) // width
    return row == col


def spread(rows, blocks):
    return jnp.concatenate([rows] * HEADS, axis=0) * blocks


def head_scale(raw, ones):
    width = raw.shape[1] // HEADS
    mean_sq = nn((raw * raw).astype(BF), ones) * (1.0 / width)
    factor = lax.rsqrt(jnp.maximum(mean_sq, FLOOR))
    live = jnp.where(mean_sq > FLOOR, 1.0, jnp.where(mean_sq == FLOOR, 0.5, 0.0))
    return factor, live


def cell_forward(x, gain, w_proj, w_out, ones, members):
    rows, channels = x.shape
    cells = rows // members
    scale = 1.0 / math.sqrt(channels // HEADS)
    inputs = x.astype(F32)
    inv = lax.rsqrt(jnp.mean(inputs * inputs, axis=-1, keepdims=True) + EPSILON)
    normed = (inputs * inv * gain).astype(BF)
    proj = nn(normed, w_proj).astype(BF)
    q_raw = proj[:, :channels].astype(F32)
    k_raw = proj[:, channels : 2 * channels].astype(F32)
    values = proj[:, 2 * channels :]
    q_fac, q_live = head_scale(q_raw, ones)
    k_fac, k_live = head_scale(k_raw, ones)
    queries = (q_raw * q_fac).astype(BF)
    keys = (k_raw * k_fac).astype(BF)
    part = [slice(c * members, (c + 1) * members) for c in range(cells)]
    k_bd = [spread(keys[s], ones) for s in part]
    v_bd = [spread(values[s], ones) for s in part]
    scores = jnp.concatenate([nt(queries[s], k) for s, k in zip(part, k_bd)], axis=0)
    expd = jnp.exp(scores * scale)
    narrow = expd.astype(BF)
    inv_total = 1.0 / nn(narrow, ones)
    mixed = jnp.concatenate([nn(narrow[s], v) for s, v in zip(part, v_bd)], axis=0)
    updated = (inputs + nn((mixed * inv_total).astype(BF), w_out)).astype(BF)
    soft = expd * inv_total
    rounded = soft.astype(BF)
    saved = (inputs, inv, q_raw, k_raw, q_fac, k_fac, q_live, k_live, queries, k_bd, v_bd, soft, rounded)
    return updated, saved


def head_pull(raw, factor, live, grad, ones):
    width = raw.shape[1] // HEADS
    inner = nn((raw * grad).astype(BF), ones) * (1.0 / width)
    return grad * factor - raw * (factor * factor * factor * live * inner)


def fold(full, ones, members):
    kept = full * ones.astype(F32)
    total = kept[:members]
    for h in range(1, HEADS):
        total = total + kept[h * members : (h + 1) * members]
    return total


def cell_backward(grad_field, saved, gain, w_proj, w_out, ones, members):
    inputs, inv, q_raw, k_raw, q_fac, k_fac, q_live, k_live, queries, k_bd, v_bd, soft, rounded = saved
    rows, channels = inputs.shape
    cells = rows // members
    scale = 1.0 / math.sqrt(channels // HEADS)
    part = [slice(c * members, (c + 1) * members) for c in range(cells)]
    grad_mixed = nt(grad_field, w_out).astype(BF)
    dprob = jnp.concatenate([nt(grad_mixed[s], v) for s, v in zip(part, v_bd)], axis=0)
    delta = nn((soft * dprob).astype(BF), ones)
    dscore = (soft * (dprob - delta)).astype(BF)
    q_grad = jnp.concatenate([nn(dscore[s], k) for s, k in zip(part, k_bd)], axis=0) * scale
    k_grad = jnp.concatenate([fold(tn(dscore[s], queries[s]), ones, members) for s in part], axis=0) * scale
    v_grad = jnp.concatenate([fold(tn(rounded[s], grad_mixed[s]), ones, members) for s in part], axis=0)
    gq = head_pull(q_raw, q_fac, q_live, q_grad, ones).astype(BF)
    gk = head_pull(k_raw, k_fac, k_live, k_grad, ones).astype(BF)
    gv = v_grad.astype(BF)
    grad_normed = (
        nt(gq, w_proj[:, :channels])
        + nt(gk, w_proj[:, channels : 2 * channels])
        + nt(gv, w_proj[:, 2 * channels :])
    )
    lifted = grad_normed * gain
    inner = jnp.mean(lifted * inputs, axis=-1, keepdims=True)
    return lifted * inv - inputs * (inv * inv * inv * inner)


def iota(shape, dim):
    return lax.broadcasted_iota(jnp.int32, shape, dim)


def one_hot(shape, source):
    return jnp.where(iota(shape, 1) == source(iota(shape, 0)), 1.0, 0.0).astype(BF)


def pack(rows, peers):
    half = rows.shape[1] // 2
    per = rows.shape[0] // peers
    low = rows[:, :half].reshape(peers, per, half)
    high = rows[:, half:].reshape(peers, per, half)
    return jnp.concatenate([low, high], axis=1).astype(BF)


def unpack(chunks):
    peers, double, half = chunks.shape
    wide = chunks.astype(F32)
    low = wide[:, : double // 2].reshape(peers * double // 2, half)
    high = wide[:, double // 2 :].reshape(peers * double // 2, half)
    return jnp.concatenate([low, high], axis=1).astype(BF)


X, G, U, B = range(4)


def kernel(
    dims,
    ens_any,
    gain_any,
    w_proj_any,
    w_out_any,
    conv_any,
    cot_any,
    result_ref,
    grad_ref,
    ens_ref,
    cot_ref,
    gain_ref,
    w_proj_ref,
    w_out_ref,
    conv_ref,
    out_buf,
    in_buf,
    halo_cot,
    edge_cot,
    gf_ref,
    side_out,
    rim_in,
    side_in,
    corner_in,
    column_ref,
    load_sem,
    ex_send,
    ex_recv,
    halo_send,
    halo_recv,
    rim_send,
    rim_recv,
    side_send,
    side_recv,
    corner_send,
    corner_recv,
    flag,
):
    mem, lat, lon, channels, peers, lats, lons = dims
    cells = mem * lat * lon
    members = mem * peers
    me = lax.axis_index("member")
    my_lat = lax.axis_index("lat")
    my_lon = lax.axis_index("lon")

    pairs = (
        (ens_any, ens_ref),
        (cot_any, cot_ref),
        (conv_any, conv_ref),
        (w_proj_any, w_proj_ref),
        (w_out_any, w_out_ref),
        (gain_any, gain_ref),
    )
    loads = [
        pltpu.make_async_copy(src, dst, load_sem.at[i]) for i, (src, dst) in enumerate(pairs)
    ]
    for load in loads:
        load.start()

    def partner(j):
        return {"member": lax.rem(me + j, peers)}

    def near(d_lat, d_lon):
        return {
            "lat": lax.rem(my_lat + d_lat + lats, lats),
            "lon": lax.rem(my_lon + d_lon + lons, lons),
        }

    around = [(a, b) for a in (-1, 0, 1) for b in (-1, 0, 1) if (a, b) != (0, 0)]
    barrier = pltpu.get_barrier_semaphore()
    far_first = sorted(range(1, peers), key=lambda j: -(min(j, peers - j) // 2 + 2 * (j % 2)))
    ring = peers // 2
    my_z, my_y = me // 2, lax.rem(me, 2)

    def along(dz):
        return {"member": lax.rem(my_z + dz, ring) * 2 + my_y}

    twin = {"member": my_z * 2 + 1 - my_y}
    z_steps = sorted(range(1, ring), key=lambda j: -min(j, ring - j))
    close = [along(dz) for dz in z_steps] + [twin]
    for device in close:
        pl.semaphore_signal(barrier, inc=1, device_id=device, device_id_type=MESH)
    for d_lat, d_lon in around:
        pl.semaphore_signal(barrier, inc=1, device_id=near(d_lat, d_lon), device_id_type=MESH)

    blocks = peers // lat
    width = lon // blocks
    my_row, my_block = me // blocks, lax.rem(me, blocks)

    def home_source(i):
        j, m, c = i // (mem * width), (i // width) % mem, i % width
        q = lax.rem(me + j, peers)
        return (m * lat + q // blocks) * lon + lax.rem(q, blocks) * width + c

    def home_target(i):
        m, a, b = i // (lat * lon), (i // lon) % lat, i % lon
        j = lax.rem(a * blocks + b // width - me + peers, peers)
        return (j * mem + m) * width + b % width

    def cell_source(i):
        c, j, m = i // members, (i // mem) % peers, i % mem
        return (j * mem + m) * width + c

    def cell_target(i):
        j, m, c = i // (mem * width), (i // width) % mem, i % width
        return (c * peers + j) * mem + m

    def edge_source(i):
        count = mem * lat
        return (i % count) * lon + (i // count) * (lon - 1)

    square = (cells, cells)
    home_out = one_hot(square, home_source)
    home_in = one_hot(square, home_target)
    cell_in = one_hot(square, cell_source)
    cell_out = one_hot(square, cell_target)
    edges = one_hot((2 * mem * lat, cells), edge_source)

    def exchange(kind, sign, group):
        return [
            pltpu.make_async_remote_copy(
                src_ref=out_buf.at[kind, j],
                dst_ref=in_buf.at[kind, j],
                send_sem=ex_send.at[kind],
                recv_sem=ex_recv.at[kind],
                device_id=partner(j if sign > 0 else peers - j),
                device_id_type=MESH,
            )
            for j in group
        ]

    def exchange_all(kind):
        return pltpu.make_async_remote_copy(
            src_ref=out_buf.at[kind, pl.ds(1, peers - 1)],
            dst_ref=in_buf.at[kind, pl.ds(1, peers - 1)],
            send_sem=ex_send.at[kind],
            recv_sem=ex_recv.at[kind],
            device_id=partner(1),
            device_id_type=MESH,
        )

    def send(kind, order, rows, sign):
        packed = pack(nn(order, rows), peers)
        out_buf[kind] = packed
        in_buf[kind, 0] = packed[0]
        for copy in exchange(kind, sign, far_first):
            copy.start()

    def receive(kind, order):
        exchange_all(kind).wait_recv()
        return nn(order, unpack(in_buf[kind]))

    has_low, has_high = my_lat > 0, my_lat < lats - 1

    def halo_group(d_lat):
        which = 1 - d_lat
        copies = [
            pltpu.make_async_remote_copy(
                src_ref=edge_cot,
                dst_ref=halo_cot.at[0 if d_lon > 0 else 1, lat + 2 + which],
                send_sem=halo_send.at[which],
                recv_sem=halo_recv.at[which],
                device_id=near(d_lat, d_lon),
                device_id_type=MESH,
            )
            for d_lon in (-1, 1)
        ]
        if d_lat:
            copies.append(
                pltpu.make_async_remote_copy(
                    src_ref=cot_ref.at[:, lat - 1 if d_lat > 0 else 0],
                    dst_ref=halo_cot.at[:, 0 if d_lat > 0 else lat + 1],
                    send_sem=halo_send.at[3 + (which > 1)],
                    recv_sem=halo_recv.at[3 + (which > 1)],
                    device_id=near(d_lat, 0),
                    device_id_type=MESH,
                )
            )
        return copies

    def halo_columns(which):
        columns = halo_cot.at[:, lat + 2 + which]
        return pltpu.make_async_remote_copy(
            src_ref=columns,
            dst_ref=columns,
            send_sem=halo_send.at[which],
            recv_sem=halo_recv.at[which],
            device_id=near(0, 1),
            device_id_type=MESH,
        )

    def start_halo():
        @pl.when(has_high)
        def _():
            for copy in halo_group(1):
                copy.start()

        @pl.when(has_low)
        def _():
            for copy in halo_group(-1):
                copy.start()

        for copy in halo_group(0):
            copy.start()

    def wait_halo():
        halo_columns(1).wait_recv()

        @pl.when(has_low)
        def _():
            halo_columns(0).wait_recv()
            halo_group(1)[2].wait_recv()

        @pl.when(has_high)
        def _():
            halo_columns(2).wait_recv()
            halo_group(-1)[2].wait_recv()

    def wait_halo_sent():
        halo_columns(1).wait_send()

        @pl.when(has_high)
        def _():
            halo_columns(0).wait_send()
            halo_group(1)[2].wait_send()

        @pl.when(has_low)
        def _():
            halo_columns(2).wait_send()
            halo_group(-1)[2].wait_send()

    far, close_by = far_first[: peers // 2], far_first[peers // 2 :] + [0]

    def home_of(j, rim, side):
        return {
            "member": lax.rem(me + peers - j, peers),
            "lat": lax.rem(my_lat + (0 if rim is None else 1 if rim == 0 else lats - 1), lats),
            "lon": lax.rem(my_lon + (0 if side is None else 1 if side == 0 else lons - 1), lons),
        }

    def rim_copies(rim, group):
        return [
            pltpu.make_async_remote_copy(
                src_ref=out_buf.at[U, j],
                dst_ref=rim_in.at[rim, my_block],
                send_sem=rim_send.at[rim],
                recv_sem=rim_recv.at[rim],
                device_id=home_of(j, rim, None),
                device_id_type=MESH,
            )
            for j in group
        ]

    def side_copies(side, group):
        return [
            pltpu.make_async_remote_copy(
                src_ref=side_out.at[side, j],
                dst_ref=side_in.at[side, my_row],
                send_sem=side_send.at[side],
                recv_sem=side_recv.at[side],
                device_id=home_of(j, None, side),
                device_id_type=MESH,
            )
            for j in group
        ]

    def corner_copies(side, rim, group):
        return [
            pltpu.make_async_remote_copy(
                src_ref=side_out.at[side, j],
                dst_ref=corner_in.at[side, rim],
                send_sem=corner_send.at[side, rim],
                recv_sem=corner_recv.at[side, rim],
                device_id=home_of(j, rim, side),
                device_id_type=MESH,
            )
            for j in group
        ]

    def bytes_of(ref, send_sem, recv_sem):
        return pltpu.make_async_remote_copy(
            src_ref=ref,
            dst_ref=ref,
            send_sem=send_sem,
            recv_sem=recv_sem,
            device_id=partner(1),
            device_id_type=MESH,
        )

    def gets_rim(rim):
        return has_low if rim == 0 else has_high

    def sends_rim(rim):
        if rim == 0:
            return jnp.logical_and(has_high, my_row == lat - 1)
        return jnp.logical_and(has_low, my_row == 0)

    def sends_side(side):
        return my_block == (blocks - 1 if side == 0 else 0)

    def start_rims(group):
        for rim in range(2):

            @pl.when(sends_rim(rim))
            def _():
                for copy in rim_copies(rim, group):
                    copy.start()

        for side in range(2):

            @pl.when(sends_side(side))
            def _():
                for copy in side_copies(side, group):
                    copy.start()

                for rim in range(2):

                    @pl.when(sends_rim(rim))
                    def _():
                        for copy in corner_copies(side, rim, group):
                            copy.start()

    def wait_rims():
        for side in range(2):
            bytes_of(side_in.at[side], side_send.at[side], side_recv.at[side]).wait_recv()
        for rim in range(2):

            @pl.when(gets_rim(rim))
            def _():
                bytes_of(rim_in.at[rim], rim_send.at[rim], rim_recv.at[rim]).wait_recv()
                for side in range(2):
                    bytes_of(
                        corner_in.at[side, rim], corner_send.at[side, rim], corner_recv.at[side, rim]
                    ).wait_recv()

    def wait_rims_sent():
        for rim in range(2):

            @pl.when(sends_rim(rim))
            def _():
                bytes_of(out_buf.at[U], rim_send.at[rim], rim_recv.at[rim]).wait_send()

        for side in range(2):

            @pl.when(sends_side(side))
            def _():
                bytes_of(side_out.at[side], side_send.at[side], side_recv.at[side]).wait_send()
                for rim in range(2):

                    @pl.when(sends_rim(rim))
                    def _():
                        bytes_of(
                            side_out.at[side], corner_send.at[side, rim], corner_recv.at[side, rim]
                        ).wait_send()

    def side_pack(rows):
        half = channels // 2
        shape = (2 * mem * peers, mem * peers)
        i, k = iota(shape, 0), iota(shape, 1)
        same = (i // (2 * mem)) * mem + i % mem == k
        upper = (i // mem) % 2 == 1
        low = jnp.where(jnp.logical_and(same, jnp.logical_not(upper)), 1.0, 0.0).astype(BF)
        high = jnp.where(jnp.logical_and(same, upper), 1.0, 0.0).astype(BF)
        return nn(low, rows[:, :half]) + nn(high, rows[:, half:])

    def rim_source(i):
        m, b = i // lon, i % lon
        return ((b // width) * mem + m) * width + b % width

    def rim_rows(rim, pick):
        return nn(pick, unpack(rim_in[rim])).astype(BF)

    def side_column(side):
        half = channels // 2
        parts = [side_in.at[side, a] for a in range(lat)] + [corner_in.at[side, rim] for rim in range(2)]
        for n, part in enumerate(parts):
            rows = part[...].astype(F32)
            column_ref[side, n * mem : (n + 1) * mem, 0:half] = rows[:mem]
            column_ref[side, n * mem : (n + 1) * mem, half:channels] = rows[mem:]
        return column_ref[side].astype(BF)

    strip = lat + 2

    def cot_edge(m, shift, a):
        which = jnp.where(a == 0, 0, jnp.where(a == strip - 1, 2, 1))
        row = jnp.where(a == 0, lat - 1, jnp.where(a == strip - 1, 0, a - 1))
        return which * lon + (mem * lat if shift < 0 else 0) + m * lat + row

    def up_edge(m, shift, a):
        outer = jnp.where(a == 0, lat, jnp.where(a == strip - 1, lat + 1, a - 1))
        return outer * mem + m

    def picks_of(edge_row, count):
        return {(m, shift): pick_of(count, edge_row, m, shift) for m in range(mem) for shift in (-1, 1)}

    def pick_of(count, edge_row, m, shift):
        shape = (strip * lon, strip * lon + count)
        a, b = iota(shape, 0) // lon, iota(shape, 0) % lon
        outer = strip * lon + edge_row(m, shift, a)
        source = jnp.where(b == (0 if shift < 0 else lon - 1), outer, a * lon + b + shift)
        open_row = jnp.logical_and(
            jnp.logical_or(a > 0, has_low), jnp.logical_or(a < strip - 1, has_high)
        )
        return jnp.where(jnp.logical_and(iota(shape, 1) == source, open_row), 1.0, 0.0).astype(BF)

    def shifted(field, columns, picks, m, shift):
        if shift == 0:
            return field
        return nn(picks[m, shift], jnp.concatenate([field, columns], axis=0)).astype(BF)

    def conv(fields, columns, picks, adjoint):
        total = None
        for c in range(3):
            shift = 1 - c if adjoint else c - 1
            side = 0 if shift < 0 else 1
            wide = [shifted(fields[m], columns[side], picks, m, shift) for m in range(mem)]
            for r in range(3):
                start = (2 - r if adjoint else r) * lon
                window = jnp.concatenate([w[start : start + lat * lon] for w in wide], axis=0)
                term = nt(window, conv_ref[r, c]) if adjoint else nn(window, conv_ref[r, c])
                total = term if total is None else total + term
        return total

    def closed(rows, there):
        return jnp.where(there, rows.astype(F32), 0.0).astype(BF)

    @pl.when(jnp.logical_not(has_low))
    def _():
        halo_cot[:, 0] = jnp.zeros((mem, lon, channels), BF)
        halo_cot[:, lat + 2] = jnp.zeros((mem, lon, channels), BF)
        rim_in[0] = jnp.zeros(rim_in.shape[1:], BF)
        corner_in[:, 0] = jnp.zeros((2,) + corner_in.shape[2:], BF)

    @pl.when(jnp.logical_not(has_high))
    def _():
        halo_cot[:, lat + 1] = jnp.zeros((mem, lon, channels), BF)
        halo_cot[:, lat + 4] = jnp.zeros((mem, lon, channels), BF)
        rim_in[1] = jnp.zeros(rim_in.shape[1:], BF)
        corner_in[:, 1] = jnp.zeros((2,) + corner_in.shape[2:], BF)

    column_ref[...] = jnp.zeros(column_ref.shape, F32)
    loads[0].wait()
    ens = ens_ref[...].reshape(cells, channels)
    loads[1].wait()
    cot = cot_ref[...].reshape(cells, channels)
    packed = pack(nn(home_out, ens), peers)
    out_buf[X] = packed
    in_buf[X, 0] = packed[0]
    edge_cot[...] = nn(edges, cot).astype(BF)
    pl.semaphore_wait(barrier, len(close) + len(around))
    pl.semaphore_signal(flag, inc=1, device_id=twin, device_id_type=MESH)
    start_halo()
    copies = dict(zip(far_first, exchange(X, 1, far_first)))
    for j in far_first:
        if j % 2 == 0:
            copies[j].start()
    pl.semaphore_wait(flag, 1)
    for j in far_first:
        if j % 2 == 1:
            copies[j].start()

    ones = head_blocks(channels, members).astype(BF)
    loads[2].wait()
    cot_picks = picks_of(cot_edge, 3 * lon)
    wait_halo()
    cot_fields = [
        jnp.concatenate(
            [
                closed(halo_cot[m, 0], has_low),
                cot_ref[m].reshape(lat * lon, channels),
                closed(halo_cot[m, lat + 1], has_high),
            ],
            axis=0,
        )
        for m in range(mem)
    ]
    cot_columns = [halo_cot[side, lat + 2 : lat + 5].reshape(3 * lon, channels) for side in range(2)]
    grad_field = cot.astype(F32) + conv(cot_fields, cot_columns, cot_picks, True)
    gf_ref[...] = grad_field
    send(G, home_out, grad_field.astype(BF), 1)

    for load in loads[3:]:
        load.wait()
    gain = gain_ref[...]
    w_proj = w_proj_ref[...]
    w_out = w_out_ref[...]
    x = receive(X, cell_in).astype(BF)
    updated, saved = cell_forward(x, gain, w_proj, w_out, ones, members)
    packed = pack(nn(cell_out, updated), peers)
    out_buf[U] = packed
    in_buf[U, 0] = packed[0]
    for side, c in enumerate((width - 1, 0)):
        rows = updated[c * members : (c + 1) * members]
        side_out[side] = side_pack(rows).reshape(side_out.shape[1:]).astype(BF)
    for group in (far, close_by):
        for copy in exchange(U, -1, [j for j in group if j]):
            copy.start()
        start_rims(group)

    grads = receive(G, cell_in).astype(BF)
    grad_inputs = cell_backward(grads, saved, gain, w_proj, w_out, ones, members)
    send(B, cell_out, grad_inputs.astype(BF), -1)

    up_picks = picks_of(up_edge, column_ref.shape[1])
    rim_pick = one_hot((mem * lon, mem * lon), rim_source)
    field = receive(U, home_in)
    wait_rims()
    rows = field.astype(BF)
    low = closed(rim_rows(0, rim_pick), has_low)
    high = closed(rim_rows(1, rim_pick), has_high)
    up_fields = [
        jnp.concatenate(
            [
                low[m * lon : (m + 1) * lon],
                rows[m * lat * lon : (m + 1) * lat * lon],
                high[m * lon : (m + 1) * lon],
            ],
            axis=0,
        )
        for m in range(mem)
    ]
    result = field + conv(up_fields, [side_column(0), side_column(1)], up_picks, False)
    result_ref[...] = result.astype(BF).reshape(result_ref.shape)

    back = receive(B, home_in)
    grad_ref[...] = (gf_ref[...] + back).astype(BF).reshape(grad_ref.shape)

    for kind in (X, G, U, B):
        exchange_all(kind).wait_send()
    wait_halo_sent()
    wait_rims_sent()


def store_kernel(result_in, grad_in, result_out, grad_out, sem):
    copies = [
        pltpu.make_async_copy(result_in, result_out, sem.at[0]),
        pltpu.make_async_copy(grad_in, grad_out, sem.at[1]),
    ]
    for copy in copies:
        copy.start()
    for copy in copies:
        copy.wait()


MESH = pl.DeviceIdType.MESH
LIMIT = 16 * 1024 * 1024


def per_device(ensemble, norm_gain, project_weight, output_weight, conv_kernel, cotangent):
    mem, lat, lon, channels = ensemble.shape
    peers = lax.axis_size("member")
    dims = (mem, lat, lon, channels, peers, lax.axis_size("lat"), lax.axis_size("lon"))
    vmem = pl.BlockSpec(memory_space=pltpu.VMEM)
    anywhere = pl.BlockSpec(memory_space=pl.ANY)
    chunk = (4, peers, 2 * mem * lat, channels // 2)
    halo = (mem, lat + 5, lon, channels)
    field = jax.ShapeDtypeStruct(ensemble.shape, BF)
    outs = pl.pallas_call(
        functools.partial(kernel, dims),
        out_shape=(field, field),
        in_specs=[pl.BlockSpec(memory_space=pltpu.HBM)] * 6,
        out_specs=(vmem, vmem),
        scratch_shapes=[
            pltpu.VMEM(ensemble.shape, BF),
            pltpu.VMEM(ensemble.shape, BF),
            pltpu.VMEM((1, channels), F32),
            pltpu.VMEM(project_weight.shape, BF),
            pltpu.VMEM(output_weight.shape, BF),
            pltpu.VMEM(conv_kernel.shape, BF),
            pltpu.VMEM(chunk, BF),
            pltpu.VMEM(chunk, BF),
            pltpu.VMEM(halo, BF),
            pltpu.VMEM((2 * mem * lat, channels), BF),
            pltpu.VMEM((mem * lat * lon, channels), F32),
            pltpu.VMEM((2, peers, 2 * mem, channels // 2), BF),
            pltpu.VMEM((2, peers // lat) + chunk[2:], BF),
            pltpu.VMEM((2, lat, 2 * mem, channels // 2), BF),
            pltpu.VMEM((2, 2, 2 * mem, channels // 2), BF),
            pltpu.VMEM((2, 16, channels), F32),
            pltpu.SemaphoreType.DMA((6,)),
            pltpu.SemaphoreType.DMA((4,)),
            pltpu.SemaphoreType.DMA((4,)),
            pltpu.SemaphoreType.DMA((5,)),
            pltpu.SemaphoreType.DMA((5,)),
            pltpu.SemaphoreType.DMA((2,)),
            pltpu.SemaphoreType.DMA((2,)),
            pltpu.SemaphoreType.DMA((2,)),
            pltpu.SemaphoreType.DMA((2,)),
            pltpu.SemaphoreType.DMA((2, 2)),
            pltpu.SemaphoreType.DMA((2, 2)),
            pltpu.SemaphoreType.REGULAR,
        ],
        compiler_params=pltpu.CompilerParams(
            collective_id=0, has_side_effects=True, vmem_limit_bytes=LIMIT
        ),
    )(
        *(
            pltpu.with_memory_space_constraint(value, pltpu.HBM)
            for value in (
                ensemble,
                norm_gain.reshape(1, channels),
                project_weight,
                output_weight,
                conv_kernel,
                cotangent,
            )
        )
    )
    return pl.pallas_call(
        store_kernel,
        out_shape=(field, field),
        in_specs=[vmem, vmem],
        out_specs=(anywhere, anywhere),
        scratch_shapes=[pltpu.SemaphoreType.DMA((2,))],
        compiler_params=pltpu.CompilerParams(vmem_limit_bytes=LIMIT),
    )(*outs)


def solution(mesh):
    field = P("member", "lat", "lon", None)
    return jax.shard_map(
        per_device,
        mesh=mesh,
        in_specs=(field, P(), P(), P(), P(), field),
        out_specs=(field, field),
        check_vma=False,
    )
```

```python
import functools
import math

import jax
import jax.numpy as jnp
from jax import lax
from jax.experimental import pallas as pl
from jax.experimental.pallas import tpu as pltpu
from jax.sharding import PartitionSpec as P

HEADS = 8
FLOOR = 0.5
EPSILON = 1e-06
BF = jnp.bfloat16
F32 = jnp.float32


def mm(a, b, dims):
    return lax.dot_general(a, b, (dims, ((), ())), preferred_element_type=F32)


def nn(a, b):
    return mm(a, b, ((1,), (0,)))


def nt(a, b):
    return mm(a, b, ((1,), (1,)))


def tn(a, b):
    return mm(a, b, ((0,), (0,)))


def head_blocks(channels, members):
    width = channels // HEADS
    row = lax.broadcasted_iota(jnp.int32, (HEADS * members, channels), 0) // members
    col = lax.broadcasted_iota(jnp.int32, (HEADS * members, channels), 1) // width
    return row == col


def spread(rows, blocks):
    return jnp.concatenate([rows] * HEADS, axis=0) * blocks


def head_scale(raw, ones):
    width = raw.shape[1] // HEADS
    mean_sq = nn((raw * raw).astype(BF), ones) * (1.0 / width)
    factor = lax.rsqrt(jnp.maximum(mean_sq, FLOOR))
    live = jnp.where(mean_sq > FLOOR, 1.0, jnp.where(mean_sq == FLOOR, 0.5, 0.0))
    return factor, live


def cell_forward(x, gain, w_proj, w_out, ones, members):
    rows, channels = x.shape
    cells = rows // members
    scale = 1.0 / math.sqrt(channels // HEADS)
    inputs = x.astype(F32)
    inv = lax.rsqrt(jnp.mean(inputs * inputs, axis=-1, keepdims=True) + EPSILON)
    normed = (inputs * inv * gain).astype(BF)
    proj = nn(normed, w_proj).astype(BF)
    q_raw = proj[:, :channels].astype(F32)
    k_raw = proj[:, channels : 2 * channels].astype(F32)
    values = proj[:, 2 * channels :]
    q_fac, q_live = head_scale(q_raw, ones)
    k_fac, k_live = head_scale(k_raw, ones)
    queries = (q_raw * q_fac).astype(BF)
    keys = (k_raw * k_fac).astype(BF)
    part = [slice(c * members, (c + 1) * members) for c in range(cells)]
    k_bd = [spread(keys[s], ones) for s in part]
    v_bd = [spread(values[s], ones) for s in part]
    scores = jnp.concatenate([nt(queries[s], k) for s, k in zip(part, k_bd)], axis=0)
    expd = jnp.exp(scores * scale)
    narrow = expd.astype(BF)
    inv_total = 1.0 / nn(narrow, ones)
    mixed = jnp.concatenate([nn(narrow[s], v) for s, v in zip(part, v_bd)], axis=0)
    updated = (inputs + nn((mixed * inv_total).astype(BF), w_out)).astype(BF)
    soft = expd * inv_total
    rounded = soft.astype(BF)
    saved = (inputs, inv, q_raw, k_raw, q_fac, k_fac, q_live, k_live, queries, k_bd, v_bd, soft, rounded)
    return updated, saved


def head_pull(raw, factor, live, grad, ones):
    width = raw.shape[1] // HEADS
    inner = nn((raw * grad).astype(BF), ones) * (1.0 / width)
    return grad * factor - raw * (factor * factor * factor * live * inner)


def fold(full, ones, members):
    kept = full * ones.astype(F32)
    total = kept[:members]
    for h in range(1, HEADS):
        total = total + kept[h * members : (h + 1) * members]
    return total


def cell_backward(grad_field, saved, gain, w_proj, w_out, ones, members):
    inputs, inv, q_raw, k_raw, q_fac, k_fac, q_live, k_live, queries, k_bd, v_bd, soft, rounded = saved
    rows, channels = inputs.shape
    cells = rows // members
    scale = 1.0 / math.sqrt(channels // HEADS)
    part = [slice(c * members, (c + 1) * members) for c in range(cells)]
    grad_mixed = nt(grad_field, w_out).astype(BF)
    dprob = jnp.concatenate([nt(grad_mixed[s], v) for s, v in zip(part, v_bd)], axis=0)
    delta = nn((soft * dprob).astype(BF), ones)
    dscore = (soft * (dprob - delta)).astype(BF)
    q_grad = jnp.concatenate([nn(dscore[s], k) for s, k in zip(part, k_bd)], axis=0) * scale
    k_grad = jnp.concatenate([fold(tn(dscore[s], queries[s]), ones, members) for s in part], axis=0) * scale
    v_grad = jnp.concatenate([fold(tn(rounded[s], grad_mixed[s]), ones, members) for s in part], axis=0)
    gq = head_pull(q_raw, q_fac, q_live, q_grad, ones).astype(BF)
    gk = head_pull(k_raw, k_fac, k_live, k_grad, ones).astype(BF)
    gv = v_grad.astype(BF)
    grad_normed = (
        nt(gq, w_proj[:, :channels])
        + nt(gk, w_proj[:, channels : 2 * channels])
        + nt(gv, w_proj[:, 2 * channels :])
    )
    lifted = grad_normed * gain
    inner = jnp.mean(lifted * inputs, axis=-1, keepdims=True)
    return lifted * inv - inputs * (inv * inv * inv * inner)


def iota(shape, dim):
    return lax.broadcasted_iota(jnp.int32, shape, dim)


def one_hot(shape, source):
    return jnp.where(iota(shape, 1) == source(iota(shape, 0)), 1.0, 0.0).astype(BF)


def pack(rows, peers):
    half = rows.shape[1] // 2
    per = rows.shape[0] // peers
    low = rows[:, :half].reshape(peers, per, half)
    high = rows[:, half:].reshape(peers, per, half)
    return jnp.concatenate([low, high], axis=1).astype(BF)


def unpack(chunks):
    peers, double, half = chunks.shape
    wide = chunks.astype(F32)
    low = wide[:, : double // 2].reshape(peers * double // 2, half)
    high = wide[:, double // 2 :].reshape(peers * double // 2, half)
    return jnp.concatenate([low, high], axis=1).astype(BF)


X, G, U, B = range(4)


def kernel(
    dims,
    ens_any,
    gain_any,
    w_proj_any,
    w_out_any,
    conv_any,
    cot_any,
    result_ref,
    grad_ref,
    ens_ref,
    cot_ref,
    gain_ref,
    w_proj_ref,
    w_out_ref,
    conv_ref,
    out_buf,
    in_buf,
    halo_cot,
    edge_cot,
    gf_ref,
    side_out,
    rim_in,
    side_in,
    corner_in,
    column_ref,
    load_sem,
    ex_send,
    ex_recv,
    halo_send,
    halo_recv,
    rim_send,
    rim_recv,
    side_send,
    side_recv,
    corner_send,
    corner_recv,
    flag,
):
    mem, lat, lon, channels, peers, lats, lons = dims
    cells = mem * lat * lon
    members = mem * peers
    me = lax.axis_index("member")
    my_lat = lax.axis_index("lat")
    my_lon = lax.axis_index("lon")

    pairs = (
        (ens_any, ens_ref),
        (cot_any, cot_ref),
        (conv_any, conv_ref),
        (w_proj_any, w_proj_ref),
        (w_out_any, w_out_ref),
        (gain_any, gain_ref),
    )
    loads = [
        pltpu.make_async_copy(src, dst, load_sem.at[i]) for i, (src, dst) in enumerate(pairs)
    ]
    def partner(j):
        return {"member": lax.rem(me + j, peers)}

    def near(d_lat, d_lon):
        return {
            "lat": lax.rem(my_lat + d_lat + lats, lats),
            "lon": lax.rem(my_lon + d_lon + lons, lons),
        }

    around = [(a, b) for a in (-1, 0, 1) for b in (-1, 0, 1) if (a, b) != (0, 0)]
    barrier = pltpu.get_barrier_semaphore()
    far_first = sorted(range(1, peers), key=lambda j: -(min(j, peers - j) // 2 + 2 * (j % 2)))
    ring = peers // 2
    my_z, my_y = me // 2, lax.rem(me, 2)

    def along(dz):
        return {"member": lax.rem(my_z + dz, ring) * 2 + my_y}

    twin = {"member": my_z * 2 + 1 - my_y}
    z_steps = sorted(range(1, ring), key=lambda j: -min(j, ring - j))
    close = [along(dz) for dz in z_steps] + [twin]
    for device in close:
        pl.semaphore_signal(barrier, inc=1, device_id=device, device_id_type=MESH)
    for d_lat, d_lon in around:
        pl.semaphore_signal(barrier, inc=1, device_id=near(d_lat, d_lon), device_id_type=MESH)

    for load in loads:
        load.start()

    blocks = peers // lat
    width = lon // blocks
    my_row, my_block = me // blocks, lax.rem(me, blocks)

    def home_source(i):
        j, m, c = i // (mem * width), (i // width) % mem, i % width
        q = lax.rem(me + j, peers)
        return (m * lat + q // blocks) * lon + lax.rem(q, blocks) * width + c

    def home_target(i):
        m, a, b = i // (lat * lon), (i // lon) % lat, i % lon
        j = lax.rem(a * blocks + b // width - me + peers, peers)
        return (j * mem + m) * width + b % width

    def cell_source(i):
        c, j, m = i // members, (i // mem) % peers, i % mem
        return (j * mem + m) * width + c

    def cell_target(i):
        j, m, c = i // (mem * width), (i // width) % mem, i % width
        return (c * peers + j) * mem + m

    def edge_source(i):
        count = mem * lat
        return (i % count) * lon + (i // count) * (lon - 1)

    square = (cells, cells)
    home_out = one_hot(square, home_source)
    home_in = one_hot(square, home_target)
    cell_in = one_hot(square, cell_source)
    cell_out = one_hot(square, cell_target)
    edges = one_hot((2 * mem * lat, cells), edge_source)

    def exchange(kind, sign, group):
        return [
            pltpu.make_async_remote_copy(
                src_ref=out_buf.at[kind, j],
                dst_ref=in_buf.at[kind, j],
                send_sem=ex_send.at[kind],
                recv_sem=ex_recv.at[kind],
                device_id=partner(j if sign > 0 else peers - j),
                device_id_type=MESH,
            )
            for j in group
        ]

    def exchange_all(kind):
        return pltpu.make_async_remote_copy(
            src_ref=out_buf.at[kind, pl.ds(1, peers - 1)],
            dst_ref=in_buf.at[kind, pl.ds(1, peers - 1)],
            send_sem=ex_send.at[kind],
            recv_sem=ex_recv.at[kind],
            device_id=partner(1),
            device_id_type=MESH,
        )

    def send(kind, order, rows, sign):
        packed = pack(nn(order, rows), peers)
        out_buf[kind] = packed
        in_buf[kind, 0] = packed[0]
        for copy in exchange(kind, sign, far_first):
            copy.start()

    def receive(kind, order):
        exchange_all(kind).wait_recv()
        return nn(order, unpack(in_buf[kind]))

    has_low, has_high = my_lat > 0, my_lat < lats - 1

    def halo_group(d_lat):
        which = 1 - d_lat
        copies = [
            pltpu.make_async_remote_copy(
                src_ref=edge_cot,
                dst_ref=halo_cot.at[0 if d_lon > 0 else 1, lat + 2 + which],
                send_sem=halo_send.at[which],
                recv_sem=halo_recv.at[which],
                device_id=near(d_lat, d_lon),
                device_id_type=MESH,
            )
            for d_lon in (-1, 1)
        ]
        if d_lat:
            copies.append(
                pltpu.make_async_remote_copy(
                    src_ref=cot_ref.at[:, lat - 1 if d_lat > 0 else 0],
                    dst_ref=halo_cot.at[:, 0 if d_lat > 0 else lat + 1],
                    send_sem=halo_send.at[3 + (which > 1)],
                    recv_sem=halo_recv.at[3 + (which > 1)],
                    device_id=near(d_lat, 0),
                    device_id_type=MESH,
                )
            )
        return copies

    def halo_columns(which):
        columns = halo_cot.at[:, lat + 2 + which]
        return pltpu.make_async_remote_copy(
            src_ref=columns,
            dst_ref=columns,
            send_sem=halo_send.at[which],
            recv_sem=halo_recv.at[which],
            device_id=near(0, 1),
            device_id_type=MESH,
        )

    def start_halo():
        @pl.when(has_high)
        def _():
            for copy in halo_group(1):
                copy.start()

        @pl.when(has_low)
        def _():
            for copy in halo_group(-1):
                copy.start()

        for copy in halo_group(0):
            copy.start()

    def wait_halo():
        halo_columns(1).wait_recv()

        @pl.when(has_low)
        def _():
            halo_columns(0).wait_recv()
            halo_group(1)[2].wait_recv()

        @pl.when(has_high)
        def _():
            halo_columns(2).wait_recv()
            halo_group(-1)[2].wait_recv()

    def wait_halo_sent():
        halo_columns(1).wait_send()

        @pl.when(has_high)
        def _():
            halo_columns(0).wait_send()
            halo_group(1)[2].wait_send()

        @pl.when(has_low)
        def _():
            halo_columns(2).wait_send()
            halo_group(-1)[2].wait_send()

    far, close_by = far_first[: peers // 2], far_first[peers // 2 :] + [0]

    def home_of(j, rim, side):
        return {
            "member": lax.rem(me + peers - j, peers),
            "lat": lax.rem(my_lat + (0 if rim is None else 1 if rim == 0 else lats - 1), lats),
            "lon": lax.rem(my_lon + (0 if side is None else 1 if side == 0 else lons - 1), lons),
        }

    def rim_copies(rim, group):
        return [
            pltpu.make_async_remote_copy(
                src_ref=out_buf.at[U, j],
                dst_ref=rim_in.at[rim, my_block],
                send_sem=rim_send.at[rim],
                recv_sem=rim_recv.at[rim],
                device_id=home_of(j, rim, None),
                device_id_type=MESH,
            )
            for j in group
        ]

    def side_copies(side, group):
        return [
            pltpu.make_async_remote_copy(
                src_ref=side_out.at[side, j],
                dst_ref=side_in.at[side, my_row],
                send_sem=side_send.at[side],
                recv_sem=side_recv.at[side],
                device_id=home_of(j, None, side),
                device_id_type=MESH,
            )
            for j in group
        ]

    def corner_copies(side, rim, group):
        return [
            pltpu.make_async_remote_copy(
                src_ref=side_out.at[side, j],
                dst_ref=corner_in.at[side, rim],
                send_sem=corner_send.at[side, rim],
                recv_sem=corner_recv.at[side, rim],
                device_id=home_of(j, rim, side),
                device_id_type=MESH,
            )
            for j in group
        ]

    def bytes_of(ref, send_sem, recv_sem):
        return pltpu.make_async_remote_copy(
            src_ref=ref,
            dst_ref=ref,
            send_sem=send_sem,
            recv_sem=recv_sem,
            device_id=partner(1),
            device_id_type=MESH,
        )

    def gets_rim(rim):
        return has_low if rim == 0 else has_high

    def sends_rim(rim):
        if rim == 0:
            return jnp.logical_and(has_high, my_row == lat - 1)
        return jnp.logical_and(has_low, my_row == 0)

    def sends_side(side):
        return my_block == (blocks - 1 if side == 0 else 0)

    def start_rims(group):
        for rim in range(2):

            @pl.when(sends_rim(rim))
            def _():
                for copy in rim_copies(rim, group):
                    copy.start()

        for side in range(2):

            @pl.when(sends_side(side))
            def _():
                for copy in side_copies(side, group):
                    copy.start()

                for rim in range(2):

                    @pl.when(sends_rim(rim))
                    def _():
                        for copy in corner_copies(side, rim, group):
                            copy.start()

    def wait_rims():
        for side in range(2):
            bytes_of(side_in.at[side], side_send.at[side], side_recv.at[side]).wait_recv()
        for rim in range(2):

            @pl.when(gets_rim(rim))
            def _():
                bytes_of(rim_in.at[rim], rim_send.at[rim], rim_recv.at[rim]).wait_recv()
                for side in range(2):
                    bytes_of(
                        corner_in.at[side, rim], corner_send.at[side, rim], corner_recv.at[side, rim]
                    ).wait_recv()

    def wait_rims_sent():
        for rim in range(2):

            @pl.when(sends_rim(rim))
            def _():
                bytes_of(out_buf.at[U], rim_send.at[rim], rim_recv.at[rim]).wait_send()

        for side in range(2):

            @pl.when(sends_side(side))
            def _():
                bytes_of(side_out.at[side], side_send.at[side], side_recv.at[side]).wait_send()
                for rim in range(2):

                    @pl.when(sends_rim(rim))
                    def _():
                        bytes_of(
                            side_out.at[side], corner_send.at[side, rim], corner_recv.at[side, rim]
                        ).wait_send()

    def side_pack(rows):
        half = channels // 2
        shape = (2 * mem * peers, mem * peers)
        i, k = iota(shape, 0), iota(shape, 1)
        same = (i // (2 * mem)) * mem + i % mem == k
        upper = (i // mem) % 2 == 1
        low = jnp.where(jnp.logical_and(same, jnp.logical_not(upper)), 1.0, 0.0).astype(BF)
        high = jnp.where(jnp.logical_and(same, upper), 1.0, 0.0).astype(BF)
        return nn(low, rows[:, :half]) + nn(high, rows[:, half:])

    def rim_source(i):
        m, b = i // lon, i % lon
        return ((b // width) * mem + m) * width + b % width

    def rim_rows(rim, pick):
        return nn(pick, unpack(rim_in[rim])).astype(BF)

    def side_column(side):
        half = channels // 2
        parts = [side_in.at[side, a] for a in range(lat)] + [corner_in.at[side, rim] for rim in range(2)]
        for n, part in enumerate(parts):
            rows = part[...].astype(F32)
            column_ref[side, n * mem : (n + 1) * mem, 0:half] = rows[:mem]
            column_ref[side, n * mem : (n + 1) * mem, half:channels] = rows[mem:]
        return column_ref[side].astype(BF)

    strip = lat + 2

    def cot_edge(m, shift, a):
        which = jnp.where(a == 0, 0, jnp.where(a == strip - 1, 2, 1))
        row = jnp.where(a == 0, lat - 1, jnp.where(a == strip - 1, 0, a - 1))
        return which * lon + (mem * lat if shift < 0 else 0) + m * lat + row

    def up_edge(m, shift, a):
        outer = jnp.where(a == 0, lat, jnp.where(a == strip - 1, lat + 1, a - 1))
        return outer * mem + m

    def picks_of(edge_row, count):
        return {(m, shift): pick_of(count, edge_row, m, shift) for m in range(mem) for shift in (-1, 1)}

    def pick_of(count, edge_row, m, shift):
        shape = (strip * lon, strip * lon + count)
        a, b = iota(shape, 0) // lon, iota(shape, 0) % lon
        outer = strip * lon + edge_row(m, shift, a)
        source = jnp.where(b == (0 if shift < 0 else lon - 1), outer, a * lon + b + shift)
        open_row = jnp.logical_and(
            jnp.logical_or(a > 0, has_low), jnp.logical_or(a < strip - 1, has_high)
        )
        return jnp.where(jnp.logical_and(iota(shape, 1) == source, open_row), 1.0, 0.0).astype(BF)

    def shifted(field, columns, picks, m, shift):
        if shift == 0:
            return field
        return nn(picks[m, shift], jnp.concatenate([field, columns], axis=0)).astype(BF)

    def conv(fields, columns, picks, adjoint):
        total = None
        for c in range(3):
            shift = 1 - c if adjoint else c - 1
            side = 0 if shift < 0 else 1
            wide = [shifted(fields[m], columns[side], picks, m, shift) for m in range(mem)]
            for r in range(3):
                start = (2 - r if adjoint else r) * lon
                window = jnp.concatenate([w[start : start + lat * lon] for w in wide], axis=0)
                term = nt(window, conv_ref[r, c]) if adjoint else nn(window, conv_ref[r, c])
                total = term if total is None else total + term
        return total

    def closed(rows, there):
        return jnp.where(there, rows.astype(F32), 0.0).astype(BF)

    @pl.when(jnp.logical_not(has_low))
    def _():
        halo_cot[:, 0] = jnp.zeros((mem, lon, channels), BF)
        halo_cot[:, lat + 2] = jnp.zeros((mem, lon, channels), BF)
        rim_in[0] = jnp.zeros(rim_in.shape[1:], BF)
        corner_in[:, 0] = jnp.zeros((2,) + corner_in.shape[2:], BF)

    @pl.when(jnp.logical_not(has_high))
    def _():
        halo_cot[:, lat + 1] = jnp.zeros((mem, lon, channels), BF)
        halo_cot[:, lat + 4] = jnp.zeros((mem, lon, channels), BF)
        rim_in[1] = jnp.zeros(rim_in.shape[1:], BF)
        corner_in[:, 1] = jnp.zeros((2,) + corner_in.shape[2:], BF)

    column_ref[...] = jnp.zeros(column_ref.shape, F32)
    loads[0].wait()
    ens = ens_ref[...].reshape(cells, channels)
    loads[1].wait()
    cot = cot_ref[...].reshape(cells, channels)
    packed = pack(nn(home_out, ens), peers)
    out_buf[X] = packed
    in_buf[X, 0] = packed[0]
    edge_cot[...] = nn(edges, cot).astype(BF)
    pl.semaphore_wait(barrier, len(close) + len(around))
    pl.semaphore_signal(flag, inc=1, device_id=twin, device_id_type=MESH)
    copies = dict(zip(far_first, exchange(X, 1, far_first)))
    for j in far_first:
        if j % 2 == 0:
            copies[j].start()
    start_halo()
    pl.semaphore_wait(flag, 1)
    for j in far_first:
        if j % 2 == 1:
            copies[j].start()

    ones = head_blocks(channels, members).astype(BF)
    loads[2].wait()
    cot_picks = picks_of(cot_edge, 3 * lon)
    wait_halo()
    cot_fields = [
        jnp.concatenate(
            [
                closed(halo_cot[m, 0], has_low),
                cot_ref[m].reshape(lat * lon, channels),
                closed(halo_cot[m, lat + 1], has_high),
            ],
            axis=0,
        )
        for m in range(mem)
    ]
    cot_columns = [halo_cot[side, lat + 2 : lat + 5].reshape(3 * lon, channels) for side in range(2)]
    grad_field = cot.astype(F32) + conv(cot_fields, cot_columns, cot_picks, True)
    gf_ref[...] = grad_field
    send(G, home_out, grad_field.astype(BF), 1)

    for load in loads[3:]:
        load.wait()
    gain = gain_ref[...]
    w_proj = w_proj_ref[...]
    w_out = w_out_ref[...]
    x = receive(X, cell_in).astype(BF)
    updated, saved = cell_forward(x, gain, w_proj, w_out, ones, members)
    packed = pack(nn(cell_out, updated), peers)
    out_buf[U] = packed
    in_buf[U, 0] = packed[0]
    for side, c in enumerate((width - 1, 0)):
        rows = updated[c * members : (c + 1) * members]
        side_out[side] = side_pack(rows).reshape(side_out.shape[1:]).astype(BF)
    for group in (far, close_by):
        for copy in exchange(U, -1, [j for j in group if j]):
            copy.start()
        start_rims(group)

    grads = receive(G, cell_in).astype(BF)
    grad_inputs = cell_backward(grads, saved, gain, w_proj, w_out, ones, members)
    send(B, cell_out, grad_inputs.astype(BF), -1)

    up_picks = picks_of(up_edge, column_ref.shape[1])
    rim_pick = one_hot((mem * lon, mem * lon), rim_source)
    field = receive(U, home_in)
    wait_rims()
    rows = field.astype(BF)
    low = closed(rim_rows(0, rim_pick), has_low)
    high = closed(rim_rows(1, rim_pick), has_high)
    up_fields = [
        jnp.concatenate(
            [
                low[m * lon : (m + 1) * lon],
                rows[m * lat * lon : (m + 1) * lat * lon],
                high[m * lon : (m + 1) * lon],
            ],
            axis=0,
        )
        for m in range(mem)
    ]
    result = field + conv(up_fields, [side_column(0), side_column(1)], up_picks, False)
    result_ref[...] = result.astype(BF).reshape(result_ref.shape)

    back = receive(B, home_in)
    grad_ref[...] = (gf_ref[...] + back).astype(BF).reshape(grad_ref.shape)

    for kind in (X, G, U, B):
        exchange_all(kind).wait_send()
    wait_halo_sent()
    wait_rims_sent()


def store_kernel(result_in, grad_in, result_out, grad_out, sem):
    copies = [
        pltpu.make_async_copy(result_in, result_out, sem.at[0]),
        pltpu.make_async_copy(grad_in, grad_out, sem.at[1]),
    ]
    for copy in copies:
        copy.start()
    for copy in copies:
        copy.wait()


MESH = pl.DeviceIdType.MESH
LIMIT = 16 * 1024 * 1024


def per_device(ensemble, norm_gain, project_weight, output_weight, conv_kernel, cotangent):
    mem, lat, lon, channels = ensemble.shape
    peers = lax.axis_size("member")
    dims = (mem, lat, lon, channels, peers, lax.axis_size("lat"), lax.axis_size("lon"))
    vmem = pl.BlockSpec(memory_space=pltpu.VMEM)
    anywhere = pl.BlockSpec(memory_space=pl.ANY)
    chunk = (4, peers, 2 * mem * lat, channels // 2)
    halo = (mem, lat + 5, lon, channels)
    field = jax.ShapeDtypeStruct(ensemble.shape, BF)
    outs = pl.pallas_call(
        functools.partial(kernel, dims),
        out_shape=(field, field),
        in_specs=[pl.BlockSpec(memory_space=pltpu.HBM)] * 6,
        out_specs=(vmem, vmem),
        scratch_shapes=[
            pltpu.VMEM(ensemble.shape, BF),
            pltpu.VMEM(ensemble.shape, BF),
            pltpu.VMEM((1, channels), F32),
            pltpu.VMEM(project_weight.shape, BF),
            pltpu.VMEM(output_weight.shape, BF),
            pltpu.VMEM(conv_kernel.shape, BF),
            pltpu.VMEM(chunk, BF),
            pltpu.VMEM(chunk, BF),
            pltpu.VMEM(halo, BF),
            pltpu.VMEM((2 * mem * lat, channels), BF),
            pltpu.VMEM((mem * lat * lon, channels), F32),
            pltpu.VMEM((2, peers, 2 * mem, channels // 2), BF),
            pltpu.VMEM((2, peers // lat) + chunk[2:], BF),
            pltpu.VMEM((2, lat, 2 * mem, channels // 2), BF),
            pltpu.VMEM((2, 2, 2 * mem, channels // 2), BF),
            pltpu.VMEM((2, 16, channels), F32),
            pltpu.SemaphoreType.DMA((6,)),
            pltpu.SemaphoreType.DMA((4,)),
            pltpu.SemaphoreType.DMA((4,)),
            pltpu.SemaphoreType.DMA((5,)),
            pltpu.SemaphoreType.DMA((5,)),
            pltpu.SemaphoreType.DMA((2,)),
            pltpu.SemaphoreType.DMA((2,)),
            pltpu.SemaphoreType.DMA((2,)),
            pltpu.SemaphoreType.DMA((2,)),
            pltpu.SemaphoreType.DMA((2, 2)),
            pltpu.SemaphoreType.DMA((2, 2)),
            pltpu.SemaphoreType.REGULAR,
        ],
        compiler_params=pltpu.CompilerParams(
            collective_id=0, has_side_effects=True, vmem_limit_bytes=LIMIT
        ),
    )(
        *(
            pltpu.with_memory_space_constraint(value, pltpu.HBM)
            for value in (
                ensemble,
                norm_gain.reshape(1, channels),
                project_weight,
                output_weight,
                conv_kernel,
                cotangent,
            )
        )
    )
    return pl.pallas_call(
        store_kernel,
        out_shape=(field, field),
        in_specs=[vmem, vmem],
        out_specs=(anywhere, anywhere),
        scratch_shapes=[pltpu.SemaphoreType.DMA((2,))],
        compiler_params=pltpu.CompilerParams(vmem_limit_bytes=LIMIT),
    )(*outs)


def solution(mesh):
    field = P("member", "lat", "lon", None)
    return jax.shard_map(
        per_device,
        mesh=mesh,
        in_specs=(field, P(), P(), P(), P(), field),
        out_specs=(field, field),
        check_vma=False,
    )
```

```python
import functools
import math

import jax
import jax.numpy as jnp
from jax import lax
from jax.experimental import pallas as pl
from jax.experimental.pallas import tpu as pltpu
from jax.sharding import PartitionSpec as P

HEADS = 8
FLOOR = 0.5
EPSILON = 1e-06
BF = jnp.bfloat16
F32 = jnp.float32


def mm(a, b, dims):
    return lax.dot_general(a, b, (dims, ((), ())), preferred_element_type=F32)


def nn(a, b):
    return mm(a, b, ((1,), (0,)))


def nt(a, b):
    return mm(a, b, ((1,), (1,)))


def tn(a, b):
    return mm(a, b, ((0,), (0,)))


def head_blocks(channels, members):
    width = channels // HEADS
    row = lax.broadcasted_iota(jnp.int32, (HEADS * members, channels), 0) // members
    col = lax.broadcasted_iota(jnp.int32, (HEADS * members, channels), 1) // width
    return row == col


def spread(rows, blocks):
    return jnp.concatenate([rows] * HEADS, axis=0) * blocks


def head_scale(raw, ones):
    width = raw.shape[1] // HEADS
    mean_sq = nn((raw * raw).astype(BF), ones) * (1.0 / width)
    factor = lax.rsqrt(jnp.maximum(mean_sq, FLOOR))
    live = jnp.where(mean_sq > FLOOR, 1.0, jnp.where(mean_sq == FLOOR, 0.5, 0.0))
    return factor, live


def cell_forward(x, gain, w_proj, w_out, ones, members):
    rows, channels = x.shape
    cells = rows // members
    scale = 1.0 / math.sqrt(channels // HEADS)
    inputs = x.astype(F32)
    inv = lax.rsqrt(jnp.mean(inputs * inputs, axis=-1, keepdims=True) + EPSILON)
    normed = (inputs * inv * gain).astype(BF)
    k_raw = nn(normed, w_proj[:, channels : 2 * channels]).astype(BF).astype(F32)
    q_raw = nn(normed, w_proj[:, :channels]).astype(BF).astype(F32)
    values = nn(normed, w_proj[:, 2 * channels :]).astype(BF)
    q_fac, q_live = head_scale(q_raw, ones)
    k_fac, k_live = head_scale(k_raw, ones)
    queries = (q_raw * q_fac).astype(BF)
    keys = (k_raw * k_fac).astype(BF)
    part = [slice(c * members, (c + 1) * members) for c in range(cells)]
    k_bd = [spread(keys[s], ones) for s in part]
    v_bd = [spread(values[s], ones) for s in part]
    scores = jnp.concatenate([nt(queries[s], k) for s, k in zip(part, k_bd)], axis=0)
    expd = jnp.exp(scores * scale)
    narrow = expd.astype(BF)
    inv_total = 1.0 / nn(narrow, ones)
    mixed = jnp.concatenate([nn(narrow[s], v) for s, v in zip(part, v_bd)], axis=0)
    updated = (inputs + nn((mixed * inv_total).astype(BF), w_out)).astype(BF)
    soft = expd * inv_total
    rounded = soft.astype(BF)
    saved = (inputs, inv, q_raw, k_raw, q_fac, k_fac, q_live, k_live, queries, k_bd, v_bd, soft, rounded)
    return updated, saved


def head_pull(raw, factor, live, grad, ones):
    width = raw.shape[1] // HEADS
    inner = nn((raw * grad).astype(BF), ones) * (1.0 / width)
    return grad * factor - raw * (factor * factor * factor * live * inner)


def fold(full, ones, members):
    kept = full * ones.astype(F32)
    total = kept[:members]
    for h in range(1, HEADS):
        total = total + kept[h * members : (h + 1) * members]
    return total


def cell_backward(grad_field, saved, gain, w_proj, w_out, ones, members):
    inputs, inv, q_raw, k_raw, q_fac, k_fac, q_live, k_live, queries, k_bd, v_bd, soft, rounded = saved
    rows, channels = inputs.shape
    cells = rows // members
    scale = 1.0 / math.sqrt(channels // HEADS)
    part = [slice(c * members, (c + 1) * members) for c in range(cells)]
    grad_mixed = nt(grad_field, w_out).astype(BF)
    dprob = jnp.concatenate([nt(grad_mixed[s], v) for s, v in zip(part, v_bd)], axis=0)
    delta = nn((soft * dprob).astype(BF), ones)
    dscore = (soft * (dprob - delta)).astype(BF)
    q_grad = jnp.concatenate([nn(dscore[s], k) for s, k in zip(part, k_bd)], axis=0) * scale
    k_grad = jnp.concatenate([fold(tn(dscore[s], queries[s]), ones, members) for s in part], axis=0) * scale
    v_grad = jnp.concatenate([fold(tn(rounded[s], grad_mixed[s]), ones, members) for s in part], axis=0)
    gq = head_pull(q_raw, q_fac, q_live, q_grad, ones).astype(BF)
    gk = head_pull(k_raw, k_fac, k_live, k_grad, ones).astype(BF)
    gv = v_grad.astype(BF)
    grad_normed = (
        nt(gq, w_proj[:, :channels])
        + nt(gk, w_proj[:, channels : 2 * channels])
        + nt(gv, w_proj[:, 2 * channels :])
    )
    lifted = grad_normed * gain
    inner = jnp.mean(lifted * inputs, axis=-1, keepdims=True)
    return lifted * inv - inputs * (inv * inv * inv * inner)


def iota(shape, dim):
    return lax.broadcasted_iota(jnp.int32, shape, dim)


def one_hot(shape, source):
    return jnp.where(iota(shape, 1) == source(iota(shape, 0)), 1.0, 0.0).astype(BF)


def pack(rows, peers):
    half = rows.shape[1] // 2
    per = rows.shape[0] // peers
    low = rows[:, :half].reshape(peers, per, half)
    high = rows[:, half:].reshape(peers, per, half)
    return jnp.concatenate([low, high], axis=1).astype(BF)


def unpack(chunks):
    peers, double, half = chunks.shape
    wide = chunks.astype(F32)
    low = wide[:, : double // 2].reshape(peers * double // 2, half)
    high = wide[:, double // 2 :].reshape(peers * double // 2, half)
    return jnp.concatenate([low, high], axis=1).astype(BF)


X, G, U, B = range(4)


def kernel(
    dims,
    ens_any,
    gain_any,
    w_proj_any,
    w_out_any,
    conv_any,
    cot_any,
    result_ref,
    grad_ref,
    ens_ref,
    cot_ref,
    gain_ref,
    w_proj_ref,
    w_out_ref,
    conv_ref,
    out_buf,
    in_buf,
    halo_cot,
    edge_cot,
    gf_ref,
    side_out,
    rim_in,
    side_in,
    corner_in,
    column_ref,
    load_sem,
    ex_send,
    ex_recv,
    halo_send,
    halo_recv,
    rim_send,
    rim_recv,
    side_send,
    side_recv,
    corner_send,
    corner_recv,
    flag,
):
    mem, lat, lon, channels, peers, lats, lons = dims
    cells = mem * lat * lon
    members = mem * peers
    me = lax.axis_index("member")
    my_lat = lax.axis_index("lat")
    my_lon = lax.axis_index("lon")

    pairs = (
        (ens_any, ens_ref),
        (cot_any, cot_ref),
        (conv_any, conv_ref),
        (w_proj_any, w_proj_ref),
        (w_out_any, w_out_ref),
        (gain_any, gain_ref),
    )
    loads = [
        pltpu.make_async_copy(src, dst, load_sem.at[i]) for i, (src, dst) in enumerate(pairs)
    ]
    for load in loads:
        load.start()

    def partner(j):
        return {"member": lax.rem(me + j, peers)}

    def near(d_lat, d_lon):
        return {
            "lat": lax.rem(my_lat + d_lat + lats, lats),
            "lon": lax.rem(my_lon + d_lon + lons, lons),
        }

    around = [(a, b) for a in (-1, 0, 1) for b in (-1, 0, 1) if (a, b) != (0, 0)]
    barrier = pltpu.get_barrier_semaphore()
    far_first = sorted(range(1, peers), key=lambda j: -(min(j, peers - j) // 2 + 2 * (j % 2)))
    ring = peers // 2
    my_z, my_y = me // 2, lax.rem(me, 2)

    def along(dz):
        return {"member": lax.rem(my_z + dz, ring) * 2 + my_y}

    twin = {"member": my_z * 2 + 1 - my_y}
    z_steps = sorted(range(1, ring), key=lambda j: -min(j, ring - j))
    close = [along(dz) for dz in z_steps] + [twin]
    for device in close:
        pl.semaphore_signal(barrier, inc=1, device_id=device, device_id_type=MESH)
    for d_lat, d_lon in around:
        pl.semaphore_signal(barrier, inc=1, device_id=near(d_lat, d_lon), device_id_type=MESH)

    blocks = peers // lat
    width = lon // blocks
    my_row, my_block = me // blocks, lax.rem(me, blocks)

    def home_source(i):
        j, m, c = i // (mem * width), (i // width) % mem, i % width
        q = lax.rem(me + j, peers)
        return (m * lat + q // blocks) * lon + lax.rem(q, blocks) * width + c

    def home_target(i):
        m, a, b = i // (lat * lon), (i // lon) % lat, i % lon
        j = lax.rem(a * blocks + b // width - me + peers, peers)
        return (j * mem + m) * width + b % width

    def cell_source(i):
        c, j, m = i // members, (i // mem) % peers, i % mem
        return (j * mem + m) * width + c

    def cell_target(i):
        j, m, c = i // (mem * width), (i // width) % mem, i % width
        return (c * peers + j) * mem + m

    def edge_source(i):
        count = mem * lat
        return (i % count) * lon + (i // count) * (lon - 1)

    square = (cells, cells)
    home_out = one_hot(square, home_source)
    home_in = one_hot(square, home_target)
    cell_in = one_hot(square, cell_source)
    cell_out = one_hot(square, cell_target)
    edges = one_hot((2 * mem * lat, cells), edge_source)

    def exchange(kind, sign, group):
        return [
            pltpu.make_async_remote_copy(
                src_ref=out_buf.at[kind, j],
                dst_ref=in_buf.at[kind, j],
                send_sem=ex_send.at[kind],
                recv_sem=ex_recv.at[kind],
                device_id=partner(j if sign > 0 else peers - j),
                device_id_type=MESH,
            )
            for j in group
        ]

    def exchange_all(kind):
        return pltpu.make_async_remote_copy(
            src_ref=out_buf.at[kind, pl.ds(1, peers - 1)],
            dst_ref=in_buf.at[kind, pl.ds(1, peers - 1)],
            send_sem=ex_send.at[kind],
            recv_sem=ex_recv.at[kind],
            device_id=partner(1),
            device_id_type=MESH,
        )

    def send(kind, order, rows, sign):
        packed = pack(nn(order, rows), peers)
        out_buf[kind] = packed
        in_buf[kind, 0] = packed[0]
        for copy in exchange(kind, sign, far_first):
            copy.start()

    def receive(kind, order):
        exchange_all(kind).wait_recv()
        return nn(order, unpack(in_buf[kind]))

    has_low, has_high = my_lat > 0, my_lat < lats - 1

    def halo_group(d_lat):
        which = 1 - d_lat
        copies = [
            pltpu.make_async_remote_copy(
                src_ref=edge_cot,
                dst_ref=halo_cot.at[0 if d_lon > 0 else 1, lat + 2 + which],
                send_sem=halo_send.at[which],
                recv_sem=halo_recv.at[which],
                device_id=near(d_lat, d_lon),
                device_id_type=MESH,
            )
            for d_lon in (-1, 1)
        ]
        if d_lat:
            copies.append(
                pltpu.make_async_remote_copy(
                    src_ref=cot_ref.at[:, lat - 1 if d_lat > 0 else 0],
                    dst_ref=halo_cot.at[:, 0 if d_lat > 0 else lat + 1],
                    send_sem=halo_send.at[3 + (which > 1)],
                    recv_sem=halo_recv.at[3 + (which > 1)],
                    device_id=near(d_lat, 0),
                    device_id_type=MESH,
                )
            )
        return copies

    def halo_columns(which):
        columns = halo_cot.at[:, lat + 2 + which]
        return pltpu.make_async_remote_copy(
            src_ref=columns,
            dst_ref=columns,
            send_sem=halo_send.at[which],
            recv_sem=halo_recv.at[which],
            device_id=near(0, 1),
            device_id_type=MESH,
        )

    def start_halo():
        @pl.when(has_high)
        def _():
            for copy in halo_group(1):
                copy.start()

        @pl.when(has_low)
        def _():
            for copy in halo_group(-1):
                copy.start()

        for copy in halo_group(0):
            copy.start()

    def wait_halo():
        halo_columns(1).wait_recv()

        @pl.when(has_low)
        def _():
            halo_columns(0).wait_recv()
            halo_group(1)[2].wait_recv()

        @pl.when(has_high)
        def _():
            halo_columns(2).wait_recv()
            halo_group(-1)[2].wait_recv()

    def wait_halo_sent():
        halo_columns(1).wait_send()

        @pl.when(has_high)
        def _():
            halo_columns(0).wait_send()
            halo_group(1)[2].wait_send()

        @pl.when(has_low)
        def _():
            halo_columns(2).wait_send()
            halo_group(-1)[2].wait_send()

    far, close_by = far_first[: peers // 2], far_first[peers // 2 :] + [0]

    def home_of(j, rim, side):
        return {
            "member": lax.rem(me + peers - j, peers),
            "lat": lax.rem(my_lat + (0 if rim is None else 1 if rim == 0 else lats - 1), lats),
            "lon": lax.rem(my_lon + (0 if side is None else 1 if side == 0 else lons - 1), lons),
        }

    def rim_copies(rim, group):
        return [
            pltpu.make_async_remote_copy(
                src_ref=out_buf.at[U, j],
                dst_ref=rim_in.at[rim, my_block],
                send_sem=rim_send.at[rim],
                recv_sem=rim_recv.at[rim],
                device_id=home_of(j, rim, None),
                device_id_type=MESH,
            )
            for j in group
        ]

    def side_copies(side, group):
        return [
            pltpu.make_async_remote_copy(
                src_ref=side_out.at[side, j],
                dst_ref=side_in.at[side, my_row],
                send_sem=side_send.at[side],
                recv_sem=side_recv.at[side],
                device_id=home_of(j, None, side),
                device_id_type=MESH,
            )
            for j in group
        ]

    def corner_copies(side, rim, group):
        return [
            pltpu.make_async_remote_copy(
                src_ref=side_out.at[side, j],
                dst_ref=corner_in.at[side, rim],
                send_sem=corner_send.at[side, rim],
                recv_sem=corner_recv.at[side, rim],
                device_id=home_of(j, rim, side),
                device_id_type=MESH,
            )
            for j in group
        ]

    def bytes_of(ref, send_sem, recv_sem):
        return pltpu.make_async_remote_copy(
            src_ref=ref,
            dst_ref=ref,
            send_sem=send_sem,
            recv_sem=recv_sem,
            device_id=partner(1),
            device_id_type=MESH,
        )

    def gets_rim(rim):
        return has_low if rim == 0 else has_high

    def sends_rim(rim):
        if rim == 0:
            return jnp.logical_and(has_high, my_row == lat - 1)
        return jnp.logical_and(has_low, my_row == 0)

    def sends_side(side):
        return my_block == (blocks - 1 if side == 0 else 0)

    def start_rims(group):
        for rim in range(2):

            @pl.when(sends_rim(rim))
            def _():
                for copy in rim_copies(rim, group):
                    copy.start()

        for side in range(2):

            @pl.when(sends_side(side))
            def _():
                for copy in side_copies(side, group):
                    copy.start()

                for rim in range(2):

                    @pl.when(sends_rim(rim))
                    def _():
                        for copy in corner_copies(side, rim, group):
                            copy.start()

    def wait_rims():
        for side in range(2):
            bytes_of(side_in.at[side], side_send.at[side], side_recv.at[side]).wait_recv()
        for rim in range(2):

            @pl.when(gets_rim(rim))
            def _():
                bytes_of(rim_in.at[rim], rim_send.at[rim], rim_recv.at[rim]).wait_recv()
                for side in range(2):
                    bytes_of(
                        corner_in.at[side, rim], corner_send.at[side, rim], corner_recv.at[side, rim]
                    ).wait_recv()

    def wait_rims_sent():
        for rim in range(2):

            @pl.when(sends_rim(rim))
            def _():
                bytes_of(out_buf.at[U], rim_send.at[rim], rim_recv.at[rim]).wait_send()

        for side in range(2):

            @pl.when(sends_side(side))
            def _():
                bytes_of(side_out.at[side], side_send.at[side], side_recv.at[side]).wait_send()
                for rim in range(2):

                    @pl.when(sends_rim(rim))
                    def _():
                        bytes_of(
                            side_out.at[side], corner_send.at[side, rim], corner_recv.at[side, rim]
                        ).wait_send()

    def side_pack(rows):
        half = channels // 2
        shape = (2 * mem * peers, mem * peers)
        i, k = iota(shape, 0), iota(shape, 1)
        same = (i // (2 * mem)) * mem + i % mem == k
        upper = (i // mem) % 2 == 1
        low = jnp.where(jnp.logical_and(same, jnp.logical_not(upper)), 1.0, 0.0).astype(BF)
        high = jnp.where(jnp.logical_and(same, upper), 1.0, 0.0).astype(BF)
        return nn(low, rows[:, :half]) + nn(high, rows[:, half:])

    def rim_source(i):
        m, b = i // lon, i % lon
        return ((b // width) * mem + m) * width + b % width

    def rim_rows(rim, pick):
        return nn(pick, unpack(rim_in[rim])).astype(BF)

    def side_column(side):
        half = channels // 2
        parts = [side_in.at[side, a] for a in range(lat)] + [corner_in.at[side, rim] for rim in range(2)]
        for n, part in enumerate(parts):
            rows = part[...].astype(F32)
            column_ref[side, n * mem : (n + 1) * mem, 0:half] = rows[:mem]
            column_ref[side, n * mem : (n + 1) * mem, half:channels] = rows[mem:]
        return column_ref[side].astype(BF)

    strip = lat + 2

    def cot_edge(m, shift, a):
        which = jnp.where(a == 0, 0, jnp.where(a == strip - 1, 2, 1))
        row = jnp.where(a == 0, lat - 1, jnp.where(a == strip - 1, 0, a - 1))
        return which * lon + (mem * lat if shift < 0 else 0) + m * lat + row

    def up_edge(m, shift, a):
        outer = jnp.where(a == 0, lat, jnp.where(a == strip - 1, lat + 1, a - 1))
        return outer * mem + m

    def picks_of(edge_row, count):
        return {(m, shift): pick_of(count, edge_row, m, shift) for m in range(mem) for shift in (-1, 1)}

    def pick_of(count, edge_row, m, shift):
        shape = (strip * lon, strip * lon + count)
        a, b = iota(shape, 0) // lon, iota(shape, 0) % lon
        outer = strip * lon + edge_row(m, shift, a)
        source = jnp.where(b == (0 if shift < 0 else lon - 1), outer, a * lon + b + shift)
        open_row = jnp.logical_and(
            jnp.logical_or(a > 0, has_low), jnp.logical_or(a < strip - 1, has_high)
        )
        return jnp.where(jnp.logical_and(iota(shape, 1) == source, open_row), 1.0, 0.0).astype(BF)

    def shifted(field, columns, picks, m, shift):
        if shift == 0:
            return field
        return nn(picks[m, shift], jnp.concatenate([field, columns], axis=0)).astype(BF)

    def conv(fields, columns, picks, adjoint):
        halves = []
        wide = {}
        for c in range(3):
            shift = 1 - c if adjoint else c - 1
            side = 0 if shift < 0 else 1
            wide[c] = [shifted(fields[m], columns[side], picks, m, shift) for m in range(mem)]
        count = channels // 2 if adjoint else channels
        for at in range(0, channels, count):
            part = pl.ds(at, count)
            total = None
            for c in range(3):
                for r in range(3):
                    start = (2 - r if adjoint else r) * lon
                    window = jnp.concatenate([w[start : start + lat * lon] for w in wide[c]], axis=0)
                    if adjoint:
                        term = nt(window, conv_ref[r, c, part, :])
                    else:
                        term = nn(window, conv_ref[r, c, :, part])
                    total = term if total is None else total + term
            halves.append(total)
        return jnp.concatenate(halves, axis=1) if adjoint else halves[0]

    def closed(rows, there):
        return jnp.where(there, rows.astype(F32), 0.0).astype(BF)

    @pl.when(jnp.logical_not(has_low))
    def _():
        halo_cot[:, 0] = jnp.zeros((mem, lon, channels), BF)
        halo_cot[:, lat + 2] = jnp.zeros((mem, lon, channels), BF)
        rim_in[0] = jnp.zeros(rim_in.shape[1:], BF)
        corner_in[:, 0] = jnp.zeros((2,) + corner_in.shape[2:], BF)

    @pl.when(jnp.logical_not(has_high))
    def _():
        halo_cot[:, lat + 1] = jnp.zeros((mem, lon, channels), BF)
        halo_cot[:, lat + 4] = jnp.zeros((mem, lon, channels), BF)
        rim_in[1] = jnp.zeros(rim_in.shape[1:], BF)
        corner_in[:, 1] = jnp.zeros((2,) + corner_in.shape[2:], BF)

    column_ref[...] = jnp.zeros(column_ref.shape, F32)
    loads[0].wait()
    ens = ens_ref[...].reshape(cells, channels)
    loads[1].wait()
    cot = cot_ref[...].reshape(cells, channels)
    packed = pack(nn(home_out, ens), peers)
    out_buf[X] = packed
    in_buf[X, 0] = packed[0]
    edge_cot[...] = nn(edges, cot).astype(BF)
    pl.semaphore_wait(barrier, len(close) + len(around))
    pl.semaphore_signal(flag, inc=1, device_id=twin, device_id_type=MESH)
    start_halo()
    copies = dict(zip(far_first, exchange(X, 1, far_first)))
    for j in far_first:
        if j % 2 == 0:
            copies[j].start()
    pl.semaphore_wait(flag, 1)
    for j in far_first:
        if j % 2 == 1:
            copies[j].start()

    ones = head_blocks(channels, members).astype(BF)
    loads[2].wait()
    cot_picks = picks_of(cot_edge, 3 * lon)
    wait_halo()
    cot_fields = [
        jnp.concatenate(
            [
                closed(halo_cot[m, 0], has_low),
                cot_ref[m].reshape(lat * lon, channels),
                closed(halo_cot[m, lat + 1], has_high),
            ],
            axis=0,
        )
        for m in range(mem)
    ]
    cot_columns = [halo_cot[side, lat + 2 : lat + 5].reshape(3 * lon, channels) for side in range(2)]
    grad_field = cot.astype(F32) + conv(cot_fields, cot_columns, cot_picks, True)
    gf_ref[...] = grad_field
    send(G, home_out, grad_field.astype(BF), 1)

    for load in loads[3:]:
        load.wait()
    gain = gain_ref[...]
    w_proj = w_proj_ref[...]
    w_out = w_out_ref[...]
    x = receive(X, cell_in).astype(BF)
    updated, saved = cell_forward(x, gain, w_proj, w_out, ones, members)
    packed = pack(nn(cell_out, updated), peers)
    out_buf[U] = packed
    in_buf[U, 0] = packed[0]
    for side, c in enumerate((width - 1, 0)):
        rows = updated[c * members : (c + 1) * members]
        side_out[side] = side_pack(rows).reshape(side_out.shape[1:]).astype(BF)
    for group in (far, close_by):
        for copy in exchange(U, -1, [j for j in group if j]):
            copy.start()
        start_rims(group)

    grads = receive(G, cell_in).astype(BF)
    grad_inputs = cell_backward(grads, saved, gain, w_proj, w_out, ones, members)
    send(B, cell_out, grad_inputs.astype(BF), -1)

    up_picks = picks_of(up_edge, column_ref.shape[1])
    rim_pick = one_hot((mem * lon, mem * lon), rim_source)
    field = receive(U, home_in)
    wait_rims()
    rows = field.astype(BF)
    low = closed(rim_rows(0, rim_pick), has_low)
    high = closed(rim_rows(1, rim_pick), has_high)
    up_fields = [
        jnp.concatenate(
            [
                low[m * lon : (m + 1) * lon],
                rows[m * lat * lon : (m + 1) * lat * lon],
                high[m * lon : (m + 1) * lon],
            ],
            axis=0,
        )
        for m in range(mem)
    ]
    result = field + conv(up_fields, [side_column(0), side_column(1)], up_picks, False)
    result_ref[...] = result.astype(BF).reshape(result_ref.shape)

    back = receive(B, home_in)
    grad_ref[...] = (gf_ref[...] + back).astype(BF).reshape(grad_ref.shape)

    for kind in (X, G, U, B):
        exchange_all(kind).wait_send()
    wait_halo_sent()
    wait_rims_sent()


def store_kernel(result_in, grad_in, result_out, grad_out, sem):
    copies = [
        pltpu.make_async_copy(result_in, result_out, sem.at[0]),
        pltpu.make_async_copy(grad_in, grad_out, sem.at[1]),
    ]
    for copy in copies:
        copy.start()
    for copy in copies:
        copy.wait()


MESH = pl.DeviceIdType.MESH
LIMIT = 16 * 1024 * 1024


def per_device(ensemble, norm_gain, project_weight, output_weight, conv_kernel, cotangent):
    mem, lat, lon, channels = ensemble.shape
    peers = lax.axis_size("member")
    dims = (mem, lat, lon, channels, peers, lax.axis_size("lat"), lax.axis_size("lon"))
    vmem = pl.BlockSpec(memory_space=pltpu.VMEM)
    anywhere = pl.BlockSpec(memory_space=pl.ANY)
    chunk = (4, peers, 2 * mem * lat, channels // 2)
    halo = (mem, lat + 5, lon, channels)
    field = jax.ShapeDtypeStruct(ensemble.shape, BF)
    outs = pl.pallas_call(
        functools.partial(kernel, dims),
        out_shape=(field, field),
        in_specs=[pl.BlockSpec(memory_space=pltpu.HBM)] * 6,
        out_specs=(vmem, vmem),
        scratch_shapes=[
            pltpu.VMEM(ensemble.shape, BF),
            pltpu.VMEM(ensemble.shape, BF),
            pltpu.VMEM((1, channels), F32),
            pltpu.VMEM(project_weight.shape, BF),
            pltpu.VMEM(output_weight.shape, BF),
            pltpu.VMEM(conv_kernel.shape, BF),
            pltpu.VMEM(chunk, BF),
            pltpu.VMEM(chunk, BF),
            pltpu.VMEM(halo, BF),
            pltpu.VMEM((2 * mem * lat, channels), BF),
            pltpu.VMEM((mem * lat * lon, channels), F32),
            pltpu.VMEM((2, peers, 2 * mem, channels // 2), BF),
            pltpu.VMEM((2, peers // lat) + chunk[2:], BF),
            pltpu.VMEM((2, lat, 2 * mem, channels // 2), BF),
            pltpu.VMEM((2, 2, 2 * mem, channels // 2), BF),
            pltpu.VMEM((2, 16, channels), F32),
            pltpu.SemaphoreType.DMA((6,)),
            pltpu.SemaphoreType.DMA((4,)),
            pltpu.SemaphoreType.DMA((4,)),
            pltpu.SemaphoreType.DMA((5,)),
            pltpu.SemaphoreType.DMA((5,)),
            pltpu.SemaphoreType.DMA((2,)),
            pltpu.SemaphoreType.DMA((2,)),
            pltpu.SemaphoreType.DMA((2,)),
            pltpu.SemaphoreType.DMA((2,)),
            pltpu.SemaphoreType.DMA((2, 2)),
            pltpu.SemaphoreType.DMA((2, 2)),
            pltpu.SemaphoreType.REGULAR,
        ],
        compiler_params=pltpu.CompilerParams(
            collective_id=0, has_side_effects=True, vmem_limit_bytes=LIMIT
        ),
    )(
        *(
            pltpu.with_memory_space_constraint(value, pltpu.HBM)
            for value in (
                ensemble,
                norm_gain.reshape(1, channels),
                project_weight,
                output_weight,
                conv_kernel,
                cotangent,
            )
        )
    )
    return pl.pallas_call(
        store_kernel,
        out_shape=(field, field),
        in_specs=[vmem, vmem],
        out_specs=(anywhere, anywhere),
        scratch_shapes=[pltpu.SemaphoreType.DMA((2,))],
        compiler_params=pltpu.CompilerParams(vmem_limit_bytes=LIMIT),
    )(*outs)


def solution(mesh):
    field = P("member", "lat", "lon", None)
    return jax.shard_map(
        per_device,
        mesh=mesh,
        in_specs=(field, P(), P(), P(), P(), field),
        out_specs=(field, field),
        check_vma=False,
    )
```

```python
import functools
import math

import jax
import jax.numpy as jnp
from jax import lax
from jax.experimental import pallas as pl
from jax.experimental.pallas import tpu as pltpu
from jax.sharding import PartitionSpec as P

HEADS = 8
FLOOR = 0.5
EPSILON = 1e-06
BF = jnp.bfloat16
F32 = jnp.float32


def mm(a, b, dims):
    return lax.dot_general(a, b, (dims, ((), ())), preferred_element_type=F32)


def nn(a, b):
    return mm(a, b, ((1,), (0,)))


def nt(a, b):
    return mm(a, b, ((1,), (1,)))


def tn(a, b):
    return mm(a, b, ((0,), (0,)))


def head_blocks(channels, members):
    width = channels // HEADS
    row = lax.broadcasted_iota(jnp.int32, (HEADS * members, channels), 0) // members
    col = lax.broadcasted_iota(jnp.int32, (HEADS * members, channels), 1) // width
    return row == col


def spread(rows, blocks):
    return jnp.concatenate([rows] * HEADS, axis=0) * blocks


def head_scale(raw, ones):
    width = raw.shape[1] // HEADS
    mean_sq = nn((raw * raw).astype(BF), ones) * (1.0 / width)
    factor = lax.rsqrt(jnp.maximum(mean_sq, FLOOR))
    live = jnp.where(mean_sq > FLOOR, 1.0, jnp.where(mean_sq == FLOOR, 0.5, 0.0))
    return factor, live


def cell_forward(x, gain, w_proj, w_out, ones, members):
    rows, channels = x.shape
    cells = rows // members
    scale = 1.0 / math.sqrt(channels // HEADS)
    inputs = x.astype(F32)
    inv = lax.rsqrt(jnp.mean(inputs * inputs, axis=-1, keepdims=True) + EPSILON)
    normed = (inputs * inv * gain).astype(BF)
    k_raw = nn(normed, w_proj[:, channels : 2 * channels]).astype(BF).astype(F32)
    q_raw = nn(normed, w_proj[:, :channels]).astype(BF).astype(F32)
    values = nn(normed, w_proj[:, 2 * channels :]).astype(BF)
    q_fac, q_live = head_scale(q_raw, ones)
    k_fac, k_live = head_scale(k_raw, ones)
    queries = (q_raw * q_fac).astype(BF)
    keys = (k_raw * k_fac).astype(BF)
    part = [slice(c * members, (c + 1) * members) for c in range(cells)]
    k_bd = [spread(keys[s], ones) for s in part]
    v_bd = [spread(values[s], ones) for s in part]
    scores = jnp.concatenate([nt(queries[s], k) for s, k in zip(part, k_bd)], axis=0)
    expd = jnp.exp(scores * scale)
    narrow = expd.astype(BF)
    inv_total = 1.0 / nn(narrow, ones)
    mixed = jnp.concatenate([nn(narrow[s], v) for s, v in zip(part, v_bd)], axis=0)
    updated = (inputs + nn((mixed * inv_total).astype(BF), w_out)).astype(BF)
    soft = expd * inv_total
    rounded = soft.astype(BF)
    saved = (inputs, inv, q_raw, k_raw, q_fac, k_fac, q_live, k_live, queries, k_bd, v_bd, soft, rounded)
    return updated, saved


def head_pull(raw, factor, live, grad, ones):
    width = raw.shape[1] // HEADS
    inner = nn((raw * grad).astype(BF), ones) * (1.0 / width)
    return grad * factor - raw * (factor * factor * factor * live * inner)


def fold(full, ones, members):
    kept = full * ones.astype(F32)
    total = kept[:members]
    for h in range(1, HEADS):
        total = total + kept[h * members : (h + 1) * members]
    return total


def cell_backward(grad_field, saved, gain, w_proj, w_out, ones, members):
    inputs, inv, q_raw, k_raw, q_fac, k_fac, q_live, k_live, queries, k_bd, v_bd, soft, rounded = saved
    rows, channels = inputs.shape
    cells = rows // members
    scale = 1.0 / math.sqrt(channels // HEADS)
    part = [slice(c * members, (c + 1) * members) for c in range(cells)]
    grad_mixed = nt(grad_field, w_out).astype(BF)
    dprob = jnp.concatenate([nt(grad_mixed[s], v) for s, v in zip(part, v_bd)], axis=0)
    delta = nn((soft * dprob).astype(BF), ones)
    dscore = (soft * (dprob - delta)).astype(BF)
    q_grad = jnp.concatenate([nn(dscore[s], k) for s, k in zip(part, k_bd)], axis=0) * scale
    k_grad = jnp.concatenate([fold(tn(dscore[s], queries[s]), ones, members) for s in part], axis=0) * scale
    v_grad = jnp.concatenate([fold(tn(rounded[s], grad_mixed[s]), ones, members) for s in part], axis=0)
    gq = head_pull(q_raw, q_fac, q_live, q_grad, ones).astype(BF)
    gk = head_pull(k_raw, k_fac, k_live, k_grad, ones).astype(BF)
    gv = v_grad.astype(BF)
    grad_normed = (
        nt(gq, w_proj[:, :channels])
        + nt(gk, w_proj[:, channels : 2 * channels])
        + nt(gv, w_proj[:, 2 * channels :])
    )
    lifted = grad_normed * gain
    inner = jnp.mean(lifted * inputs, axis=-1, keepdims=True)
    return lifted * inv - inputs * (inv * inv * inv * inner)


def iota(shape, dim):
    return lax.broadcasted_iota(jnp.int32, shape, dim)


def one_hot(shape, source):
    return jnp.where(iota(shape, 1) == source(iota(shape, 0)), 1.0, 0.0).astype(BF)


def pack(rows, peers):
    half = rows.shape[1] // 2
    per = rows.shape[0] // peers
    low = rows[:, :half].reshape(peers, per, half)
    high = rows[:, half:].reshape(peers, per, half)
    return jnp.concatenate([low, high], axis=1).astype(BF)


def unpack(chunks):
    peers, double, half = chunks.shape
    wide = chunks.astype(F32)
    low = wide[:, : double // 2].reshape(peers * double // 2, half)
    high = wide[:, double // 2 :].reshape(peers * double // 2, half)
    return jnp.concatenate([low, high], axis=1).astype(BF)


X, G, U, B = range(4)


def kernel(
    dims,
    ens_any,
    gain_any,
    w_proj_any,
    w_out_any,
    conv_any,
    cot_any,
    result_ref,
    grad_ref,
    ens_ref,
    cot_ref,
    gain_ref,
    w_proj_ref,
    w_out_ref,
    conv_ref,
    out_buf,
    in_buf,
    halo_cot,
    edge_cot,
    gf_ref,
    side_out,
    rim_in,
    side_in,
    corner_in,
    column_ref,
    load_sem,
    ex_send,
    ex_recv,
    halo_send,
    halo_recv,
    rim_send,
    rim_recv,
    side_send,
    side_recv,
    corner_send,
    corner_recv,
    flag,
):
    mem, lat, lon, channels, peers, lats, lons = dims
    cells = mem * lat * lon
    members = mem * peers
    me = lax.axis_index("member")
    my_lat = lax.axis_index("lat")
    my_lon = lax.axis_index("lon")

    pairs = (
        (ens_any, ens_ref),
        (cot_any, cot_ref),
        (conv_any, conv_ref),
        (w_proj_any, w_proj_ref),
        (w_out_any, w_out_ref),
        (gain_any, gain_ref),
    )
    loads = [
        pltpu.make_async_copy(src, dst, load_sem.at[i]) for i, (src, dst) in enumerate(pairs)
    ]
    for load in loads:
        load.start()

    def partner(j):
        return {"member": lax.rem(me + j, peers)}

    def near(d_lat, d_lon):
        return {
            "lat": lax.rem(my_lat + d_lat + lats, lats),
            "lon": lax.rem(my_lon + d_lon + lons, lons),
        }

    around = [(a, b) for a in (-1, 0, 1) for b in (-1, 0, 1) if (a, b) != (0, 0)]
    barrier = pltpu.get_barrier_semaphore()
    far_first = sorted(range(1, peers), key=lambda j: -(min(j, peers - j) // 2 + 2 * (j % 2)))
    ring = peers // 2
    my_z, my_y = me // 2, lax.rem(me, 2)

    def along(dz):
        return {"member": lax.rem(my_z + dz, ring) * 2 + my_y}

    twin = {"member": my_z * 2 + 1 - my_y}
    z_steps = sorted(range(1, ring), key=lambda j: -min(j, ring - j))
    close = [along(dz) for dz in z_steps] + [twin]
    for device in close:
        pl.semaphore_signal(barrier, inc=1, device_id=device, device_id_type=MESH)
    for d_lat, d_lon in around:
        pl.semaphore_signal(barrier, inc=1, device_id=near(d_lat, d_lon), device_id_type=MESH)

    blocks = peers // lat
    width = lon // blocks
    my_row, my_block = me // blocks, lax.rem(me, blocks)

    def home_source(i):
        j, m, c = i // (mem * width), (i // width) % mem, i % width
        q = lax.rem(me + j, peers)
        return (m * lat + q // blocks) * lon + lax.rem(q, blocks) * width + c

    def home_target(i):
        m, a, b = i // (lat * lon), (i // lon) % lat, i % lon
        j = lax.rem(a * blocks + b // width - me + peers, peers)
        return (j * mem + m) * width + b % width

    def cell_source(i):
        c, j, m = i // members, (i // mem) % peers, i % mem
        return (j * mem + m) * width + c

    def cell_target(i):
        j, m, c = i // (mem * width), (i // width) % mem, i % width
        return (c * peers + j) * mem + m

    def edge_source(i):
        count = mem * lat
        return (i % count) * lon + (i // count) * (lon - 1)

    square = (cells, cells)
    home_out = one_hot(square, home_source)
    home_in = one_hot(square, home_target)
    cell_in = one_hot(square, cell_source)
    cell_out = one_hot(square, cell_target)
    edges = one_hot((2 * mem * lat, cells), edge_source)

    def exchange(kind, sign, group):
        return [
            pltpu.make_async_remote_copy(
                src_ref=out_buf.at[kind, j],
                dst_ref=in_buf.at[kind, j],
                send_sem=ex_send.at[kind],
                recv_sem=ex_recv.at[kind],
                device_id=partner(j if sign > 0 else peers - j),
                device_id_type=MESH,
            )
            for j in group
        ]

    def exchange_all(kind):
        return pltpu.make_async_remote_copy(
            src_ref=out_buf.at[kind, pl.ds(1, peers - 1)],
            dst_ref=in_buf.at[kind, pl.ds(1, peers - 1)],
            send_sem=ex_send.at[kind],
            recv_sem=ex_recv.at[kind],
            device_id=partner(1),
            device_id_type=MESH,
        )

    def send(kind, order, rows, sign):
        packed = pack(nn(order, rows), peers)
        out_buf[kind] = packed
        in_buf[kind, 0] = packed[0]
        for copy in exchange(kind, sign, far_first):
            copy.start()

    def receive(kind, order):
        exchange_all(kind).wait_recv()
        return nn(order, unpack(in_buf[kind]))

    has_low, has_high = my_lat > 0, my_lat < lats - 1

    def halo_group(d_lat):
        which = 1 - d_lat
        copies = [
            pltpu.make_async_remote_copy(
                src_ref=edge_cot,
                dst_ref=halo_cot.at[0 if d_lon > 0 else 1, lat + 2 + which],
                send_sem=halo_send.at[which],
                recv_sem=halo_recv.at[which],
                device_id=near(d_lat, d_lon),
                device_id_type=MESH,
            )
            for d_lon in (-1, 1)
        ]
        if d_lat:
            copies.append(
                pltpu.make_async_remote_copy(
                    src_ref=cot_ref.at[:, lat - 1 if d_lat > 0 else 0],
                    dst_ref=halo_cot.at[:, 0 if d_lat > 0 else lat + 1],
                    send_sem=halo_send.at[3 + (which > 1)],
                    recv_sem=halo_recv.at[3 + (which > 1)],
                    device_id=near(d_lat, 0),
                    device_id_type=MESH,
                )
            )
        return copies

    def halo_columns(which):
        columns = halo_cot.at[:, lat + 2 + which]
        return pltpu.make_async_remote_copy(
            src_ref=columns,
            dst_ref=columns,
            send_sem=halo_send.at[which],
            recv_sem=halo_recv.at[which],
            device_id=near(0, 1),
            device_id_type=MESH,
        )

    def start_halo():
        @pl.when(has_high)
        def _():
            for copy in halo_group(1):
                copy.start()

        @pl.when(has_low)
        def _():
            for copy in halo_group(-1):
                copy.start()

        for copy in halo_group(0):
            copy.start()

    def wait_halo():
        halo_columns(1).wait_recv()

        @pl.when(has_low)
        def _():
            halo_columns(0).wait_recv()
            halo_group(1)[2].wait_recv()

        @pl.when(has_high)
        def _():
            halo_columns(2).wait_recv()
            halo_group(-1)[2].wait_recv()

    def wait_halo_sent():
        halo_columns(1).wait_send()

        @pl.when(has_high)
        def _():
            halo_columns(0).wait_send()
            halo_group(1)[2].wait_send()

        @pl.when(has_low)
        def _():
            halo_columns(2).wait_send()
            halo_group(-1)[2].wait_send()

    far, close_by = far_first[: peers // 2], far_first[peers // 2 :] + [0]

    def home_of(j, rim, side):
        return {
            "member": lax.rem(me + peers - j, peers),
            "lat": lax.rem(my_lat + (0 if rim is None else 1 if rim == 0 else lats - 1), lats),
            "lon": lax.rem(my_lon + (0 if side is None else 1 if side == 0 else lons - 1), lons),
        }

    def rim_copies(rim, group):
        return [
            pltpu.make_async_remote_copy(
                src_ref=out_buf.at[U, j],
                dst_ref=rim_in.at[rim, my_block],
                send_sem=rim_send.at[rim],
                recv_sem=rim_recv.at[rim],
                device_id=home_of(j, rim, None),
                device_id_type=MESH,
            )
            for j in group
        ]

    def side_copies(side, group):
        return [
            pltpu.make_async_remote_copy(
                src_ref=side_out.at[side, j],
                dst_ref=side_in.at[side, my_row],
                send_sem=side_send.at[side],
                recv_sem=side_recv.at[side],
                device_id=home_of(j, None, side),
                device_id_type=MESH,
            )
            for j in group
        ]

    def corner_copies(side, rim, group):
        return [
            pltpu.make_async_remote_copy(
                src_ref=side_out.at[side, j],
                dst_ref=corner_in.at[side, rim],
                send_sem=corner_send.at[side, rim],
                recv_sem=corner_recv.at[side, rim],
                device_id=home_of(j, rim, side),
                device_id_type=MESH,
            )
            for j in group
        ]

    def bytes_of(ref, send_sem, recv_sem):
        return pltpu.make_async_remote_copy(
            src_ref=ref,
            dst_ref=ref,
            send_sem=send_sem,
            recv_sem=recv_sem,
            device_id=partner(1),
            device_id_type=MESH,
        )

    def gets_rim(rim):
        return has_low if rim == 0 else has_high

    def sends_rim(rim):
        if rim == 0:
            return jnp.logical_and(has_high, my_row == lat - 1)
        return jnp.logical_and(has_low, my_row == 0)

    def sends_side(side):
        return my_block == (blocks - 1 if side == 0 else 0)

    def start_rims(group):
        for rim in range(2):

            @pl.when(sends_rim(rim))
            def _():
                for copy in rim_copies(rim, group):
                    copy.start()

        for side in range(2):

            @pl.when(sends_side(side))
            def _():
                for copy in side_copies(side, group):
                    copy.start()

                for rim in range(2):

                    @pl.when(sends_rim(rim))
                    def _():
                        for copy in corner_copies(side, rim, group):
                            copy.start()

    def wait_rims():
        for side in range(2):
            bytes_of(side_in.at[side], side_send.at[side], side_recv.at[side]).wait_recv()
        for rim in range(2):

            @pl.when(gets_rim(rim))
            def _():
                bytes_of(rim_in.at[rim], rim_send.at[rim], rim_recv.at[rim]).wait_recv()
                for side in range(2):
                    bytes_of(
                        corner_in.at[side, rim], corner_send.at[side, rim], corner_recv.at[side, rim]
                    ).wait_recv()

    def wait_rims_sent():
        for rim in range(2):

            @pl.when(sends_rim(rim))
            def _():
                bytes_of(out_buf.at[U], rim_send.at[rim], rim_recv.at[rim]).wait_send()

        for side in range(2):

            @pl.when(sends_side(side))
            def _():
                bytes_of(side_out.at[side], side_send.at[side], side_recv.at[side]).wait_send()
                for rim in range(2):

                    @pl.when(sends_rim(rim))
                    def _():
                        bytes_of(
                            side_out.at[side], corner_send.at[side, rim], corner_recv.at[side, rim]
                        ).wait_send()

    def side_pack(rows):
        half = channels // 2
        shape = (2 * mem * peers, mem * peers)
        i, k = iota(shape, 0), iota(shape, 1)
        same = (i // (2 * mem)) * mem + i % mem == k
        upper = (i // mem) % 2 == 1
        low = jnp.where(jnp.logical_and(same, jnp.logical_not(upper)), 1.0, 0.0).astype(BF)
        high = jnp.where(jnp.logical_and(same, upper), 1.0, 0.0).astype(BF)
        return nn(low, rows[:, :half]) + nn(high, rows[:, half:])

    def rim_source(i):
        m, b = i // lon, i % lon
        return ((b // width) * mem + m) * width + b % width

    def rim_rows(rim, pick):
        return nn(pick, unpack(rim_in[rim])).astype(BF)

    def side_column(side):
        half = channels // 2
        parts = [side_in.at[side, a] for a in range(lat)] + [corner_in.at[side, rim] for rim in range(2)]
        for n, part in enumerate(parts):
            rows = part[...].astype(F32)
            column_ref[side, n * mem : (n + 1) * mem, 0:half] = rows[:mem]
            column_ref[side, n * mem : (n + 1) * mem, half:channels] = rows[mem:]
        return column_ref[side].astype(BF)

    strip = lat + 2

    def cot_edge(m, shift, a):
        which = jnp.where(a == 0, 0, jnp.where(a == strip - 1, 2, 1))
        row = jnp.where(a == 0, lat - 1, jnp.where(a == strip - 1, 0, a - 1))
        return which * lon + (mem * lat if shift < 0 else 0) + m * lat + row

    def up_edge(m, shift, a):
        outer = jnp.where(a == 0, lat, jnp.where(a == strip - 1, lat + 1, a - 1))
        return outer * mem + m

    def picks_of(edge_row, count):
        return {(m, shift): pick_of(count, edge_row, m, shift) for m in range(mem) for shift in (-1, 1)}

    def pick_of(count, edge_row, m, shift):
        shape = (strip * lon, strip * lon + count)
        a, b = iota(shape, 0) // lon, iota(shape, 0) % lon
        outer = strip * lon + edge_row(m, shift, a)
        source = jnp.where(b == (0 if shift < 0 else lon - 1), outer, a * lon + b + shift)
        open_row = jnp.logical_and(
            jnp.logical_or(a > 0, has_low), jnp.logical_or(a < strip - 1, has_high)
        )
        return jnp.where(jnp.logical_and(iota(shape, 1) == source, open_row), 1.0, 0.0).astype(BF)

    def shifted(field, columns, picks, m, shift):
        if shift == 0:
            return field
        return nn(picks[m, shift], jnp.concatenate([field, columns], axis=0)).astype(BF)

    def conv(fields, columns, picks, adjoint):
        halves = []
        wide = {}
        for c in range(3):
            shift = 1 - c if adjoint else c - 1
            side = 0 if shift < 0 else 1
            wide[c] = [shifted(fields[m], columns[side], picks, m, shift) for m in range(mem)]
        for at in range(0, channels, channels // 2):
            part = pl.ds(at, channels // 2)
            total = None
            for c in range(3):
                for r in range(3):
                    start = (2 - r if adjoint else r) * lon
                    window = jnp.concatenate([w[start : start + lat * lon] for w in wide[c]], axis=0)
                    if adjoint:
                        term = nt(window, conv_ref[r, c, part, :])
                    else:
                        term = nn(window, conv_ref[r, c, :, part])
                    total = term if total is None else total + term
            halves.append(total)
        return jnp.concatenate(halves, axis=1)

    def closed(rows, there):
        return jnp.where(there, rows.astype(F32), 0.0).astype(BF)

    @pl.when(jnp.logical_not(has_low))
    def _():
        halo_cot[:, 0] = jnp.zeros((mem, lon, channels), BF)
        halo_cot[:, lat + 2] = jnp.zeros((mem, lon, channels), BF)
        rim_in[0] = jnp.zeros(rim_in.shape[1:], BF)
        corner_in[:, 0] = jnp.zeros((2,) + corner_in.shape[2:], BF)

    @pl.when(jnp.logical_not(has_high))
    def _():
        halo_cot[:, lat + 1] = jnp.zeros((mem, lon, channels), BF)
        halo_cot[:, lat + 4] = jnp.zeros((mem, lon, channels), BF)
        rim_in[1] = jnp.zeros(rim_in.shape[1:], BF)
        corner_in[:, 1] = jnp.zeros((2,) + corner_in.shape[2:], BF)

    column_ref[...] = jnp.zeros(column_ref.shape, F32)
    loads[0].wait()
    ens = ens_ref[...].reshape(cells, channels)
    loads[1].wait()
    cot = cot_ref[...].reshape(cells, channels)
    packed = pack(nn(home_out, ens), peers)
    out_buf[X] = packed
    in_buf[X, 0] = packed[0]
    edge_cot[...] = nn(edges, cot).astype(BF)
    pl.semaphore_wait(barrier, len(close) + len(around))
    pl.semaphore_signal(flag, inc=1, device_id=twin, device_id_type=MESH)
    start_halo()
    copies = dict(zip(far_first, exchange(X, 1, far_first)))
    for j in far_first:
        if j % 2 == 0:
            copies[j].start()
    pl.semaphore_wait(flag, 1)
    for j in far_first:
        if j % 2 == 1:
            copies[j].start()

    ones = head_blocks(channels, members).astype(BF)
    loads[2].wait()
    cot_picks = picks_of(cot_edge, 3 * lon)
    wait_halo()
    cot_fields = [
        jnp.concatenate(
            [
                closed(halo_cot[m, 0], has_low),
                cot_ref[m].reshape(lat * lon, channels),
                closed(halo_cot[m, lat + 1], has_high),
            ],
            axis=0,
        )
        for m in range(mem)
    ]
    cot_columns = [halo_cot[side, lat + 2 : lat + 5].reshape(3 * lon, channels) for side in range(2)]
    grad_field = cot.astype(F32) + conv(cot_fields, cot_columns, cot_picks, True)
    gf_ref[...] = grad_field
    send(G, home_out, grad_field.astype(BF), 1)

    for load in loads[3:]:
        load.wait()
    gain = gain_ref[...]
    w_proj = w_proj_ref[...]
    w_out = w_out_ref[...]
    x = receive(X, cell_in).astype(BF)
    updated, saved = cell_forward(x, gain, w_proj, w_out, ones, members)
    packed = pack(nn(cell_out, updated), peers)
    out_buf[U] = packed
    in_buf[U, 0] = packed[0]
    for side, c in enumerate((width - 1, 0)):
        rows = updated[c * members : (c + 1) * members]
        side_out[side] = side_pack(rows).reshape(side_out.shape[1:]).astype(BF)
    for group in (far, close_by):
        for copy in exchange(U, -1, [j for j in group if j]):
            copy.start()
        start_rims(group)

    grads = receive(G, cell_in).astype(BF)
    grad_inputs = cell_backward(grads, saved, gain, w_proj, w_out, ones, members)
    send(B, cell_out, grad_inputs.astype(BF), -1)

    up_picks = picks_of(up_edge, column_ref.shape[1])
    rim_pick = one_hot((mem * lon, mem * lon), rim_source)
    field = receive(U, home_in)
    wait_rims()
    rows = field.astype(BF)
    low = closed(rim_rows(0, rim_pick), has_low)
    high = closed(rim_rows(1, rim_pick), has_high)
    up_fields = [
        jnp.concatenate(
            [
                low[m * lon : (m + 1) * lon],
                rows[m * lat * lon : (m + 1) * lat * lon],
                high[m * lon : (m + 1) * lon],
            ],
            axis=0,
        )
        for m in range(mem)
    ]
    result = field + conv(up_fields, [side_column(0), side_column(1)], up_picks, False)
    result_ref[...] = result.astype(BF).reshape(result_ref.shape)

    back = receive(B, home_in)
    grad_ref[...] = (gf_ref[...] + back).astype(BF).reshape(grad_ref.shape)

    for kind in (X, G, U, B):
        exchange_all(kind).wait_send()
    wait_halo_sent()
    wait_rims_sent()


def store_kernel(result_in, grad_in, result_out, grad_out, sem):
    copies = [
        pltpu.make_async_copy(result_in, result_out, sem.at[0]),
        pltpu.make_async_copy(grad_in, grad_out, sem.at[1]),
    ]
    for copy in copies:
        copy.start()
    for copy in copies:
        copy.wait()


MESH = pl.DeviceIdType.MESH
LIMIT = 16 * 1024 * 1024


def per_device(ensemble, norm_gain, project_weight, output_weight, conv_kernel, cotangent):
    mem, lat, lon, channels = ensemble.shape
    peers = lax.axis_size("member")
    dims = (mem, lat, lon, channels, peers, lax.axis_size("lat"), lax.axis_size("lon"))
    vmem = pl.BlockSpec(memory_space=pltpu.VMEM)
    anywhere = pl.BlockSpec(memory_space=pl.ANY)
    chunk = (4, peers, 2 * mem * lat, channels // 2)
    halo = (mem, lat + 5, lon, channels)
    field = jax.ShapeDtypeStruct(ensemble.shape, BF)
    outs = pl.pallas_call(
        functools.partial(kernel, dims),
        out_shape=(field, field),
        in_specs=[pl.BlockSpec(memory_space=pltpu.HBM)] * 6,
        out_specs=(vmem, vmem),
        scratch_shapes=[
            pltpu.VMEM(ensemble.shape, BF),
            pltpu.VMEM(ensemble.shape, BF),
            pltpu.VMEM((1, channels), F32),
            pltpu.VMEM(project_weight.shape, BF),
            pltpu.VMEM(output_weight.shape, BF),
            pltpu.VMEM(conv_kernel.shape, BF),
            pltpu.VMEM(chunk, BF),
            pltpu.VMEM(chunk, BF),
            pltpu.VMEM(halo, BF),
            pltpu.VMEM((2 * mem * lat, channels), BF),
            pltpu.VMEM((mem * lat * lon, channels), F32),
            pltpu.VMEM((2, peers, 2 * mem, channels // 2), BF),
            pltpu.VMEM((2, peers // lat) + chunk[2:], BF),
            pltpu.VMEM((2, lat, 2 * mem, channels // 2), BF),
            pltpu.VMEM((2, 2, 2 * mem, channels // 2), BF),
            pltpu.VMEM((2, 16, channels), F32),
            pltpu.SemaphoreType.DMA((6,)),
            pltpu.SemaphoreType.DMA((4,)),
            pltpu.SemaphoreType.DMA((4,)),
            pltpu.SemaphoreType.DMA((5,)),
            pltpu.SemaphoreType.DMA((5,)),
            pltpu.SemaphoreType.DMA((2,)),
            pltpu.SemaphoreType.DMA((2,)),
            pltpu.SemaphoreType.DMA((2,)),
            pltpu.SemaphoreType.DMA((2,)),
            pltpu.SemaphoreType.DMA((2, 2)),
            pltpu.SemaphoreType.DMA((2, 2)),
            pltpu.SemaphoreType.REGULAR,
        ],
        compiler_params=pltpu.CompilerParams(
            collective_id=0, has_side_effects=True, vmem_limit_bytes=LIMIT
        ),
    )(
        *(
            pltpu.with_memory_space_constraint(value, pltpu.HBM)
            for value in (
                ensemble,
                norm_gain.reshape(1, channels),
                project_weight,
                output_weight,
                conv_kernel,
                cotangent,
            )
        )
    )
    return pl.pallas_call(
        store_kernel,
        out_shape=(field, field),
        in_specs=[vmem, vmem],
        out_specs=(anywhere, anywhere),
        scratch_shapes=[pltpu.SemaphoreType.DMA((2,))],
        compiler_params=pltpu.CompilerParams(vmem_limit_bytes=LIMIT),
    )(*outs)


def solution(mesh):
    field = P("member", "lat", "lon", None)
    return jax.shard_map(
        per_device,
        mesh=mesh,
        in_specs=(field, P(), P(), P(), P(), field),
        out_specs=(field, field),
        check_vma=False,
    )
```
